32 devices in a mesh: dp: 8 (over z, x), tensor: 4 (over y, core).
Axes of the slice: x: 2, y: 2, z: 4, core: 2. Of those that a mesh axis runs over, the one named last changes fastest.
Arguments:
- hidden_in: float32 [8, 1024, 1280], P('dp', 'tensor'), may hold values from -0.2 to 0.2
- lengths: int32 [8], P('dp'), may hold values from 256 to 1024
- teacher: float32 [8, 1024, 1280], P('dp', 'tensor'), may hold values from -0.2 to 0.2
- w_query: bfloat16 [1280, 1280], P('dp', 'tensor'), may hold values from -0.15625 to 0.15625
- w_key: bfloat16 [1280, 1280], P('dp', 'tensor'), may hold values from -0.15625 to 0.15625
- w_value: bfloat16 [1280, 1280], P('dp', 'tensor'), may hold values from -0.15625 to 0.15625
- w_attn_out: bfloat16 [1280, 1280], P('tensor', 'dp'), may hold values from -0.15625 to 0.15625
- w_up: bfloat16 [1280, 5120], P('dp', 'tensor'), may hold values from -0.15625 to 0.15625
- w_gate: bfloat16 [1280, 5120], P('dp', 'tensor'), may hold values from -0.15625 to 0.15625
- w_down: bfloat16 [5120, 1280], P('tensor', 'dp'), may hold values from -0.078125 to 0.078125
- s_qk: float32 [1280], replicated, may hold values from 0.8 to 1.6
- alpha_attn: float32 [1280], replicated, may hold values from 0.15 to 0.6
- alpha_mlp: float32 [1280], replicated, may hold values from 0.15 to 0.6
- s_up: float32 [5120], replicated, may hold values from 0.5 to 2
- s_gate: float32 [5120], replicated, may hold values from 0.5 to 2
Outputs:
- loss: float32 [], replicated
- output: float32 [8, 1024, 1280], P('dp', 'tensor')
- grad_input: float32 [8, 1024, 1280], P('dp', 'tensor')
- grad_w_query: float32 [1280, 1280], P('dp', 'tensor')
- grad_w_key: float32 [1280, 1280], P('dp', 'tensor')
- grad_w_value: float32 [1280, 1280], P('dp', 'tensor')
- grad_w_attn_out: float32 [1280, 1280], P('tensor', 'dp')
- grad_w_up: float32 [1280, 5120], P('dp', 'tensor')
- grad_w_gate: float32 [1280, 5120], P('dp', 'tensor')
- grad_w_down: float32 [5120, 1280], P('tensor', 'dp')
- grad_s_qk: float32 [1280], replicated
- grad_alpha_attn: float32 [1280], replicated
- grad_alpha_mlp: float32 [1280], replicated
- grad_s_up: float32 [5120], replicated
- grad_s_gate: float32 [5120], replicated
The draws below stay inside these ranges and needn't reach their ends.
All inputs are finite; a program needn't handle non-finite values.
Results may differ from the reference program's by a relative error of at most 0.018.
Values may be sent and summed in bfloat16 or wider, within the bound.
No kernel may reach another device: no remote copies, remote signals or barrier semaphores. Data moves between devices by JAX's collectives and lax.ppermute only.
A program may use at most 192 MiB of HBM per device.

```python
import math
import jax
import jax.numpy as jnp
from jax import lax

D = 1280
HEADS = 20
HEAD = 64
FF = 5120
SLOTS = 1024
SEQS = 8
TOKENS = 8192


def plant(array, key, low, top_value):
    longest = array.shape.index(max(array.shape))
    spots = []
    for shift in (0, 1):
        where = [jax.random.randint(jax.random.fold_in(key, axis), (), 0, length) for axis, length in enumerate(array.shape)]
        where[longest] = (where[longest] + shift) % array.shape[longest]
        spots.append(tuple(where))
    return array.at[spots[0]].set(low).at[spots[1]].set(top_value)


def steps_of(stream_key, dims, cuts, smallest, high):
    def one(position, blocks):
        draws = jax.random.uniform(jax.random.fold_in(jax.random.fold_in(stream_key, 6), position), (blocks,), jnp.float32, smallest / len(cuts), high / len(cuts))
        return jnp.repeat(jnp.exp(draws), dims[position] // blocks).reshape((-1,) + (1,) * (len(dims) - position - 1))

    factor_of = one(*cuts[0])
    for cut in cuts[1:]:
        factor_of = factor_of * one(*cut)
    return factor_of


def normal_values(key, dims, deviation, reach, shards=(), held_as=jnp.bfloat16):
    array = jax.random.normal(key, dims, jnp.float32) * deviation
    if len(shards) > 0:
        array = steps_of(key, dims, shards, -0.22, 0.18) * array
    return jnp.clip(array, min=-reach, max=reach).astype(held_as)


def setup_inputs(seed: int = 0) -> dict:
    keys = jax.random.split(jax.random.key(seed), 16)
    hidden_in = normal_values(keys[0], (SEQS, SLOTS, D), 0.03, 0.2, ((0, 8), (1, 4)), jnp.float32)
    lengths = plant(jax.random.randint(keys[1], (SEQS,), SLOTS // 4, SLOTS + 1), jax.random.fold_in(keys[1], 1), SLOTS // 4, SLOTS).astype(jnp.int32)
    teacher = normal_values(keys[2], (SEQS, SLOTS, D), 0.03, 0.2, ((0, 8), (1, 4)), jnp.float32)
    w_query = normal_values(keys[3], (D, D), D ** -0.5, 0.15625, ((0, 8), (1, 4)))
    w_key = normal_values(keys[4], (D, D), D ** -0.5, 0.15625, ((0, 8), (1, 4)))
    w_value = normal_values(keys[5], (D, D), D ** -0.5, 0.15625, ((0, 8), (1, 4)))
    w_attn_out = normal_values(keys[6], (D, D), D ** -0.5, 0.15625, ((0, 4), (1, 8)))
    w_up = normal_values(keys[7], (D, FF), D ** -0.5, 0.15625, ((0, 8), (1, 4)))
    w_gate = normal_values(keys[8], (D, FF), D ** -0.5, 0.15625, ((0, 8), (1, 4)))
    w_down = normal_values(keys[9], (FF, D), FF ** -0.5, 0.078125, ((0, 4), (1, 8)))
    s_qk = jnp.clip(jnp.exp(jax.random.uniform(keys[10], (D,), jnp.float32, math.log(0.8), math.log(1.6))), 0.8, 1.6)
    alpha_attn = jnp.clip(jnp.exp(jax.random.uniform(keys[11], (D,), jnp.float32, math.log(0.15), math.log(0.6))), 0.15, 0.6)
    alpha_mlp = jnp.clip(jnp.exp(jax.random.uniform(keys[12], (D,), jnp.float32, math.log(0.15), math.log(0.6))), 0.15, 0.6)
    s_up = jnp.clip(jnp.exp(jax.random.uniform(keys[13], (FF,), jnp.float32, math.log(0.5), math.log(2.0))), 0.5, 2.0)
    s_gate = jnp.clip(jnp.exp(jax.random.uniform(keys[14], (FF,), jnp.float32, math.log(0.5), math.log(2.0))), 0.5, 2.0)
    return {"hidden_in": hidden_in, "lengths": lengths, "teacher": teacher, "w_query": w_query, "w_key": w_key, "w_value": w_value, "w_attn_out": w_attn_out, "w_up": w_up, "w_gate": w_gate, "w_down": w_down, "s_qk": s_qk, "alpha_attn": alpha_attn, "alpha_mlp": alpha_mlp, "s_up": s_up, "s_gate": s_gate}


@jax.custom_vjp
def low(v):
    return lax.optimization_barrier(v.astype(jnp.bfloat16)).astype(jnp.float32)

@jax.custom_vjp
def low_back(v):
    return v

def low_keep(v):
    return (low(v), None)

def low_pass(kept, grad):
    return (grad,)

def back_keep(v):
    return (v, None)

def back_low(kept, grad):
    return (low(grad),)
low.defvjp(low_keep, low_pass)
low_back.defvjp(back_keep, back_low)
EPSILON = 1e-06

def matmul(left, right):
    return jnp.dot(left, right, precision=lax.Precision.HIGHEST, preferred_element_type=jnp.float32)

def normalize(vector):
    return vector * lax.rsqrt(lax.optimization_barrier(jnp.sum(vector * vector, axis=-1, keepdims=True)) + EPSILON)

def layer_seq(params, hidden_seq, length, teacher_seq):
    w_query, w_key, w_value, w_attn_out, w_up, w_gate, w_down, s_qk, alpha_attn, alpha_mlp, s_up, s_gate = params
    slot_count = hidden_seq.shape[0]
    stream_low = low(hidden_seq)
    q_raw = low_back(matmul(stream_low, w_query)).reshape(slot_count, HEADS, HEAD)
    k_raw = low_back(matmul(stream_low, w_key)).reshape(slot_count, HEADS, HEAD)
    v_low = low(low_back(matmul(stream_low, w_value))).reshape(slot_count, HEADS, HEAD)
    qk_gain = s_qk.reshape(HEADS, HEAD)
    q_low = low(normalize(q_raw) * qk_gain)
    k_low = low(normalize(k_raw) * qk_gain)
    scores = math.sqrt(HEAD) * jnp.einsum('qhd,khd->hqk', q_low, k_low, precision=lax.Precision.HIGHEST)
    scores = low_back(scores)
    query_ids = lax.broadcasted_iota(jnp.int32, (slot_count, slot_count), 0)
    key_ids = lax.broadcasted_iota(jnp.int32, (slot_count, slot_count), 1)
    allowed = (key_ids <= query_ids) & (key_ids < length)
    scores = jnp.where(allowed[None], scores, -1e+30)
    probs = low(jax.nn.softmax(scores, axis=-1))
    attended = jnp.einsum('hqk,khd->qhd', probs, v_low, precision=lax.Precision.HIGHEST).reshape(slot_count, D)
    attended = low(low_back(attended))
    attn_sum = low_back(matmul(attended, w_attn_out))
    attn_unit = normalize(attn_sum)
    first_out = normalize(hidden_seq + alpha_attn * (attn_unit - hidden_seq))
    first_low = low(first_out)
    up_raw = low_back(matmul(first_low, w_up))
    gate_raw = low_back(matmul(first_low, w_gate))
    scaled_up = up_raw * s_up
    scaled_gate = gate_raw * (s_gate * math.sqrt(D))
    hidden_low = low(scaled_up * jax.nn.silu(scaled_gate))
    mlp_sum = low_back(matmul(hidden_low, w_down))
    mlp_unit = normalize(mlp_sum)
    output = normalize(first_out + alpha_mlp * (mlp_unit - first_out))
    valid_mask = (jnp.arange(slot_count, dtype=jnp.int32) < length).astype(jnp.float32)
    difference = output - teacher_seq
    error = jnp.sum(lax.optimization_barrier(jnp.sum(difference * difference, axis=-1)) * valid_mask)
    return (output, error)

def reference(hidden_in, lengths, teacher, w_query, w_key, w_value, w_attn_out, w_up, w_gate, w_down, s_qk, alpha_attn, alpha_mlp, s_up, s_gate):
    weights = tuple((weight_arg.astype(jnp.float32) for weight_arg in (w_query, w_key, w_value, w_attn_out, w_up, w_gate, w_down)))
    vectors = (s_qk, alpha_attn, alpha_mlp, s_up, s_gate)
    token_count = jnp.sum(lengths).astype(jnp.float32)

    def forward(hidden_all, *params):

        def one_seq(seq_entry):
            return jax.checkpoint(layer_seq)(params, seq_entry[0], seq_entry[1], seq_entry[2])
        output, errors = lax.map(one_seq, (hidden_all, lengths, teacher))
        loss = jnp.sum(errors) / token_count
        return (TOKENS * loss, (output, loss))
    objective, pullback, extras = jax.vjp(forward, hidden_in, *weights, *vectors, has_aux=True)
    gradients = pullback(jnp.ones_like(objective))
    return (extras[1], extras[0]) + tuple(gradients)
```

```python
import math

import jax
import jax.numpy as jnp
from jax import lax
from jax.sharding import PartitionSpec as P

HEAD = 64


EPSILON = 1e-06


def normalize(vector):
    factor = lax.rsqrt(jnp.sum(vector * vector, axis=-1, keepdims=True) + EPSILON)
    return (vector * factor, factor)


def norm_back(cotangent, normed, factor):
    return factor * (cotangent - normed * jnp.sum(cotangent * normed, axis=-1, keepdims=True))


BF16 = jnp.bfloat16
F32 = jnp.float32


def ring_order(size):
    return list(range(0, size, 2)) + list(range(size - 1, 0, -2))


def ring_steps(size):
    order = ring_order(size)
    ahead = [(order[i], order[(i + 1) % size]) for i in range(size)]
    return ahead, [(b, a) for a, b in ahead]


def ring_block(size, offset):
    order = ring_order(size)
    place = [order.index(i) for i in range(size)]
    target = [order[(place[i] + offset) % size] for i in range(size)]
    return jnp.asarray(target, jnp.int32)[lax.axis_index("dp")]


def use_ring(size):
    return size % 2 == 0 and size <= 16


def ring_gather(shard):
    size = lax.axis_size("dp")
    if not use_ring(size):
        return lax.all_gather(shard, "dp", axis=0, tiled=True)
    ahead, back = ring_steps(size)
    rows, cols = shard.shape
    half = cols // 2
    full = jnp.zeros((rows * size, cols), shard.dtype)
    full = lax.dynamic_update_slice(full, shard, (lax.axis_index("dp") * rows, 0))
    fore, hind = shard, shard
    for step in range(1, size // 2):
        fore = lax.ppermute(fore, "dp", ahead)
        hind = lax.ppermute(hind, "dp", back)
        full = lax.dynamic_update_slice(full, fore, (ring_block(size, -step) * rows, 0))
        full = lax.dynamic_update_slice(full, hind, (ring_block(size, step) * rows, 0))
    fore = lax.ppermute(fore[:, :half], "dp", ahead)
    hind = lax.ppermute(hind[:, half:], "dp", back)
    far = ring_block(size, size // 2) * rows
    full = lax.dynamic_update_slice(full, fore, (far, 0))
    return lax.dynamic_update_slice(full, hind, (far, half))


def ring_reduce(partial):
    size = lax.axis_size("dp")
    if not use_ring(size):
        return lax.psum_scatter(partial, "dp", scatter_dimension=0, tiled=True).astype(F32)
    ahead, back = ring_steps(size)
    rows, cols = partial.shape[0] // size, partial.shape[1]
    half = cols // 2

    def block(offset):
        return lax.dynamic_slice(partial, (ring_block(size, offset) * rows, 0), (rows, cols))

    def total(mine, came):
        return (mine.astype(F32) + came.astype(F32)).astype(BF16)

    far = size // 2
    fore = lax.ppermute(block(far)[:, :half], "dp", ahead)
    hind = lax.ppermute(block(far)[:, half:], "dp", back)
    for step in range(far - 1, 0, -1):
        mine_fore, mine_hind = block(step), block(-step)
        if step == far - 1:
            fore = jnp.concatenate(
                [total(mine_fore[:, :half], fore), mine_fore[:, half:]], axis=1
            )
            hind = jnp.concatenate(
                [mine_hind[:, :half], total(mine_hind[:, half:], hind)], axis=1
            )
        else:
            fore, hind = total(mine_fore, fore), total(mine_hind, hind)
        fore = lax.ppermute(fore, "dp", ahead)
        hind = lax.ppermute(hind, "dp", back)
    return block(0).astype(F32) + fore.astype(F32) + hind.astype(F32)


def tensor_swap(values, bit):
    size = lax.axis_size("tensor")
    return lax.ppermute(values, "tensor", [(i, i ^ bit) for i in range(size)])


def gather_rows(rows):
    across = tensor_swap(rows, 2)
    beside = tensor_swap(rows, 1)
    return jnp.concatenate([rows, beside, across, tensor_swap(across, 1)], axis=0)


def scatter_rows(partial):
    count = partial.shape[0] // 4
    own, beside, across, opposite = (partial[k * count : (k + 1) * count] for k in range(4))
    across = across.astype(F32) + tensor_swap(opposite.astype(BF16), 1).astype(F32)
    across = tensor_swap(across.astype(BF16), 2)
    own = own.astype(F32) + tensor_swap(beside.astype(BF16), 1).astype(F32)
    return own + across.astype(F32)


def all_sum(values):
    dp_size = lax.axis_size("dp")
    if dp_size & (dp_size - 1) or dp_size > 16:
        return lax.psum(values, "dp")
    bit = 1
    while bit < dp_size:
        values = values + lax.ppermute(values, "dp", [(i, i ^ bit) for i in range(dp_size)])
        bit *= 2
    return values


def tensor_sum(values):
    values = values + tensor_swap(values, 1)
    return values + tensor_swap(values, 2)


def slot_order(slot_count):
    count = slot_count // 4
    index = jnp.arange(slot_count, dtype=jnp.int32)
    return ((index // count) ^ lax.axis_index("tensor")) * count + index % count


def masked_scores(query_block, k_seq, first_row, length):
    slot_count = k_seq.shape[0]
    block_rows = query_block.shape[0]
    scores = math.sqrt(query_block.shape[2]) * jnp.einsum(
        "qhd,khd->hqk", query_block, k_seq, preferred_element_type=jnp.float32
    )
    key_ids = slot_order(slot_count).reshape(1, slot_count)
    query_ids = lax.dynamic_slice_in_dim(slot_order(slot_count), first_row, block_rows).reshape(
        block_rows, 1
    )
    allowed = (key_ids <= query_ids) & (key_ids < length)
    return jnp.where(allowed[None], scores, -1e30)


def attend(q_seq, k_seq, v_seq, length, block_rows):
    slot_count = q_seq.shape[0]

    def one_block(first_row):
        query_block = lax.dynamic_slice_in_dim(q_seq, first_row, block_rows, 0)
        scores = masked_scores(query_block, k_seq, first_row, length)
        row_max = jnp.max(scores, axis=-1, keepdims=True)
        exponent = jnp.exp(scores - row_max)
        row_total = jnp.sum(exponent, axis=-1, keepdims=True)
        probabilities = (exponent / row_total).astype(jnp.bfloat16)
        block_out = jnp.einsum(
            "hqk,khd->qhd", probabilities, v_seq, preferred_element_type=jnp.float32
        )
        return (block_out, (row_max + jnp.log(row_total))[..., 0])

    starts = jnp.arange(slot_count // block_rows, dtype=jnp.int32) * block_rows
    block_outs, log_totals = lax.map(one_block, starts)
    return (block_outs.reshape(q_seq.shape), log_totals)


def attend_back(q_seq, k_seq, v_seq, log_totals, grad_seq, length, block_rows):
    slot_count = q_seq.shape[0]
    root_scale = math.sqrt(q_seq.shape[2])

    def one_block(running, block_item):
        first_row, block_totals = block_item
        grad_keys, grad_values = running
        query_block = lax.dynamic_slice_in_dim(q_seq, first_row, block_rows, 0)
        grad_block = lax.dynamic_slice_in_dim(grad_seq, first_row, block_rows, 0)
        scores = masked_scores(query_block, k_seq, first_row, length)
        probabilities = jnp.exp(scores - block_totals[..., None])
        grad_probs = jnp.einsum(
            "qhd,khd->hqk", grad_block, v_seq, preferred_element_type=jnp.float32
        )
        row_delta = jnp.sum(grad_probs * probabilities, axis=-1, keepdims=True)
        grad_scores = (probabilities * (grad_probs - row_delta)).astype(jnp.bfloat16)
        grad_query = root_scale * jnp.einsum(
            "hqk,khd->qhd", grad_scores, k_seq, preferred_element_type=jnp.float32
        )
        grad_keys = grad_keys + root_scale * jnp.einsum(
            "hqk,qhd->khd", grad_scores, query_block, preferred_element_type=jnp.float32
        )
        grad_values = grad_values + jnp.einsum(
            "hqk,qhd->khd",
            probabilities.astype(jnp.bfloat16),
            grad_block,
            preferred_element_type=jnp.float32,
        )
        return ((grad_keys, grad_values), grad_query)

    starts = jnp.arange(slot_count // block_rows, dtype=jnp.int32) * block_rows
    zeros_kv = jnp.zeros(q_seq.shape, jnp.float32)
    (grad_keys, grad_values), grad_queries = lax.scan(
        one_block, (zeros_kv, zeros_kv), (starts, log_totals)
    )
    return (grad_queries.reshape(q_seq.shape), grad_keys, grad_values)


def on_device(
    hidden_in,
    lengths,
    teacher,
    w_query,
    w_key,
    w_value,
    w_attn_out,
    w_up,
    w_gate,
    w_down,
    s_qk,
    alpha_attn,
    alpha_mlp,
    s_up,
    s_gate,
):
    tensor_rank = lax.axis_index("tensor")
    seq_count, local_slots, model_width = hidden_in.shape
    slot_count = local_slots * lax.axis_size("tensor")
    heads_width = w_query.shape[1]
    head_count = heads_width // HEAD
    ff_local = w_up.shape[1]
    block_rows = min(512, slot_count)
    gate_root = math.sqrt(model_width)
    total_slots = slot_count * seq_count * lax.axis_size("dp")
    hidden = hidden_in.reshape(local_slots, model_width)
    teacher = teacher.reshape(local_slots, model_width)
    length = lengths[0]
    w_project = ring_gather(jnp.concatenate([w_query, w_key, w_value], axis=1))
    w_out = ring_gather(w_attn_out.T)
    token_count = all_sum(lengths.astype(F32))[0]
    stream = gather_rows(hidden.astype(BF16))
    projected = jnp.dot(stream, w_project, preferred_element_type=F32)
    q_raw = projected[:, :heads_width].reshape(slot_count, head_count, HEAD)
    k_raw = projected[:, heads_width : 2 * heads_width].reshape(slot_count, head_count, HEAD)
    v_low = projected[:, 2 * heads_width :].astype(BF16).reshape(slot_count, head_count, HEAD)
    q_unit, q_factor = normalize(q_raw)
    k_unit, k_factor = normalize(k_raw)
    qk_gain = lax.dynamic_slice_in_dim(s_qk, tensor_rank * heads_width, heads_width).reshape(
        head_count, HEAD
    )
    q_low = (q_unit * qk_gain).astype(BF16)
    k_low = (k_unit * qk_gain).astype(BF16)
    attended, log_totals = attend(q_low, k_low, v_low, length, block_rows)
    attended_low = attended.reshape(slot_count, heads_width).astype(BF16)
    attn_part = jnp.einsum("rc,dc->rd", attended_low, w_out, preferred_element_type=F32)
    attn_sum = scatter_rows(attn_part)
    attn_unit, attn_factor = normalize(attn_sum)
    first_out, first_factor = normalize(hidden + alpha_attn * (attn_unit - hidden))
    w_pair = ring_gather(jnp.concatenate([w_up, w_gate], axis=1))
    w_low = ring_gather(w_down.T)
    mlp_in = gather_rows(first_out.astype(BF16))
    up_gate = jnp.dot(mlp_in, w_pair, preferred_element_type=F32)
    up_raw = up_gate[:, :ff_local]
    gate_raw = up_gate[:, ff_local:]
    up_gain = lax.dynamic_slice_in_dim(s_up, tensor_rank * ff_local, ff_local)
    gate_gain = lax.dynamic_slice_in_dim(s_gate, tensor_rank * ff_local, ff_local) * gate_root
    scaled_up = up_raw * up_gain
    scaled_gate = gate_raw * gate_gain
    sigmoid_gate = jax.nn.sigmoid(scaled_gate)
    activated = scaled_gate * sigmoid_gate
    hidden_low = (scaled_up * activated).astype(BF16)
    mlp_part = jnp.einsum("rf,df->rd", hidden_low, w_low, preferred_element_type=F32)
    mlp_sum = scatter_rows(mlp_part)
    mlp_unit, mlp_factor = normalize(mlp_sum)
    output, out_factor = normalize(first_out + alpha_mlp * (mlp_unit - first_out))
    slot_ids = tensor_rank * local_slots + lax.broadcasted_iota(jnp.int32, (local_slots, 1), 0)
    valid_mask = (slot_ids < length).astype(F32)
    difference = output - teacher
    error_sum = jnp.sum(jnp.sum(difference * difference, axis=-1, keepdims=True) * valid_mask)
    grad_output = 2.0 * total_slots / token_count * difference * valid_mask
    grad_mixed_two = norm_back(grad_output, output, out_factor)
    grad_alpha_mlp = jnp.sum(grad_mixed_two * (mlp_unit - first_out), axis=0)
    grad_first = grad_mixed_two * (1.0 - alpha_mlp)
    grad_mlp_sum = norm_back(grad_mixed_two * alpha_mlp, mlp_unit, mlp_factor).astype(BF16)
    grad_mlp_rows = gather_rows(grad_mlp_sum)
    grad_low = jnp.einsum("rd,rf->df", grad_mlp_rows, hidden_low, preferred_element_type=F32)
    grad_w_down = ring_reduce(grad_low.astype(BF16)).T
    grad_hidden = jnp.dot(grad_mlp_rows, w_low, preferred_element_type=F32)
    grad_scaled_up = grad_hidden * activated
    grad_scaled_gate = (
        grad_hidden * scaled_up * sigmoid_gate * (1.0 + scaled_gate * (1.0 - sigmoid_gate))
    )
    grad_up_gain = jnp.sum(grad_scaled_up * up_raw, axis=0)
    grad_gate_gain = jnp.sum(grad_scaled_gate * gate_raw, axis=0) * gate_root
    grad_pair = jnp.concatenate(
        [grad_scaled_up * up_gain, grad_scaled_gate * gate_gain], axis=1
    ).astype(BF16)
    grad_mlp_in = jnp.einsum("rf,df->rd", grad_pair, w_pair, preferred_element_type=F32)
    grad_w_pair = jnp.einsum("rd,rf->df", mlp_in, grad_pair, preferred_element_type=F32)
    grad_first = grad_first + scatter_rows(grad_mlp_in)
    grad_w_pair = ring_reduce(grad_w_pair.astype(BF16))
    grad_mixed = norm_back(grad_first, first_out, first_factor)
    grad_alpha_attn = jnp.sum(grad_mixed * (attn_unit - hidden), axis=0)
    grad_input = grad_mixed * (1.0 - alpha_attn)
    grad_attn_sum = norm_back(grad_mixed * alpha_attn, attn_unit, attn_factor).astype(BF16)
    grad_attn_rows = gather_rows(grad_attn_sum)
    grad_out = jnp.einsum("rd,rc->dc", grad_attn_rows, attended_low, preferred_element_type=F32)
    grad_attended = jnp.dot(grad_attn_rows, w_out, preferred_element_type=F32)
    grad_attended = grad_attended.astype(BF16).reshape(slot_count, head_count, HEAD)
    grad_q_low, grad_k_low, grad_v_low = attend_back(
        q_low, k_low, v_low, log_totals, grad_attended, length, block_rows
    )
    grad_gain = jnp.sum(grad_q_low * q_unit + grad_k_low * k_unit, axis=0).reshape(heads_width)
    grad_q = norm_back(grad_q_low * qk_gain, q_unit, q_factor).reshape(slot_count, heads_width)
    grad_k = norm_back(grad_k_low * qk_gain, k_unit, k_factor).reshape(slot_count, heads_width)
    grad_project = jnp.concatenate(
        [grad_q, grad_k, grad_v_low.reshape(slot_count, heads_width)], axis=1
    ).astype(BF16)
    grad_w_project = jnp.einsum("rd,rc->dc", stream, grad_project, preferred_element_type=F32)
    grad_stream = jnp.einsum("rc,dc->rd", grad_project, w_project, preferred_element_type=F32)
    grad_input = grad_input + scatter_rows(grad_stream)
    grad_w_attn = ring_reduce(
        jnp.concatenate([grad_w_project, grad_out], axis=1).astype(BF16)
    )

    def placed(values):
        width = values.shape[0]
        return lax.dynamic_update_slice_in_dim(
            jnp.zeros((width * lax.axis_size("tensor"),), F32), values, tensor_rank * width, 0
        )

    vectors = jnp.concatenate(
        [
            error_sum.reshape(1),
            grad_alpha_attn,
            grad_alpha_mlp,
            placed(grad_gain),
            placed(grad_up_gain),
            placed(grad_gate_gain),
        ]
    )
    vectors = all_sum(tensor_sum(vectors))
    loss = vectors[0] / token_count
    cuts = [1 + model_width * k for k in range(4)] + [1 + 3 * model_width + s_up.shape[0]]
    return (
        loss,
        output[None],
        (grad_input)[None],
        grad_w_attn[:, :heads_width],
        grad_w_attn[:, heads_width : 2 * heads_width],
        grad_w_attn[:, 2 * heads_width : 3 * heads_width],
        grad_w_attn[:, 3 * heads_width :].T,
        grad_w_pair[:, :ff_local],
        grad_w_pair[:, ff_local:],
        grad_w_down,
        vectors[cuts[2] : cuts[3]],
        vectors[cuts[0] : cuts[1]],
        vectors[cuts[1] : cuts[2]],
        vectors[cuts[3] : cuts[4]],
        vectors[cuts[4] :],
    )


def solution(mesh):
    in_specs = (
        P("dp", "tensor", None),
        P("dp"),
        P("dp", "tensor", None),
        P("dp", "tensor"),
        P("dp", "tensor"),
        P("dp", "tensor"),
        P("tensor", "dp"),
        P("dp", "tensor"),
        P("dp", "tensor"),
        P("tensor", "dp"),
        P(),
        P(),
        P(),
        P(),
        P(),
    )
    out_specs = (
        P(),
        P("dp", "tensor", None),
        P("dp", "tensor", None),
        P("dp", "tensor"),
        P("dp", "tensor"),
        P("dp", "tensor"),
        P("tensor", "dp"),
        P("dp", "tensor"),
        P("dp", "tensor"),
        P("tensor", "dp"),
        P(),
        P(),
        P(),
        P(),
        P(),
    )
    return jax.shard_map(
        on_device, mesh=mesh, in_specs=in_specs, out_specs=out_specs, check_vma=False
    )
```

```python
import functools
import math

import jax
import jax.numpy as jnp
from jax import lax
from jax.experimental import pallas as pl
from jax.experimental.pallas import tpu as pltpu
from jax.sharding import PartitionSpec as P

HEAD = 64
LANES = 2 * HEAD


EPSILON = 1e-06


def normalize(vector):
    factor = lax.rsqrt(jnp.sum(vector * vector, axis=-1, keepdims=True) + EPSILON)
    return (vector * factor, factor)


def norm_back(cotangent, normed, factor):
    return factor * (cotangent - normed * jnp.sum(cotangent * normed, axis=-1, keepdims=True))


BF16 = jnp.bfloat16
F32 = jnp.float32


def ring_order(size):
    return list(range(0, size, 2)) + list(range(size - 1, 0, -2))


def ring_steps(size):
    order = ring_order(size)
    ahead = [(order[i], order[(i + 1) % size]) for i in range(size)]
    return ahead, [(b, a) for a, b in ahead]


def ring_block(size, offset):
    order = ring_order(size)
    place = [order.index(i) for i in range(size)]
    target = [order[(place[i] + offset) % size] for i in range(size)]
    return jnp.asarray(target, jnp.int32)[lax.axis_index("dp")]


def use_ring(size):
    return size % 2 == 0 and size <= 16


def place_body(rows, cols, size, *refs):
    blocks = refs[0]
    pieces, full, arrived = refs[1:-2], refs[-2], refs[-1]
    half = cols // 2
    copies = []
    for index, piece in enumerate(pieces):
        target = full.at[pl.ds(blocks[index] * rows, rows)]
        if index == size - 1:
            target = full.at[pl.ds(blocks[index] * rows, rows), pl.ds(0, half)]
        elif index == size:
            target = full.at[pl.ds(blocks[size - 1] * rows, rows), pl.ds(half, cols - half)]
        copies.append(pltpu.make_async_copy(piece, target, arrived.at[index]))
    for copy in copies:
        copy.start()
    for copy in copies:
        copy.wait()


def place_shards(pieces, offsets, rows, cols):
    size = lax.axis_size("dp")
    blocks = jnp.stack([ring_block(size, offset) for offset in offsets])
    anywhere = pl.BlockSpec(memory_space=pl.ANY)
    return pl.pallas_call(
        functools.partial(place_body, rows, cols, size),
        out_shape=jax.ShapeDtypeStruct((rows * size, cols), pieces[0].dtype),
        grid_spec=pltpu.PrefetchScalarGridSpec(
            num_scalar_prefetch=1,
            grid=(),
            in_specs=[anywhere] * len(pieces),
            out_specs=pl.BlockSpec(memory_space=pltpu.VMEM),
            scratch_shapes=[pltpu.SemaphoreType.DMA((len(pieces),))],
        ),
        name="place_shards",
    )(blocks, *pieces)


def ring_gather(shards, before=None):
    size = lax.axis_size("dp")
    if not use_ring(size):
        return [lax.all_gather(shard, "dp", axis=0, tiled=True) for shard in shards], shards
    ahead, back = ring_steps(size)
    if before is not None:
        shards, _ = lax.optimization_barrier((shards, before))
    fore, hind = list(shards), list(shards)
    pieces = [[shard] for shard in shards]
    offsets = [0]
    for step in range(1, size // 2):
        offsets += [-step, step]
        for k in range(len(shards)):
            fore[k] = lax.ppermute(fore[k], "dp", ahead)
            hind[k] = lax.ppermute(hind[k], "dp", back)
            pieces[k] += [fore[k], hind[k]]
    reached = (fore, hind)
    full = []
    for k, shard in enumerate(shards):
        rows, cols = shard.shape
        half = cols // 2
        pieces[k].append(lax.ppermute(fore[k][:, :half], "dp", ahead))
        pieces[k].append(lax.ppermute(hind[k][:, half:], "dp", back))
        full.append(place_shards(pieces[k], offsets + [size // 2], rows, cols))
    return full, reached


def ring_reduce(partial):
    size = lax.axis_size("dp")
    if not use_ring(size):
        return lax.psum_scatter(partial, "dp", scatter_dimension=0, tiled=True).astype(F32)
    ahead, back = ring_steps(size)
    rows, cols = partial.shape[0] // size, partial.shape[1]
    half = cols // 2

    def block(offset):
        return lax.dynamic_slice(partial, (ring_block(size, offset) * rows, 0), (rows, cols))

    def total(mine, came):
        return (mine.astype(F32) + came.astype(F32)).astype(BF16)

    far = size // 2
    fore = lax.ppermute(block(far)[:, :half], "dp", ahead)
    hind = lax.ppermute(block(far)[:, half:], "dp", back)
    for step in range(far - 1, 0, -1):
        mine_fore, mine_hind = block(step), block(-step)
        if step == far - 1:
            fore = jnp.concatenate(
                [total(mine_fore[:, :half], fore), mine_fore[:, half:]], axis=1
            )
            hind = jnp.concatenate(
                [mine_hind[:, :half], total(mine_hind[:, half:], hind)], axis=1
            )
        else:
            fore, hind = total(mine_fore, fore), total(mine_hind, hind)
        fore = lax.ppermute(fore, "dp", ahead)
        hind = lax.ppermute(hind, "dp", back)
    return block(0).astype(F32) + fore.astype(F32) + hind.astype(F32)


def tensor_swap(values, bit):
    size = lax.axis_size("tensor")
    return lax.ppermute(values, "tensor", [(i, i ^ bit) for i in range(size)])


def gather_rows(rows):
    across = tensor_swap(rows, 2)
    beside = tensor_swap(rows, 1)
    return jnp.concatenate([rows, beside, across, tensor_swap(across, 1)], axis=0)


def scatter_rows(partial):
    count = partial.shape[0] // 4
    own, beside, across, opposite = (partial[k * count : (k + 1) * count] for k in range(4))
    across = across.astype(F32) + tensor_swap(opposite.astype(BF16), 1).astype(F32)
    across = tensor_swap(across.astype(BF16), 2)
    own = own.astype(F32) + tensor_swap(beside.astype(BF16), 1).astype(F32)
    return own + across.astype(F32)


def all_sum(values):
    dp_size = lax.axis_size("dp")
    if dp_size & (dp_size - 1) or dp_size > 16:
        return lax.psum(values, "dp")
    bit = 1
    while bit < dp_size:
        values = values + lax.ppermute(values, "dp", [(i, i ^ bit) for i in range(dp_size)])
        bit *= 2
    return values


def tensor_sum(values):
    values = values + tensor_swap(values, 1)
    return values + tensor_swap(values, 2)


def dot_nt(left, right):
    return lax.dot_general(left, right, (((1,), (1,)), ((), ())), preferred_element_type=F32)


def dot_nn(left, right):
    return lax.dot_general(left, right, (((1,), (0,)), ((), ())), preferred_element_type=F32)


def column_pair(values, start, stop):
    piece = values[:, start : min(start + LANES, stop)]
    if piece.shape[1] < LANES:
        piece = jnp.concatenate([piece, jnp.zeros((piece.shape[0], HEAD), piece.dtype)], axis=1)
    return piece


def low_half(rows):
    return lax.broadcasted_iota(jnp.int32, (rows, LANES), 1) < HEAD


def head_sums(values):
    first = low_half(values.shape[0])
    left = jnp.sum(jnp.where(first, values, 0.0), axis=-1, keepdims=True)
    right = jnp.sum(jnp.where(first, 0.0, values), axis=-1, keepdims=True)
    return jnp.where(first, left, right)


def head_norm(values):
    factor = lax.rsqrt(head_sums(values * values) + EPSILON)
    return values * factor, factor


def side_of(values, side):
    first = low_half(values.shape[0])
    zero = jnp.zeros_like(values)
    return jnp.where(first, values, zero) if side == 0 else jnp.where(first, zero, values)


def attend_body(heads, place_ref, proj_ref, gain_ref, low_ref, totals_ref, q_ref, k_ref, v_ref):
    rank, length = place_ref[0], place_ref[1]
    slots = proj_ref.shape[0]
    block = slots // 4
    width = heads * HEAD
    pairs = (heads + 1) // 2
    for a in range(4):
        rows = pl.ds(pl.multiple_of((rank ^ a) * block, block), block)
        raw = proj_ref[rows, :]
        first = low_half(block)
        for j in range(pairs):
            gain = gain_ref[:, j * LANES : (j + 1) * LANES]
            q_unit, _ = head_norm(column_pair(raw, j * LANES, width))
            k_unit, _ = head_norm(column_pair(raw, width + j * LANES, 2 * width))
            at = slice(a * block, (a + 1) * block)
            q_ref[j, at] = (q_unit * gain).astype(BF16)
            k_ref[j, at] = (k_unit * gain).astype(BF16)
            v_ref[j, at] = column_pair(raw, 2 * width + j * LANES, 3 * width).astype(BF16)
    scale = jnp.asarray(math.sqrt(HEAD), BF16)
    here = lax.broadcasted_iota(jnp.int32, (slots, LANES), 0) < length
    counted = jnp.where(here, 1.0, 0.0).astype(BF16)
    causal = lax.broadcasted_iota(jnp.int32, (block, block), 1) <= lax.broadcasted_iota(
        jnp.int32, (block, block), 0
    )
    first_rows = low_half(slots)
    first = low_half(block)
    for j in range(pairs):
        value = jnp.where(here, v_ref[j], jnp.zeros((), BF16))
        with_count = [jnp.where(first_rows, value, counted), jnp.where(first_rows, counted, value)]
        for a in range(4):
            rows = pl.ds(pl.multiple_of((rank ^ a) * block, block), block)
            keys = (a + 1) * block
            parts, logs = [], []
            for side in range(2):
                if 2 * j + side >= heads:
                    parts.append(jnp.zeros((block, LANES), F32))
                    logs.append(jnp.zeros((block, LANES), F32))
                    continue
                query = side_of(q_ref[j, a * block : keys], side) * scale
                weight = jnp.exp(dot_nt(query, k_ref[j, :keys]))
                last = jnp.where(causal, weight[:, a * block :], 0.0)
                weight = jnp.concatenate([weight[:, : a * block], last], axis=1) if a else last
                summed = dot_nn(weight.astype(BF16), with_count[side][:keys])
                count = pltpu.roll(summed, HEAD, 1)
                parts.append(summed / count)
                logs.append(jnp.log(count))
            out = jnp.where(first, parts[0], parts[1])
            log_total = jnp.where(first, logs[0], logs[1])
            totals_ref[j, :, a * block : keys] = log_total.T
            stop = min((j + 1) * LANES, width)
            low_ref[rows, j * LANES : stop] = out[:, : stop - j * LANES].astype(BF16)


def attend(projected, gain, place, heads):
    slots = projected.shape[0]
    pairs = (heads + 1) // 2
    whole = pl.BlockSpec(memory_space=pltpu.VMEM)
    flops = 3 * heads * slots * slots * LANES * 2
    return pl.pallas_call(
        functools.partial(attend_body, heads),
        out_shape=(
            jax.ShapeDtypeStruct((slots, heads * HEAD), BF16),
            jax.ShapeDtypeStruct((pairs, LANES, slots), F32),
            jax.ShapeDtypeStruct((pairs, slots, LANES), BF16),
            jax.ShapeDtypeStruct((pairs, slots, LANES), BF16),
            jax.ShapeDtypeStruct((pairs, slots, LANES), BF16),
        ),
        in_specs=[pl.BlockSpec(memory_space=pltpu.SMEM), whole, whole],
        out_specs=(whole,) * 5,
        cost_estimate=pl.CostEstimate(
            flops=flops, transcendentals=heads * slots * slots, bytes_accessed=projected.size * 4
        ),
        compiler_params=pltpu.CompilerParams(vmem_limit_bytes=56 * 2**20),
        name="attend",
    )(place, projected, gain)


def attend_back_body(
    heads, place_ref, proj_ref, gain_ref, low_ref, totals_ref, q_ref, k_ref, v_ref, grad_ref,
    gq_ref, gk_ref, gv_ref, ggain_ref, dk_ref, dv_ref,
):
    rank = place_ref[0]
    slots = proj_ref.shape[0]
    block = slots // 4
    width = heads * HEAD
    pairs = (heads + 1) // 2
    scale = jnp.asarray(math.sqrt(HEAD), BF16)
    causal = lax.broadcasted_iota(jnp.int32, (block, block), 0) <= lax.broadcasted_iota(
        jnp.int32, (block, block), 1
    )
    top = lax.broadcasted_iota(jnp.int32, (LANES, slots), 0) < HEAD
    for j in range(pairs):
        stop = min((j + 1) * LANES, width)
        key_turned = k_ref[j].T
        gain = gain_ref[:, j * LANES : (j + 1) * LANES]
        dk_ref[...] = jnp.zeros_like(dk_ref)
        dv_ref[...] = jnp.zeros_like(dv_ref)
        gain_sum = jnp.zeros((1, LANES), F32)
        for a in range(4):
            rows = pl.ds(pl.multiple_of((rank ^ a) * block, block), block)
            keys = (a + 1) * block
            grad = column_pair(grad_ref[rows, j * LANES : stop], 0, LANES)
            out = column_pair(low_ref[rows, j * LANES : stop], 0, LANES)
            delta = (grad.astype(F32) * out.astype(F32)).T
            dq_turned = jnp.zeros((LANES, block), F32)
            for side in range(2):
                if 2 * j + side >= heads:
                    continue
                query = side_of(q_ref[j, a * block : keys], side) * scale
                grad_side = side_of(grad, side)
                log_row = totals_ref[j, side * HEAD : side * HEAD + 1, a * block : keys]
                delta_row = jnp.sum(delta[side * HEAD : (side + 1) * HEAD], axis=0, keepdims=True)
                weight = jnp.exp(dot_nt(k_ref[j, :keys], query) - log_row)
                last = jnp.where(causal, weight[a * block :], 0.0)
                weight = jnp.concatenate([weight[: a * block], last], axis=0) if a else last
                grad_weight = dot_nt(v_ref[j, :keys], grad_side)
                grad_score = (weight * (grad_weight - delta_row)).astype(BF16)
                dv_ref[:keys] += dot_nn(weight.astype(BF16), grad_side)
                dk_ref[:keys] += dot_nn(grad_score, query)
                key_side = (
                    jnp.where(top, key_turned, jnp.zeros((), BF16))
                    if side == 0
                    else jnp.where(top, jnp.zeros((), BF16), key_turned)
                )[:, :keys]
                dq_turned += dot_nn(key_side, grad_score)
            dq = dq_turned.T * math.sqrt(HEAD)
            q_unit, factor = head_norm(column_pair(proj_ref[rows, :], j * LANES, width))
            gain_sum += jnp.sum(dq * q_unit, axis=0, keepdims=True)
            scaled = dq * gain
            gq = factor * (scaled - q_unit * head_sums(scaled * q_unit))
            gq_ref[rows, j * LANES : stop] = gq[:, : stop - j * LANES].astype(BF16)
        for a in range(4):
            rows = pl.ds(pl.multiple_of((rank ^ a) * block, block), block)
            dk = dk_ref[a * block : (a + 1) * block]
            k_unit, factor = head_norm(column_pair(proj_ref[rows, :], width + j * LANES, 2 * width))
            gain_sum += jnp.sum(dk * k_unit, axis=0, keepdims=True)
            scaled = dk * gain
            gk = factor * (scaled - k_unit * head_sums(scaled * k_unit))
            gk_ref[rows, j * LANES : stop] = gk[:, : stop - j * LANES].astype(BF16)
            dv = dv_ref[a * block : (a + 1) * block]
            gv_ref[rows, j * LANES : stop] = dv[:, : stop - j * LANES].astype(BF16)
        ggain_ref[:, j * LANES : (j + 1) * LANES] = gain_sum


def attend_back(projected, gain, place, low, totals, q, k, v, grad, heads):
    slots = projected.shape[0]
    pairs = (heads + 1) // 2
    whole = pl.BlockSpec(memory_space=pltpu.VMEM)
    flops = 6 * heads * slots * slots * LANES * 2
    return pl.pallas_call(
        functools.partial(attend_back_body, heads),
        out_shape=(jax.ShapeDtypeStruct((slots, heads * HEAD), BF16),) * 3
        + (jax.ShapeDtypeStruct((1, pairs * LANES), F32),),
        in_specs=[pl.BlockSpec(memory_space=pltpu.SMEM)] + [whole] * 8,
        out_specs=(whole,) * 4,
        scratch_shapes=[pltpu.VMEM((slots, LANES), F32)] * 2,
        cost_estimate=pl.CostEstimate(
            flops=flops, transcendentals=heads * slots * slots, bytes_accessed=projected.size * 4
        ),
        compiler_params=pltpu.CompilerParams(vmem_limit_bytes=56 * 2**20),
        name="attend_back",
    )(place, projected, gain, low, totals, q, k, v, grad)


def on_device(
    hidden_in,
    lengths,
    teacher,
    w_query,
    w_key,
    w_value,
    w_attn_out,
    w_up,
    w_gate,
    w_down,
    s_qk,
    alpha_attn,
    alpha_mlp,
    s_up,
    s_gate,
):
    tensor_rank = lax.axis_index("tensor")
    seq_count, local_slots, model_width = hidden_in.shape
    slot_count = local_slots * lax.axis_size("tensor")
    heads_width = w_query.shape[1]
    head_count = heads_width // HEAD
    ff_local = w_up.shape[1]
    gate_root = math.sqrt(model_width)
    total_slots = slot_count * seq_count * lax.axis_size("dp")
    hidden = hidden_in.reshape(local_slots, model_width)
    teacher = teacher.reshape(local_slots, model_width)
    length = lengths[0]
    (w_attn,), reached = ring_gather(
        [jnp.concatenate([w_query, w_key, w_value, w_attn_out.T], axis=1)]
    )
    w_project, w_out = w_attn[:, : 3 * heads_width], w_attn[:, 3 * heads_width :]
    (w_up_full, w_gate_full), reached = ring_gather([w_up, w_gate], reached)
    (w_low,), reached = ring_gather([w_down.T], reached)
    token_count = all_sum(lengths.astype(F32))[0]
    stream = gather_rows(hidden.astype(BF16))
    projected = jnp.dot(stream, w_project, preferred_element_type=F32)
    qk_gain = lax.dynamic_slice_in_dim(s_qk, tensor_rank * heads_width, heads_width)
    qk_gain = jnp.pad(qk_gain, (0, heads_width % LANES)).reshape(1, -1)
    place = jnp.stack([tensor_rank.astype(jnp.int32), length])
    attended_low, log_totals, q_low, k_low, v_low = attend(projected, qk_gain, place, head_count)
    attn_part = jnp.einsum("rc,dc->rd", attended_low, w_out, preferred_element_type=F32)
    attn_sum = scatter_rows(attn_part)
    attn_unit, attn_factor = normalize(attn_sum)
    first_out, first_factor = normalize(hidden + alpha_attn * (attn_unit - hidden))
    mlp_in = gather_rows(first_out.astype(BF16))
    up_raw = jnp.dot(mlp_in, w_up_full, preferred_element_type=F32)
    gate_raw = jnp.dot(mlp_in, w_gate_full, preferred_element_type=F32)
    up_gain = lax.dynamic_slice_in_dim(s_up, tensor_rank * ff_local, ff_local)
    gate_gain = lax.dynamic_slice_in_dim(s_gate, tensor_rank * ff_local, ff_local) * gate_root
    scaled_up = up_raw * up_gain
    scaled_gate = gate_raw * gate_gain
    sigmoid_gate = jax.nn.sigmoid(scaled_gate)
    activated = scaled_gate * sigmoid_gate
    hidden_low = (scaled_up * activated).astype(BF16)
    mlp_part = jnp.einsum("rf,df->rd", hidden_low, w_low, preferred_element_type=F32)
    mlp_sum = scatter_rows(mlp_part)
    mlp_unit, mlp_factor = normalize(mlp_sum)
    output, out_factor = normalize(first_out + alpha_mlp * (mlp_unit - first_out))
    slot_ids = tensor_rank * local_slots + lax.broadcasted_iota(jnp.int32, (local_slots, 1), 0)
    valid_mask = (slot_ids < length).astype(F32)
    difference = output - teacher
    error_sum = jnp.sum(jnp.sum(difference * difference, axis=-1, keepdims=True) * valid_mask)
    grad_output = 2.0 * total_slots / token_count * difference * valid_mask
    grad_mixed_two = norm_back(grad_output, output, out_factor)
    grad_alpha_mlp = jnp.sum(grad_mixed_two * (mlp_unit - first_out), axis=0)
    grad_first = grad_mixed_two * (1.0 - alpha_mlp)
    grad_mlp_sum = norm_back(grad_mixed_two * alpha_mlp, mlp_unit, mlp_factor).astype(BF16)
    grad_mlp_rows = gather_rows(grad_mlp_sum)
    grad_low = jnp.einsum("rd,rf->df", grad_mlp_rows, hidden_low, preferred_element_type=F32)
    grad_w_down = ring_reduce(grad_low.astype(BF16)).T
    grad_hidden = jnp.dot(grad_mlp_rows, w_low, preferred_element_type=F32)
    grad_scaled_up = grad_hidden * activated
    grad_scaled_gate = (
        grad_hidden * scaled_up * sigmoid_gate * (1.0 + scaled_gate * (1.0 - sigmoid_gate))
    )
    grad_up_gain = jnp.sum(grad_scaled_up * up_raw, axis=0)
    grad_gate_gain = jnp.sum(grad_scaled_gate * gate_raw, axis=0) * gate_root
    grad_up = (grad_scaled_up * up_gain).astype(BF16)
    grad_gate = (grad_scaled_gate * gate_gain).astype(BF16)
    grad_mlp_in = jnp.einsum(
        "rf,df->rd", grad_up, w_up_full, preferred_element_type=F32
    ) + jnp.einsum("rf,df->rd", grad_gate, w_gate_full, preferred_element_type=F32)
    grad_w_up = jnp.einsum("rd,rf->df", mlp_in, grad_up, preferred_element_type=F32)
    grad_w_gate = jnp.einsum("rd,rf->df", mlp_in, grad_gate, preferred_element_type=F32)
    grad_first = grad_first + scatter_rows(grad_mlp_in)
    grad_w_up = ring_reduce(grad_w_up.astype(BF16))
    grad_w_gate = ring_reduce(grad_w_gate.astype(BF16))
    grad_mixed = norm_back(grad_first, first_out, first_factor)
    grad_alpha_attn = jnp.sum(grad_mixed * (attn_unit - hidden), axis=0)
    grad_input = grad_mixed * (1.0 - alpha_attn)
    grad_attn_sum = norm_back(grad_mixed * alpha_attn, attn_unit, attn_factor).astype(BF16)
    grad_attn_rows = gather_rows(grad_attn_sum)
    grad_out = jnp.einsum("rd,rc->dc", grad_attn_rows, attended_low, preferred_element_type=F32)
    grad_attended = jnp.dot(grad_attn_rows, w_out, preferred_element_type=F32)
    grad_q, grad_k, grad_v, grad_gain = attend_back(
        projected,
        qk_gain,
        place,
        attended_low,
        log_totals,
        q_low,
        k_low,
        v_low,
        grad_attended.astype(BF16),
        head_count,
    )
    grad_gain = grad_gain[0, :heads_width]
    grad_project = jnp.concatenate([grad_q, grad_k, grad_v], axis=1)
    grad_w_project = jnp.einsum("rd,rc->dc", stream, grad_project, preferred_element_type=F32)
    grad_stream = jnp.einsum("rc,dc->rd", grad_project, w_project, preferred_element_type=F32)
    grad_input = grad_input + scatter_rows(grad_stream)
    grad_w_attn = ring_reduce(
        jnp.concatenate([grad_w_project, grad_out], axis=1).astype(BF16)
    )

    def placed(values):
        width = values.shape[0]
        return lax.dynamic_update_slice_in_dim(
            jnp.zeros((width * lax.axis_size("tensor"),), F32), values, tensor_rank * width, 0
        )

    vectors = jnp.concatenate(
        [
            error_sum.reshape(1),
            grad_alpha_attn,
            grad_alpha_mlp,
            placed(grad_gain),
            placed(grad_up_gain),
            placed(grad_gate_gain),
        ]
    )
    vectors = all_sum(tensor_sum(vectors))
    loss = vectors[0] / token_count
    cuts = [1 + model_width * k for k in range(4)] + [1 + 3 * model_width + s_up.shape[0]]
    return (
        loss,
        output[None],
        (grad_input)[None],
        grad_w_attn[:, :heads_width],
        grad_w_attn[:, heads_width : 2 * heads_width],
        grad_w_attn[:, 2 * heads_width : 3 * heads_width],
        grad_w_attn[:, 3 * heads_width :].T,
        grad_w_up,
        grad_w_gate,
        grad_w_down,
        vectors[cuts[2] : cuts[3]],
        vectors[cuts[0] : cuts[1]],
        vectors[cuts[1] : cuts[2]],
        vectors[cuts[3] : cuts[4]],
        vectors[cuts[4] :],
    )


def solution(mesh):
    in_specs = (
        P("dp", "tensor", None),
        P("dp"),
        P("dp", "tensor", None),
        P("dp", "tensor"),
        P("dp", "tensor"),
        P("dp", "tensor"),
        P("tensor", "dp"),
        P("dp", "tensor"),
        P("dp", "tensor"),
        P("tensor", "dp"),
        P(),
        P(),
        P(),
        P(),
        P(),
    )
    out_specs = (
        P(),
        P("dp", "tensor", None),
        P("dp", "tensor", None),
        P("dp", "tensor"),
        P("dp", "tensor"),
        P("dp", "tensor"),
        P("tensor", "dp"),
        P("dp", "tensor"),
        P("dp", "tensor"),
        P("tensor", "dp"),
        P(),
        P(),
        P(),
        P(),
        P(),
    )
    return jax.shard_map(
        on_device, mesh=mesh, in_specs=in_specs, out_specs=out_specs, check_vma=False
    )
```

```python
import functools
import math

import jax
import jax.numpy as jnp
from jax import lax
from jax.experimental import pallas as pl
from jax.experimental.pallas import tpu as pltpu
from jax.sharding import PartitionSpec as P

HEAD = 64
LANES = 2 * HEAD


EPSILON = 1e-06


def normalize(vector):
    factor = lax.rsqrt(jnp.sum(vector * vector, axis=-1, keepdims=True) + EPSILON)
    return (vector * factor, factor)


def norm_back(cotangent, normed, factor):
    return factor * (cotangent - normed * jnp.sum(cotangent * normed, axis=-1, keepdims=True))


BF16 = jnp.bfloat16
F32 = jnp.float32


def short_axis(size):
    return size % 2 == 0 and size <= 16


def after(values, *there):
    return lax.optimization_barrier((values, there))[0]


def ring_place(size, index):
    return index // 2 + (index % 2) * (size - 1 - 2 * (index // 2))


def ring_device(size, place):
    place = (place + 2 * size) % size
    later = (2 * place) // size
    return 2 * place + later * (2 * size - 1 - 4 * place)


def ring_steps(size):
    order = [ring_device(size, place) for place in range(size)]
    ahead = [(order[i], order[(i + 1) % size]) for i in range(size)]
    return ahead, [(b, a) for a, b in ahead]


def place_body(rows, cols, size, index, *refs):
    pieces, full, arrived = refs[:-2], refs[-2], refs[-1]
    half = cols // 2
    mine = ring_place(size, index[0])
    copies = []
    for k, piece in enumerate(pieces):
        step = (k + 1) // 2
        source = ring_device(size, mine + (step if k % 2 == 0 else -step))
        span = pl.ds(pl.multiple_of(source * rows, rows), rows)
        target = full.at[span]
        if step == size // 2:
            target = full.at[span, pl.ds(0, half) if k % 2 else pl.ds(half, cols - half)]
        copies.append(pltpu.make_async_copy(piece, target, arrived.at[k]))
    for copy in copies:
        copy.start()
    for copy in copies:
        copy.wait()


class RingGather:
    def __init__(self, shard):
        self.size = lax.axis_size("dp")
        self.fore, self.hind = shard, shard
        self.pieces = [shard]

    def hop(self, *there):
        if not short_axis(self.size):
            return
        ahead, back = ring_steps(self.size)
        fore, hind = self.fore, self.hind
        if there:
            fore, hind = after((fore, hind), *there)
        if len(self.pieces) == self.size - 1:
            half = fore.shape[1] // 2
            fore, hind = fore[:, :half], hind[:, half:]
        self.fore = lax.ppermute(fore, "dp", ahead)
        self.hind = lax.ppermute(hind, "dp", back)
        self.pieces += [self.fore, self.hind]

    def here(self):
        return (self.fore, self.hind)

    def full(self):
        shard = self.pieces[0]
        if not short_axis(self.size):
            return lax.all_gather(shard, "dp", axis=0, tiled=True)
        rows, cols = shard.shape
        return pl.pallas_call(
            functools.partial(place_body, rows, cols, self.size),
            out_shape=jax.ShapeDtypeStruct((rows * self.size, cols), shard.dtype),
            in_specs=[pl.BlockSpec(memory_space=pltpu.SMEM)]
            + [pl.BlockSpec(memory_space=pl.ANY)] * len(self.pieces),
            out_specs=pl.BlockSpec(memory_space=pltpu.VMEM),
            scratch_shapes=[pltpu.SemaphoreType.DMA((len(self.pieces),))],
            name="place_pieces",
        )(lax.axis_index("dp").astype(jnp.int32).reshape(1), *self.pieces)


class RingReduce:
    def __init__(self, partial, *there):
        self.size = lax.axis_size("dp")
        self.partial = partial
        if not short_axis(self.size):
            return
        self.mine = ring_place(self.size, lax.axis_index("dp"))
        self.left = self.size // 2
        half = partial.shape[1] // 2
        block = self.block(self.left)
        self.send((block[:, :half], block[:, half:]), there)

    def block(self, offset):
        rows, cols = self.partial.shape[0] // self.size, self.partial.shape[1]
        device = ring_device(self.size, self.mine + offset)
        return lax.dynamic_slice(self.partial, (device * rows, 0), (rows, cols))

    def send(self, parts, there):
        ahead, back = ring_steps(self.size)
        if there:
            parts = after(parts, *there)
        self.fore = lax.ppermute(parts[0], "dp", ahead)
        self.hind = lax.ppermute(parts[1], "dp", back)
        self.left -= 1

    def hop(self, *there):
        if not short_axis(self.size):
            return
        cols = self.partial.shape[1]

        def total(offset, came, start):
            stop = start + came.shape[1]
            block = self.block(offset)
            sum_part = (block[:, start:stop].astype(F32) + came.astype(F32)).astype(BF16)
            parts = [block[:, :start], sum_part, block[:, stop:]]
            parts = [part for part in parts if part.shape[1]]
            return jnp.concatenate(parts, axis=1) if len(parts) > 1 else sum_part

        fore = total(self.left, self.fore, 0)
        hind = total(-self.left, self.hind, cols - self.hind.shape[1])
        self.send((fore, hind), there)

    def here(self):
        return (self.fore, self.hind) if short_axis(self.size) else ()

    def total(self):
        if not short_axis(self.size):
            return lax.psum_scatter(self.partial, "dp", scatter_dimension=0, tiled=True).astype(F32)
        while self.left > 0:
            self.hop()
        return self.block(0).astype(F32) + self.fore.astype(F32) + self.hind.astype(F32)


def tensor_swap(values, bit):
    size = lax.axis_size("tensor")
    return lax.ppermute(values, "tensor", [(i, i ^ bit) for i in range(size)])


def gather_rows(rows):
    across = tensor_swap(rows, 2)
    beside = tensor_swap(rows, 1)
    return jnp.concatenate([rows, beside, across, tensor_swap(across, 1)], axis=0)


def scatter_rows(partial):
    count = partial.shape[0] // 4
    own, beside, across, opposite = (partial[k * count : (k + 1) * count] for k in range(4))
    across = across.astype(F32) + tensor_swap(opposite.astype(BF16), 1).astype(F32)
    across = tensor_swap(across.astype(BF16), 2)
    own = own.astype(F32) + tensor_swap(beside.astype(BF16), 1).astype(F32)
    return own + across.astype(F32)


def all_sum(values):
    dp_size = lax.axis_size("dp")
    if dp_size & (dp_size - 1) or dp_size > 16:
        return lax.psum(values, "dp")
    bit = 1
    while bit < dp_size:
        values = values + lax.ppermute(values, "dp", [(i, i ^ bit) for i in range(dp_size)])
        bit *= 2
    return values


def tensor_sum(values):
    values = values + tensor_swap(values, 1)
    return values + tensor_swap(values, 2)


def dot_nt(left, right):
    return lax.dot_general(left, right, (((1,), (1,)), ((), ())), preferred_element_type=F32)


def dot_nn(left, right):
    return lax.dot_general(left, right, (((1,), (0,)), ((), ())), preferred_element_type=F32)


def column_pair(values, start, stop):
    piece = values[:, start : min(start + LANES, stop)]
    if piece.shape[1] < LANES:
        piece = jnp.concatenate([piece, jnp.zeros((piece.shape[0], HEAD), piece.dtype)], axis=1)
    return piece


def low_half(rows):
    return lax.broadcasted_iota(jnp.int32, (rows, LANES), 1) < HEAD


def head_sums(values):
    first = low_half(values.shape[0])
    left = jnp.sum(jnp.where(first, values, 0.0), axis=-1, keepdims=True)
    right = jnp.sum(jnp.where(first, 0.0, values), axis=-1, keepdims=True)
    return jnp.where(first, left, right)


def head_norm(values):
    factor = lax.rsqrt(head_sums(values * values) + EPSILON)
    return values * factor, factor


def side_of(values, side):
    first = low_half(values.shape[0])
    zero = jnp.zeros_like(values)
    return jnp.where(first, values, zero) if side == 0 else jnp.where(first, zero, values)


def attend_body(heads, place_ref, proj_ref, gain_ref, low_ref, totals_ref, q_ref, k_ref, v_ref):
    rank, length = place_ref[0], place_ref[1]
    slots = proj_ref.shape[0]
    block = slots // 4
    width = heads * HEAD
    pairs = (heads + 1) // 2
    for a in range(4):
        rows = pl.ds(pl.multiple_of((rank ^ a) * block, block), block)
        raw = proj_ref[rows, :]
        first = low_half(block)
        for j in range(pairs):
            gain = gain_ref[:, j * LANES : (j + 1) * LANES]
            q_unit, _ = head_norm(column_pair(raw, j * LANES, width))
            k_unit, _ = head_norm(column_pair(raw, width + j * LANES, 2 * width))
            at = slice(a * block, (a + 1) * block)
            q_ref[j, at] = (q_unit * gain).astype(BF16)
            k_ref[j, at] = (k_unit * gain).astype(BF16)
            v_ref[j, at] = column_pair(raw, 2 * width + j * LANES, 3 * width).astype(BF16)
    scale = jnp.asarray(math.sqrt(HEAD), BF16)
    here = lax.broadcasted_iota(jnp.int32, (slots, LANES), 0) < length
    counted = jnp.where(here, 1.0, 0.0).astype(BF16)
    causal = lax.broadcasted_iota(jnp.int32, (block, block), 1) <= lax.broadcasted_iota(
        jnp.int32, (block, block), 0
    )
    first_rows = low_half(slots)
    first = low_half(block)
    for j in range(pairs):
        value = jnp.where(here, v_ref[j], jnp.zeros((), BF16))
        with_count = [jnp.where(first_rows, value, counted), jnp.where(first_rows, counted, value)]
        for a in range(4):
            rows = pl.ds(pl.multiple_of((rank ^ a) * block, block), block)
            keys = (a + 1) * block
            parts, logs = [], []
            for side in range(2):
                if 2 * j + side >= heads:
                    parts.append(jnp.zeros((block, LANES), F32))
                    logs.append(jnp.zeros((block, LANES), F32))
                    continue
                query = side_of(q_ref[j, a * block : keys], side) * scale
                weight = jnp.exp(dot_nt(query, k_ref[j, :keys]))
                last = jnp.where(causal, weight[:, a * block :], 0.0)
                weight = jnp.concatenate([weight[:, : a * block], last], axis=1) if a else last
                summed = dot_nn(weight.astype(BF16), with_count[side][:keys])
                count = pltpu.roll(summed, HEAD, 1)
                parts.append(summed / count)
                logs.append(jnp.log(count))
            out = jnp.where(first, parts[0], parts[1])
            log_total = jnp.where(first, logs[0], logs[1])
            totals_ref[j, :, a * block : keys] = log_total.T
            stop = min((j + 1) * LANES, width)
            low_ref[rows, j * LANES : stop] = out[:, : stop - j * LANES].astype(BF16)


def attend(projected, gain, place, heads):
    slots = projected.shape[0]
    pairs = (heads + 1) // 2
    whole = pl.BlockSpec(memory_space=pltpu.VMEM)
    flops = 3 * heads * slots * slots * LANES * 2
    return pl.pallas_call(
        functools.partial(attend_body, heads),
        out_shape=(
            jax.ShapeDtypeStruct((slots, heads * HEAD), BF16),
            jax.ShapeDtypeStruct((pairs, LANES, slots), F32),
            jax.ShapeDtypeStruct((pairs, slots, LANES), BF16),
            jax.ShapeDtypeStruct((pairs, slots, LANES), BF16),
            jax.ShapeDtypeStruct((pairs, slots, LANES), BF16),
        ),
        in_specs=[pl.BlockSpec(memory_space=pltpu.SMEM), whole, whole],
        out_specs=(whole,) * 5,
        cost_estimate=pl.CostEstimate(
            flops=flops, transcendentals=heads * slots * slots, bytes_accessed=projected.size * 4
        ),
        compiler_params=pltpu.CompilerParams(vmem_limit_bytes=56 * 2**20),
        name="attend",
    )(place, projected, gain)


def attend_back_body(
    heads, place_ref, proj_ref, gain_ref, low_ref, totals_ref, q_ref, k_ref, v_ref, grad_ref,
    gq_ref, gk_ref, gv_ref, ggain_ref, dk_ref, dv_ref,
):
    rank = place_ref[0]
    slots = proj_ref.shape[0]
    block = slots // 4
    width = heads * HEAD
    pairs = (heads + 1) // 2
    scale = jnp.asarray(math.sqrt(HEAD), BF16)
    causal = lax.broadcasted_iota(jnp.int32, (block, block), 0) <= lax.broadcasted_iota(
        jnp.int32, (block, block), 1
    )
    top = lax.broadcasted_iota(jnp.int32, (LANES, slots), 0) < HEAD
    for j in range(pairs):
        stop = min((j + 1) * LANES, width)
        key_turned = k_ref[j].T
        gain = gain_ref[:, j * LANES : (j + 1) * LANES]
        dk_ref[...] = jnp.zeros_like(dk_ref)
        dv_ref[...] = jnp.zeros_like(dv_ref)
        gain_sum = jnp.zeros((1, LANES), F32)
        for a in range(4):
            rows = pl.ds(pl.multiple_of((rank ^ a) * block, block), block)
            keys = (a + 1) * block
            grad = column_pair(grad_ref[rows, j * LANES : stop], 0, LANES)
            out = column_pair(low_ref[rows, j * LANES : stop], 0, LANES)
            delta = (grad.astype(F32) * out.astype(F32)).T
            dq_turned = jnp.zeros((LANES, block), F32)
            for side in range(2):
                if 2 * j + side >= heads:
                    continue
                query = side_of(q_ref[j, a * block : keys], side) * scale
                grad_side = side_of(grad, side)
                log_row = totals_ref[j, side * HEAD : side * HEAD + 1, a * block : keys]
                delta_row = jnp.sum(delta[side * HEAD : (side + 1) * HEAD], axis=0, keepdims=True)
                weight = jnp.exp(dot_nt(k_ref[j, :keys], query) - log_row)
                last = jnp.where(causal, weight[a * block :], 0.0)
                weight = jnp.concatenate([weight[: a * block], last], axis=0) if a else last
                grad_weight = dot_nt(v_ref[j, :keys], grad_side)
                grad_score = (weight * (grad_weight - delta_row)).astype(BF16)
                dv_ref[:keys] += dot_nn(weight.astype(BF16), grad_side)
                dk_ref[:keys] += dot_nn(grad_score, query)
                key_side = (
                    jnp.where(top, key_turned, jnp.zeros((), BF16))
                    if side == 0
                    else jnp.where(top, jnp.zeros((), BF16), key_turned)
                )[:, :keys]
                dq_turned += dot_nn(key_side, grad_score)
            dq = dq_turned.T * math.sqrt(HEAD)
            q_unit, factor = head_norm(column_pair(proj_ref[rows, :], j * LANES, width))
            gain_sum += jnp.sum(dq * q_unit, axis=0, keepdims=True)
            scaled = dq * gain
            gq = factor * (scaled - q_unit * head_sums(scaled * q_unit))
            gq_ref[rows, j * LANES : stop] = gq[:, : stop - j * LANES].astype(BF16)
        for a in range(4):
            rows = pl.ds(pl.multiple_of((rank ^ a) * block, block), block)
            dk = dk_ref[a * block : (a + 1) * block]
            k_unit, factor = head_norm(column_pair(proj_ref[rows, :], width + j * LANES, 2 * width))
            gain_sum += jnp.sum(dk * k_unit, axis=0, keepdims=True)
            scaled = dk * gain
            gk = factor * (scaled - k_unit * head_sums(scaled * k_unit))
            gk_ref[rows, j * LANES : stop] = gk[:, : stop - j * LANES].astype(BF16)
            dv = dv_ref[a * block : (a + 1) * block]
            gv_ref[rows, j * LANES : stop] = dv[:, : stop - j * LANES].astype(BF16)
        ggain_ref[:, j * LANES : (j + 1) * LANES] = gain_sum


def attend_back(projected, gain, place, low, totals, q, k, v, grad, heads):
    slots = projected.shape[0]
    pairs = (heads + 1) // 2
    whole = pl.BlockSpec(memory_space=pltpu.VMEM)
    flops = 6 * heads * slots * slots * LANES * 2
    return pl.pallas_call(
        functools.partial(attend_back_body, heads),
        out_shape=(jax.ShapeDtypeStruct((slots, heads * HEAD), BF16),) * 3
        + (jax.ShapeDtypeStruct((1, pairs * LANES), F32),),
        in_specs=[pl.BlockSpec(memory_space=pltpu.SMEM)] + [whole] * 8,
        out_specs=(whole,) * 4,
        scratch_shapes=[pltpu.VMEM((slots, LANES), F32)] * 2,
        cost_estimate=pl.CostEstimate(
            flops=flops, transcendentals=heads * slots * slots, bytes_accessed=projected.size * 4
        ),
        compiler_params=pltpu.CompilerParams(vmem_limit_bytes=56 * 2**20),
        name="attend_back",
    )(place, projected, gain, low, totals, q, k, v, grad)


def on_device(
    hidden_in,
    lengths,
    teacher,
    w_query,
    w_key,
    w_value,
    w_attn_out,
    w_up,
    w_gate,
    w_down,
    s_qk,
    alpha_attn,
    alpha_mlp,
    s_up,
    s_gate,
):
    tensor_rank = lax.axis_index("tensor")
    seq_count, local_slots, model_width = hidden_in.shape
    slot_count = local_slots * lax.axis_size("tensor")
    heads_width = w_query.shape[1]
    head_count = heads_width // HEAD
    ff_local = w_up.shape[1]
    gate_root = math.sqrt(model_width)
    total_slots = slot_count * seq_count * lax.axis_size("dp")
    hidden = hidden_in.reshape(local_slots, model_width)
    teacher = teacher.reshape(local_slots, model_width)
    length = lengths[0]
    attn_ring = RingGather(jnp.concatenate([w_query, w_key, w_value, w_attn_out.T], axis=1))
    pair_ring = RingGather(jnp.concatenate([w_up, w_gate], axis=1))
    low_ring = RingGather(w_down.T)
    attn_ring.hop()
    attn_ring.hop()
    attn_ring.hop()
    pair_ring.hop(attn_ring.here())
    attn_ring.hop()
    w_attn = attn_ring.full()
    w_project, w_out = w_attn[:, : 3 * heads_width], w_attn[:, 3 * heads_width :]
    token_count = all_sum(lengths.astype(F32))[0]
    stream = gather_rows(hidden.astype(BF16))
    projected = jnp.dot(stream, w_project, preferred_element_type=F32)
    qk_gain = lax.dynamic_slice_in_dim(s_qk, tensor_rank * heads_width, heads_width)
    qk_gain = jnp.pad(qk_gain, (0, heads_width % LANES)).reshape(1, -1)
    place = jnp.stack([tensor_rank.astype(jnp.int32), length])
    attended_low, log_totals, q_low, k_low, v_low = attend(projected, qk_gain, place, head_count)
    attended_low = after(attended_low, pair_ring.here())
    pair_ring.hop(attended_low)
    attn_part = jnp.einsum("rc,dc->rd", attended_low, w_out, preferred_element_type=F32)
    attn_sum = scatter_rows(attn_part)
    attn_sum = after(attn_sum, pair_ring.here())
    pair_ring.hop()
    attn_unit, attn_factor = normalize(attn_sum)
    first_out, first_factor = normalize(hidden + alpha_attn * (attn_unit - hidden))
    low_ring.hop(pair_ring.here())
    pair_ring.hop()
    mlp_in = gather_rows(first_out.astype(BF16))
    w_pair = pair_ring.full()
    low_ring.hop()
    low_ring.hop()
    low_ring.hop()
    w_low = low_ring.full()
    up_gate = jnp.dot(mlp_in, w_pair, preferred_element_type=F32)
    up_raw, gate_raw = up_gate[:, :ff_local], up_gate[:, ff_local:]
    up_gain = lax.dynamic_slice_in_dim(s_up, tensor_rank * ff_local, ff_local)
    gate_gain = lax.dynamic_slice_in_dim(s_gate, tensor_rank * ff_local, ff_local) * gate_root
    scaled_up = up_raw * up_gain
    scaled_gate = gate_raw * gate_gain
    sigmoid_gate = jax.nn.sigmoid(scaled_gate)
    activated = scaled_gate * sigmoid_gate
    hidden_low = (scaled_up * activated).astype(BF16)
    mlp_part = jnp.einsum("rf,df->rd", hidden_low, w_low, preferred_element_type=F32)
    mlp_sum = scatter_rows(mlp_part)
    mlp_unit, mlp_factor = normalize(mlp_sum)
    output, out_factor = normalize(first_out + alpha_mlp * (mlp_unit - first_out))
    slot_ids = tensor_rank * local_slots + lax.broadcasted_iota(jnp.int32, (local_slots, 1), 0)
    valid_mask = (slot_ids < length).astype(F32)
    difference = output - teacher
    error_sum = jnp.sum(jnp.sum(difference * difference, axis=-1, keepdims=True) * valid_mask)
    grad_output = 2.0 * total_slots / token_count * difference * valid_mask
    grad_mixed_two = norm_back(grad_output, output, out_factor)
    grad_alpha_mlp = jnp.sum(grad_mixed_two * (mlp_unit - first_out), axis=0)
    grad_first = grad_mixed_two * (1.0 - alpha_mlp)
    grad_mlp_sum = norm_back(grad_mixed_two * alpha_mlp, mlp_unit, mlp_factor).astype(BF16)
    grad_mlp_rows = gather_rows(grad_mlp_sum)
    grad_low = jnp.einsum("rd,rf->df", grad_mlp_rows, hidden_low, preferred_element_type=F32)
    low_reduce = RingReduce(grad_low.astype(BF16))
    grad_hidden = jnp.dot(grad_mlp_rows, w_low, preferred_element_type=F32)
    grad_scaled_up = grad_hidden * activated
    grad_scaled_gate = (
        grad_hidden * scaled_up * sigmoid_gate * (1.0 + scaled_gate * (1.0 - sigmoid_gate))
    )
    grad_up_gain = jnp.sum(grad_scaled_up * up_raw, axis=0)
    grad_gate_gain = jnp.sum(grad_scaled_gate * gate_raw, axis=0) * gate_root
    grad_pair = jnp.concatenate(
        [grad_scaled_up * up_gain, grad_scaled_gate * gate_gain], axis=1
    ).astype(BF16)
    grad_pair = after(grad_pair, low_reduce.here())
    low_reduce.hop()
    grad_mlp_in = jnp.einsum("rf,df->rd", grad_pair, w_pair, preferred_element_type=F32)
    grad_pair, mlp_in = after((grad_pair, mlp_in), low_reduce.here(), grad_mlp_in)
    low_reduce.hop()
    grad_w_pair = jnp.einsum("rd,rf->df", mlp_in, grad_pair, preferred_element_type=F32)
    grad_w_pair = after(grad_w_pair.astype(BF16), low_reduce.here())
    low_reduce.hop()
    pair_reduce = RingReduce(grad_w_pair)
    grad_first = grad_first + scatter_rows(grad_mlp_in)
    grad_w_down = low_reduce.total().T
    grad_first = after(grad_first, pair_reduce.here())
    pair_reduce.hop()
    grad_mixed = norm_back(grad_first, first_out, first_factor)
    grad_alpha_attn = jnp.sum(grad_mixed * (attn_unit - hidden), axis=0)
    grad_input = grad_mixed * (1.0 - alpha_attn)
    grad_attn_sum = norm_back(grad_mixed * alpha_attn, attn_unit, attn_factor).astype(BF16)
    grad_attn_rows = gather_rows(grad_attn_sum)
    grad_attn_rows = after(grad_attn_rows, pair_reduce.here())
    pair_reduce.hop()
    grad_out = jnp.einsum("rd,rc->dc", grad_attn_rows, attended_low, preferred_element_type=F32)
    grad_attended = jnp.dot(grad_attn_rows, w_out, preferred_element_type=F32)
    grad_q, grad_k, grad_v, grad_gain = attend_back(
        projected,
        qk_gain,
        place,
        attended_low,
        log_totals,
        q_low,
        k_low,
        v_low,
        grad_attended.astype(BF16),
        head_count,
    )
    grad_gain = grad_gain[0, :heads_width]
    grad_q = after(grad_q, pair_reduce.here())
    pair_reduce.hop()
    grad_w_pair = pair_reduce.total()
    grad_project = jnp.concatenate([grad_q, grad_k, grad_v], axis=1)
    grad_w_project = jnp.einsum("rd,rc->dc", stream, grad_project, preferred_element_type=F32)
    grad_stream = jnp.einsum("rc,dc->rd", grad_project, w_project, preferred_element_type=F32)
    grad_input = grad_input + scatter_rows(grad_stream)
    attn_reduce = RingReduce(jnp.concatenate([grad_w_project, grad_out], axis=1).astype(BF16))
    grad_w_attn = attn_reduce.total()

    def placed(values):
        width = values.shape[0]
        return lax.dynamic_update_slice_in_dim(
            jnp.zeros((width * lax.axis_size("tensor"),), F32), values, tensor_rank * width, 0
        )

    vectors = jnp.concatenate(
        [
            error_sum.reshape(1),
            grad_alpha_attn,
            grad_alpha_mlp,
            placed(grad_gain),
            placed(grad_up_gain),
            placed(grad_gate_gain),
        ]
    )
    vectors = all_sum(tensor_sum(vectors))
    loss = vectors[0] / token_count
    cuts = [1 + model_width * k for k in range(4)] + [1 + 3 * model_width + s_up.shape[0]]
    return (
        loss,
        output[None],
        (grad_input)[None],
        grad_w_attn[:, :heads_width],
        grad_w_attn[:, heads_width : 2 * heads_width],
        grad_w_attn[:, 2 * heads_width : 3 * heads_width],
        grad_w_attn[:, 3 * heads_width :].T,
        grad_w_pair[:, :ff_local],
        grad_w_pair[:, ff_local:],
        grad_w_down,
        vectors[cuts[2] : cuts[3]],
        vectors[cuts[0] : cuts[1]],
        vectors[cuts[1] : cuts[2]],
        vectors[cuts[3] : cuts[4]],
        vectors[cuts[4] :],
    )


def solution(mesh):
    in_specs = (
        P("dp", "tensor", None),
        P("dp"),
        P("dp", "tensor", None),
        P("dp", "tensor"),
        P("dp", "tensor"),
        P("dp", "tensor"),
        P("tensor", "dp"),
        P("dp", "tensor"),
        P("dp", "tensor"),
        P("tensor", "dp"),
        P(),
        P(),
        P(),
        P(),
        P(),
    )
    out_specs = (
        P(),
        P("dp", "tensor", None),
        P("dp", "tensor", None),
        P("dp", "tensor"),
        P("dp", "tensor"),
        P("dp", "tensor"),
        P("tensor", "dp"),
        P("dp", "tensor"),
        P("dp", "tensor"),
        P("tensor", "dp"),
        P(),
        P(),
        P(),
        P(),
        P(),
    )
    return jax.shard_map(
        on_device, mesh=mesh, in_specs=in_specs, out_specs=out_specs, check_vma=False
    )
```

```python
import functools
import math

import jax
import jax.numpy as jnp
from jax import lax
from jax.experimental import pallas as pl
from jax.experimental.pallas import tpu as pltpu
from jax.sharding import PartitionSpec as P

HEAD = 64
LANES = 2 * HEAD


EPSILON = 1e-06
BF16 = jnp.bfloat16
F32 = jnp.float32
VMEM_LIMIT = 60 * 2**20


def short_axis(size):
    return size % 2 == 0 and size <= 16


def after(values, *there):
    return lax.optimization_barrier((values, there))[0]


def ring_place(size, index):
    return index // 2 + (index % 2) * (size - 1 - 2 * (index // 2))


def ring_device(size, place):
    place = (place + 2 * size) % size
    later = (2 * place) // size
    return 2 * place + later * (2 * size - 1 - 4 * place)


def ring_steps(size):
    order = [ring_device(size, place) for place in range(size)]
    ahead = [(order[i], order[(i + 1) % size]) for i in range(size)]
    return ahead, [(b, a) for a, b in ahead]


def place_pieces(index, pieces, full, arrived):
    if len(pieces) == 1:
        copies = [pltpu.make_async_copy(pieces[0], full, arrived.at[0])]
    else:
        size = len(pieces) - 1
        rows, cols = full.shape[0] // size, full.shape[1]
        half = cols // 2
        mine = ring_place(size, index)
        copies = []
        for k, piece in enumerate(pieces):
            step = (k + 1) // 2
            source = ring_device(size, mine + (step if k % 2 == 0 else -step))
            span = pl.ds(pl.multiple_of(source * rows, rows), rows)
            target = full.at[span]
            if step == size // 2:
                target = full.at[span, pl.ds(0, half) if k % 2 else pl.ds(half, cols - half)]
            copies.append(pltpu.make_async_copy(piece, target, arrived.at[k]))
    for copy in copies:
        copy.start()
    return copies


class RingGather:
    def __init__(self, shard):
        self.size = lax.axis_size("dp")
        self.fore, self.hind = shard, shard
        self.pieces = [shard]
        if not short_axis(self.size):
            self.pieces = [lax.all_gather(shard, "dp", axis=0, tiled=True)]

    def hop(self, *there):
        if not short_axis(self.size):
            return
        ahead, back = ring_steps(self.size)
        fore, hind = self.fore, self.hind
        if there:
            fore, hind = after((fore, hind), *there)
        if len(self.pieces) == self.size - 1:
            half = fore.shape[1] // 2
            fore, hind = fore[:, :half], hind[:, half:]
        self.fore = lax.ppermute(fore, "dp", ahead)
        self.hind = lax.ppermute(hind, "dp", back)
        self.pieces += [self.fore, self.hind]

    def here(self):
        return (self.fore, self.hind)


class RingReduce:
    def __init__(self, partial, *there):
        self.size = lax.axis_size("dp")
        self.partial = partial
        if not short_axis(self.size):
            return
        self.mine = ring_place(self.size, lax.axis_index("dp"))
        self.left = self.size // 2
        half = partial.shape[1] // 2
        block = self.block(self.left)
        self.send((block[:, :half], block[:, half:]), there)

    def block(self, offset):
        rows, cols = self.partial.shape[0] // self.size, self.partial.shape[1]
        device = ring_device(self.size, self.mine + offset)
        return lax.dynamic_slice(self.partial, (device * rows, 0), (rows, cols))

    def send(self, parts, there):
        ahead, back = ring_steps(self.size)
        if there:
            parts = after(parts, *there)
        self.fore = lax.ppermute(parts[0], "dp", ahead)
        self.hind = lax.ppermute(parts[1], "dp", back)
        self.left -= 1

    def hop(self, *there):
        if not short_axis(self.size):
            return
        cols = self.partial.shape[1]

        def total(offset, came, start):
            stop = start + came.shape[1]
            block = self.block(offset)
            sum_part = (block[:, start:stop].astype(F32) + came.astype(F32)).astype(BF16)
            return lax.dynamic_update_slice(block, sum_part, (0, start))

        fore = total(self.left, self.fore, 0)
        hind = total(-self.left, self.hind, cols - self.hind.shape[1])
        self.send((fore, hind), there)

    def here(self):
        return (self.fore, self.hind) if short_axis(self.size) else ()

    def total(self):
        if not short_axis(self.size):
            return lax.psum_scatter(self.partial, "dp", scatter_dimension=0, tiled=True).astype(F32)
        while self.left > 0:
            self.hop()
        return self.block(0).astype(F32) + self.fore.astype(F32) + self.hind.astype(F32)


def tensor_swap(values, bit):
    size = lax.axis_size("tensor")
    return lax.ppermute(values, "tensor", [(i, i ^ bit) for i in range(size)])


def gather_rows(rows, during=lambda: ()):
    across = tensor_swap(rows, 2)
    beside = tensor_swap(rows, 1)
    across = after(across, during())
    return [rows, beside, across, tensor_swap(across, 1)]


def scatter_rows(blocks, during=lambda: ()):
    own, beside, across, opposite = blocks
    across = across.astype(F32) + tensor_swap(opposite, 1).astype(F32)
    across = tensor_swap(across.astype(BF16), 2)
    beside = tensor_swap(beside, 1)
    return [own, beside, after(across, during())]


def all_sum(values):
    dp_size = lax.axis_size("dp")
    if dp_size & (dp_size - 1) or dp_size > 16:
        return lax.psum(values, "dp")
    bit = 1
    while bit < dp_size:
        values = values + lax.ppermute(values, "dp", [(i, i ^ bit) for i in range(dp_size)])
        bit *= 2
    return values


def tensor_sum(values):
    values = values + tensor_swap(values, 1)
    return values + tensor_swap(values, 2)


def dot_nt(left, right):
    return lax.dot_general(left, right, (((1,), (1,)), ((), ())), preferred_element_type=F32)


def dot_nn(left, right):
    return lax.dot_general(left, right, (((1,), (0,)), ((), ())), preferred_element_type=F32)


def column_pair(values, start, stop):
    piece = values[:, start : min(start + LANES, stop)]
    if piece.shape[1] < LANES:
        piece = jnp.concatenate([piece, jnp.zeros((piece.shape[0], HEAD), piece.dtype)], axis=1)
    return piece


def low_half(rows):
    return lax.broadcasted_iota(jnp.int32, (rows, LANES), 1) < HEAD


def head_sums(values):
    first = low_half(values.shape[0])
    left = jnp.sum(jnp.where(first, values, 0.0), axis=-1, keepdims=True)
    right = jnp.sum(jnp.where(first, 0.0, values), axis=-1, keepdims=True)
    return jnp.where(first, left, right)


def head_norm(values):
    factor = lax.rsqrt(head_sums(values * values) + EPSILON)
    return values * factor, factor


def side_of(values, side):
    first = low_half(values.shape[0])
    zero = jnp.zeros_like(values)
    return jnp.where(first, values, zero) if side == 0 else jnp.where(first, zero, values)


def kernel_call(body, out_shape, scalars, arrays, scratch=(), anywhere=0):
    whole = pl.BlockSpec(memory_space=pltpu.VMEM)
    return pl.pallas_call(
        body,
        out_shape=out_shape,
        in_specs=[pl.BlockSpec(memory_space=pltpu.SMEM)]
        + [pl.BlockSpec(memory_space=pl.ANY)] * anywhere
        + [whole] * (len(arrays) - anywhere),
        out_specs=jax.tree.map(lambda _: whole, out_shape),
        scratch_shapes=list(scratch),
        cost_estimate=pl.CostEstimate(flops=1, transcendentals=0, bytes_accessed=1),
        compiler_params=pltpu.CompilerParams(vmem_limit_bytes=VMEM_LIMIT),
        name=(body.func if isinstance(body, functools.partial) else body).__name__,
    )(scalars, *arrays)


def shaped(dtype, *shape):
    return jax.ShapeDtypeStruct(shape, dtype)


def rank_rows(rank, slot_block, block):
    return pl.ds(pl.multiple_of((rank ^ slot_block) * block, block), block)


def attend_body(heads, count, scalars, *refs):
    pieces, (x0, x1, x2, x3, gain_ref) = refs[:count], refs[count : count + 5]
    (w_ref, raw_ref, low_ref, totals_ref, q_ref, k_ref, v_ref) = refs[count + 5 : count + 12]
    parts_out = refs[count + 12 : count + 16]
    arrived = refs[count + 16]
    rank, length = scalars[0], scalars[1]
    block = x0.shape[0]
    slots = 4 * block
    width = heads * HEAD
    pairs = (heads + 1) // 2
    for copy in place_pieces(scalars[2], pieces, w_ref, arrived):
        copy.wait()
    for k, x_ref in enumerate((x0, x1, x2, x3)):
        at = pl.ds(pl.multiple_of((rank ^ k) * block, block), block)
        raw = dot_nn(x_ref[...], w_ref[:, : 3 * width + HEAD])
        for j in range(pairs):
            gain = gain_ref[:, j * LANES : (j + 1) * LANES]
            q_raw = column_pair(raw, j * LANES, width)
            k_raw = column_pair(raw, width + j * LANES, 2 * width)
            raw_ref[j, at] = q_raw
            raw_ref[pairs + j, at] = k_raw
            q_ref[j, at] = (head_norm(q_raw)[0] * gain).astype(BF16)
            k_ref[j, at] = (head_norm(k_raw)[0] * gain).astype(BF16)
            v_ref[j, at] = column_pair(raw, 2 * width + j * LANES, 3 * width).astype(BF16)
    scale = jnp.asarray(math.sqrt(HEAD), BF16)
    here = lax.broadcasted_iota(jnp.int32, (slots, LANES), 0) < length
    counted = jnp.where(here, 1.0, 0.0).astype(BF16)
    causal = lax.broadcasted_iota(jnp.int32, (block, block), 1) <= lax.broadcasted_iota(
        jnp.int32, (block, block), 0
    )
    first_rows = low_half(slots)
    first = low_half(block)
    for j in range(pairs):
        value = jnp.where(here, v_ref[j], jnp.zeros((), BF16))
        with_count = [jnp.where(first_rows, value, counted), jnp.where(first_rows, counted, value)]
        for a in range(4):
            keys = (a + 1) * block
            parts, logs = [], []
            for side in range(2):
                if 2 * j + side >= heads:
                    parts.append(jnp.zeros((block, LANES), F32))
                    logs.append(jnp.zeros((block, LANES), F32))
                    continue
                query = side_of(q_ref[j, a * block : keys], side) * scale
                weight = jnp.exp(dot_nt(query, k_ref[j, :keys]))
                last = jnp.where(causal, weight[:, a * block :], 0.0)
                weight = jnp.concatenate([weight[:, : a * block], last], axis=1) if a else last
                summed = dot_nn(weight.astype(BF16), with_count[side][:keys])
                total = pltpu.roll(summed, HEAD, 1)
                parts.append(summed / total)
                logs.append(jnp.log(total))
            out = jnp.where(first, parts[0], parts[1])
            log_total = jnp.where(first, logs[0], logs[1])
            totals_ref[j, :, a * block : keys] = log_total.T
            stop = min((j + 1) * LANES, width)
            low_ref[rank_rows(rank, a, block), j * LANES : stop] = out[
                :, : stop - j * LANES
            ].astype(BF16)
    w_out = w_ref[:, 3 * width : 4 * width]
    for k, part_ref in enumerate(parts_out):
        part_ref[...] = dot_nt(low_ref[k * block : (k + 1) * block], w_out).astype(BF16)


def attend(scalars, pieces, blocks, gain, heads):
    block, model = blocks[0].shape
    slots = 4 * block
    pairs = (heads + 1) // 2
    low = shaped(BF16, pairs, slots, LANES)
    out_shape = [
        shaped(BF16, model, 4 * heads * HEAD),
        shaped(F32, 2 * pairs, slots, LANES),
        shaped(BF16, slots, heads * HEAD),
        shaped(F32, pairs, LANES, slots),
        low,
        low,
        low,
    ] + [shaped(BF16, block, model)] * 4
    out = kernel_call(
        functools.partial(attend_body, heads, len(pieces)),
        out_shape,
        scalars,
        [*pieces, *blocks, gain],
        [pltpu.SemaphoreType.DMA((len(pieces),))],
        anywhere=len(pieces),
    )
    return out[:7], out[7:]


def attend_back_body(
    heads, scalars, g0, g1, g2, g3, w_ref, gain_ref, raw_ref, low_ref, totals_ref, q_ref, k_ref,
    v_ref, grad_ref, ggain_ref, p0, p1, p2, p3, ga_ref, dk_ref, dv_ref, gq_ref, gk_ref, gv_ref,
):
    rank = scalars[0]
    block = g0.shape[0]
    slots = 4 * block
    width = heads * HEAD
    pairs = (heads + 1) // 2
    w_out = w_ref[:, 3 * width : 4 * width]
    for k, g_ref in enumerate((g0, g1, g2, g3)):
        ga_ref[k * block : (k + 1) * block] = dot_nn(g_ref[...], w_out).astype(BF16)
    scale = jnp.asarray(math.sqrt(HEAD), BF16)
    causal = lax.broadcasted_iota(jnp.int32, (block, block), 0) <= lax.broadcasted_iota(
        jnp.int32, (block, block), 1
    )
    top = lax.broadcasted_iota(jnp.int32, (LANES, slots), 0) < HEAD
    for j in range(pairs):
        stop = min((j + 1) * LANES, width)
        key_turned = k_ref[j].T
        key_sides = [
            jnp.where(top, key_turned, jnp.zeros((), BF16)),
            jnp.where(top, jnp.zeros((), BF16), key_turned),
        ]
        gain = gain_ref[:, j * LANES : (j + 1) * LANES]
        dk_ref[...] = jnp.zeros_like(dk_ref)
        dv_ref[...] = jnp.zeros_like(dv_ref)
        gain_sum = jnp.zeros((1, LANES), F32)
        for a in range(4):
            rows = rank_rows(rank, a, block)
            keys = (a + 1) * block
            grad = column_pair(ga_ref[rows, j * LANES : stop], 0, LANES)
            out = column_pair(low_ref[rows, j * LANES : stop], 0, LANES)
            delta = (grad.astype(F32) * out.astype(F32)).T
            dq_turned = jnp.zeros((LANES, block), F32)
            for side in range(2):
                if 2 * j + side >= heads:
                    continue
                query = side_of(q_ref[j, a * block : keys], side) * scale
                grad_side = side_of(grad, side)
                log_row = totals_ref[j, side * HEAD : side * HEAD + 1, a * block : keys]
                delta_row = jnp.sum(delta[side * HEAD : (side + 1) * HEAD], axis=0, keepdims=True)
                weight = jnp.exp(dot_nt(k_ref[j, :keys], query) - log_row)
                last = jnp.where(causal, weight[a * block :], 0.0)
                weight = jnp.concatenate([weight[: a * block], last], axis=0) if a else last
                grad_weight = dot_nt(v_ref[j, :keys], grad_side)
                grad_score = (weight * (grad_weight - delta_row)).astype(BF16)
                dv_ref[:keys] += dot_nn(weight.astype(BF16), grad_side)
                dk_ref[:keys] += dot_nn(grad_score, query)
                dq_turned += dot_nn(key_sides[side][:, :keys], grad_score)
            dq = dq_turned.T * math.sqrt(HEAD)
            q_unit, factor = head_norm(raw_ref[j, a * block : keys])
            gain_sum += jnp.sum(dq * q_unit, axis=0, keepdims=True)
            scaled = dq * gain
            gq = factor * (scaled - q_unit * head_sums(scaled * q_unit))
            gq_ref[rows, j * LANES : stop] = gq[:, : stop - j * LANES].astype(BF16)
        for a in range(4):
            rows = rank_rows(rank, a, block)
            at = slice(a * block, (a + 1) * block)
            dk = dk_ref[at]
            k_unit, factor = head_norm(raw_ref[pairs + j, at])
            gain_sum += jnp.sum(dk * k_unit, axis=0, keepdims=True)
            scaled = dk * gain
            gk = factor * (scaled - k_unit * head_sums(scaled * k_unit))
            gk_ref[rows, j * LANES : stop] = gk[:, : stop - j * LANES].astype(BF16)
            gv_ref[rows, j * LANES : stop] = dv_ref[at][:, : stop - j * LANES].astype(BF16)
        ggain_ref[:, j * LANES : (j + 1) * LANES] = gain_sum
    w_project = w_ref[:, : 3 * width]
    for k, part_ref in enumerate((p0, p1, p2, p3)):
        at = slice(k * block, (k + 1) * block)
        grad = jnp.concatenate([gq_ref[at], gk_ref[at], gv_ref[at]], axis=1)
        grad_ref[at] = grad
        part_ref[...] = dot_nt(grad, w_project).astype(BF16)


def attend_back(scalars, grads, w_attn, gain, kept, heads):
    block, model = grads[0].shape
    slots = 4 * block
    width = heads * HEAD
    pairs = (heads + 1) // 2
    out_shape = [shaped(BF16, slots, 3 * width), shaped(F32, 1, pairs * LANES)] + [
        shaped(BF16, block, model)
    ] * 4
    return kernel_call(
        functools.partial(attend_back_body, heads),
        out_shape,
        scalars,
        [*grads, w_attn, gain, *kept],
        [pltpu.VMEM((slots, width), BF16)]
        + [pltpu.VMEM((slots, LANES), F32)] * 2
        + [pltpu.VMEM((slots, width), BF16)] * 3,
    )


def row_norm(values):
    factor = lax.rsqrt(jnp.sum(values * values, axis=-1, keepdims=True) + EPSILON)
    return values * factor, factor


def row_norm_back(grad, unit, factor):
    return factor * (grad - unit * jnp.sum(grad * unit, axis=-1, keepdims=True))


def branch_sum(parts):
    own, beside, across = (part[...].astype(F32) for part in parts)
    return own + beside + across


def first_norm_body(scalars, own, beside, across, hidden_ref, alpha_ref, unit_ref, out_ref, low_ref, factors_ref):
    unit, unit_factor = row_norm(branch_sum((own, beside, across)))
    hidden = hidden_ref[...]
    out, factor = row_norm(hidden + alpha_ref[...] * (unit - hidden))
    unit_ref[...] = unit
    out_ref[...] = out
    low_ref[...] = out.astype(BF16)
    lane = lax.broadcasted_iota(jnp.int32, factors_ref.shape, 1)
    factors_ref[...] = jnp.where(lane == 0, unit_factor, factor)


def first_norm(scalars, parts, hidden, alpha):
    rows, model = hidden.shape
    full = shaped(F32, rows, model)
    return kernel_call(
        first_norm_body,
        [full, full, shaped(BF16, rows, model), shaped(F32, rows, LANES)],
        scalars,
        [*parts, hidden, alpha.reshape(1, model)],
    )


def loss_body(
    total_slots, scalars, own, beside, across, first_ref, teacher_ref, alpha_ref, tokens_ref,
    out_ref, grad_ref, rest_ref, sums_ref,
):
    rank, length = scalars[0], scalars[1]
    unit, unit_factor = row_norm(branch_sum((own, beside, across)))
    first, alpha = first_ref[...], alpha_ref[...]
    out, factor = row_norm(first + alpha * (unit - first))
    out_ref[...] = out
    rows = out.shape[0]
    slot = rank * rows + lax.broadcasted_iota(jnp.int32, (rows, 1), 0)
    difference = jnp.where(slot < length, out - teacher_ref[...], 0.0)
    mixed = row_norm_back(2.0 * total_slots / tokens_ref[...] * difference, out, factor)
    rest_ref[...] = mixed * (1.0 - alpha)
    grad_ref[...] = row_norm_back(mixed * alpha, unit, unit_factor).astype(BF16)
    sums_ref[0:1] = jnp.sum(difference * difference, axis=0, keepdims=True)
    sums_ref[1:2] = jnp.sum(mixed * (unit - first), axis=0, keepdims=True)


def loss_and_grad(scalars, parts, first, teacher, alpha, tokens, total_slots):
    rows, model = first.shape
    full = shaped(F32, rows, model)
    return kernel_call(
        functools.partial(loss_body, total_slots),
        [full, shaped(BF16, rows, model), full, shaped(F32, 2, model)],
        scalars,
        [*parts, first, teacher, alpha.reshape(1, model), tokens.reshape(1, 1)],
    )


def first_back_body(
    scalars, own, beside, across, rest_ref, first_ref, unit_ref, hidden_ref, alpha_ref, factors_ref,
    grad_ref, out_ref, sums_ref,
):
    grad = rest_ref[...] + branch_sum((own, beside, across))
    alpha, unit = alpha_ref[...], unit_ref[...]
    mixed = row_norm_back(grad, first_ref[...], factors_ref[:, 1:2])
    sums_ref[...] = jnp.sum(mixed * (unit - hidden_ref[...]), axis=0, keepdims=True)
    out_ref[...] = mixed * (1.0 - alpha)
    grad_ref[...] = row_norm_back(mixed * alpha, unit, factors_ref[:, 0:1]).astype(BF16)


def first_back(scalars, parts, rest, first, unit, hidden, alpha, factors):
    rows, model = first.shape
    return kernel_call(
        first_back_body,
        [shaped(BF16, rows, model), shaped(F32, rows, model), shaped(F32, 1, model)],
        scalars,
        [*parts, rest, first, unit, hidden, alpha.reshape(1, model), factors],
    )


def feed_body(count, scalars, *refs):
    pieces, x_refs = refs[:count], refs[count : count + 4]
    gains_ref = refs[count + 4]
    w_ref, up_ref, gate_ref, hidden_ref = refs[count + 5 : count + 9]
    parts_out, arrived = refs[count + 9 : count + 13], refs[count + 13]
    ff = gains_ref.shape[1]
    block = x_refs[0].shape[0]
    for copy in place_pieces(scalars[2], pieces, w_ref, arrived):
        copy.wait()
    for k in (3, 2, 1, 0):
        at = slice(k * block, (k + 1) * block)
        x = x_refs[k][...]
        up = dot_nn(x, w_ref[:, :ff])
        gate = dot_nn(x, w_ref[:, ff : 2 * ff])
        scaled = gate * gains_ref[1:2]
        hidden = (up * gains_ref[0:1] * (scaled * jax.nn.sigmoid(scaled))).astype(BF16)
        up_ref[at] = up.astype(BF16)
        gate_ref[at] = gate.astype(BF16)
        hidden_ref[at] = hidden
        parts_out[k][...] = dot_nt(hidden, w_ref[:, 2 * ff :]).astype(BF16)


def feed(scalars, pieces, blocks, gains):
    block, model = blocks[0].shape
    ff = gains.shape[1]
    rows = shaped(BF16, 4 * block, ff)
    out = kernel_call(
        functools.partial(feed_body, len(pieces)),
        [shaped(BF16, model, 3 * ff), rows, rows, rows] + [shaped(BF16, block, model)] * 4,
        scalars,
        [*pieces, *blocks, gains],
        [pltpu.SemaphoreType.DMA((len(pieces),))],
        anywhere=len(pieces),
    )
    return out[:4], out[4:]


def feed_back_body(scalars, g0, g1, g2, g3, w_ref, up_ref, gate_ref, gains_ref, grad_ref, sums_ref, p0, p1, p2, p3):
    ff = gains_ref.shape[1]
    block = g0.shape[0]
    grads, parts = (g0, g1, g2, g3), (p0, p1, p2, p3)
    up_gain, gate_gain = gains_ref[0:1], gains_ref[1:2]
    sums_ref[...] = jnp.zeros_like(sums_ref)
    for k in (3, 2, 1, 0):
        at = slice(k * block, (k + 1) * block)
        grad = dot_nn(grads[k][...], w_ref[:, 2 * ff :])
        up, gate = up_ref[at].astype(F32), gate_ref[at].astype(F32)
        scaled = gate * gate_gain
        chance = jax.nn.sigmoid(scaled)
        by_up = grad * (scaled * chance)
        by_gate = grad * (up * up_gain) * chance * (1.0 + scaled * (1.0 - chance))
        sums_ref[0:1] += jnp.sum(by_up * up, axis=0, keepdims=True)
        sums_ref[1:2] += jnp.sum(by_gate * gate, axis=0, keepdims=True)
        grad_ref[at, :ff] = (by_up * up_gain).astype(BF16)
        grad_ref[at, ff:] = (by_gate * gate_gain).astype(BF16)
        parts[k][...] = dot_nt(grad_ref[at], w_ref[:, : 2 * ff]).astype(BF16)


def feed_back(scalars, grads, w_feed, up, gate, gains):
    block, model = grads[0].shape
    ff = gains.shape[1]
    return kernel_call(
        feed_back_body,
        [shaped(BF16, 4 * block, 2 * ff), shaped(F32, 2, ff)] + [shaped(BF16, block, model)] * 4,
        scalars,
        [*grads, w_feed, up, gate, gains],
    )


def turned_dot(left, right):
    return jnp.einsum("rd,rf->df", left, right, preferred_element_type=F32).astype(BF16)


def on_device(
    hidden_in,
    lengths,
    teacher,
    w_query,
    w_key,
    w_value,
    w_attn_out,
    w_up,
    w_gate,
    w_down,
    s_qk,
    alpha_attn,
    alpha_mlp,
    s_up,
    s_gate,
):
    tensor_rank = lax.axis_index("tensor")
    seq_count, local_slots, model_width = hidden_in.shape
    slot_count = local_slots * lax.axis_size("tensor")
    heads_width = w_query.shape[1]
    head_count = heads_width // HEAD
    ff_local = w_up.shape[1]
    gate_root = math.sqrt(model_width)
    total_slots = slot_count * seq_count * lax.axis_size("dp")
    hidden = hidden_in.reshape(local_slots, model_width)
    teacher = teacher.reshape(local_slots, model_width)
    length = lengths[0]
    scalars = jnp.stack(
        [tensor_rank.astype(jnp.int32), length, lax.axis_index("dp").astype(jnp.int32)]
    )
    own_part = lambda vector, width: lax.dynamic_slice_in_dim(vector, tensor_rank * width, width)
    qk_gain = jnp.pad(own_part(s_qk, heads_width), (0, heads_width % LANES)).reshape(1, -1)
    gains = jnp.stack([own_part(s_up, ff_local), own_part(s_gate, ff_local) * gate_root])

    attn_ring = RingGather(jnp.concatenate([w_query, w_key, w_value, w_attn_out.T], axis=1))
    feed_ring = RingGather(jnp.concatenate([w_up, w_gate, w_down.T], axis=1))
    attn_ring.hop()
    attn_ring.hop()
    attn_ring.hop()
    attn_ring.hop()
    feed_ring.hop(attn_ring.here())
    stream = gather_rows(hidden.astype(BF16))
    kept, parts = attend(scalars, attn_ring.pieces, stream, qk_gain, head_count)
    w_attn, kept = kept[0], kept[1:]

    def feed_step():
        there = feed_ring.here()
        feed_ring.hop()
        return there

    parts = scatter_rows(parts, feed_step)
    attn_unit, first_out, first_low, factors = first_norm(scalars, parts, hidden, alpha_attn)
    mlp_in = gather_rows(first_low, feed_step)
    feed_ring.hop()
    token_count = all_sum(lengths.astype(F32))[0]
    (w_feed, up_raw, gate_raw, hidden_low), parts = feed(
        scalars, feed_ring.pieces, mlp_in, gains
    )
    parts = scatter_rows(parts)
    output, grad_mlp_sum, grad_first, loss_sums = loss_and_grad(
        scalars, parts, first_out, teacher, alpha_mlp, token_count, total_slots
    )

    grad_mlp = gather_rows(grad_mlp_sum)
    grad_low = turned_dot(jnp.concatenate(grad_mlp, axis=0), hidden_low)
    low_reduce = RingReduce(grad_low)
    grad_pair, ff_sums, *parts = feed_back(scalars, grad_mlp, w_feed, up_raw, gate_raw, gains)
    low_reduce.hop(grad_pair)
    mlp_rows = jnp.concatenate(mlp_in, axis=0)
    grad_w_up = turned_dot(mlp_rows, grad_pair[:, :ff_local])
    low_reduce.hop(grad_w_up)
    grad_w_gate = turned_dot(mlp_rows, grad_pair[:, ff_local:])
    low_reduce.hop(grad_w_gate)
    parts = scatter_rows(parts)
    pair_reduce = RingReduce(
        jnp.concatenate([grad_w_up, grad_w_gate], axis=1), low_reduce.here()
    )
    grad_w_down = low_reduce.total().T
    grad_attn_sum, grad_input, attn_sums = first_back(
        scalars, parts, grad_first, first_out, attn_unit, hidden, alpha_attn, factors
    )

    def pair_step():
        there = pair_reduce.here()
        pair_reduce.hop()
        return there

    grad_attn = gather_rows(grad_attn_sum, pair_step)
    grad_project, gain_sums, *parts = attend_back(
        scalars, grad_attn, w_attn, qk_gain, kept, head_count
    )
    parts = scatter_rows(parts)
    pair_reduce.hop(grad_project)
    grad_w_attn = jnp.concatenate(
        [
            turned_dot(jnp.concatenate(stream, axis=0), grad_project),
            turned_dot(jnp.concatenate(grad_attn, axis=0), kept[1]),
        ],
        axis=1,
    )
    pair_reduce.hop(grad_w_attn)
    attn_reduce = RingReduce(grad_w_attn, pair_reduce.here())
    grad_w_pair = pair_reduce.total()
    grad_input = grad_input + sum(part.astype(F32) for part in parts)
    grad_w_attn = attn_reduce.total()

    def placed(values):
        width = values.shape[0]
        return lax.dynamic_update_slice_in_dim(
            jnp.zeros((width * lax.axis_size("tensor"),), F32), values, tensor_rank * width, 0
        )

    vectors = jnp.concatenate(
        [
            jnp.sum(loss_sums[0]).reshape(1),
            attn_sums[0],
            loss_sums[1],
            placed(gain_sums[0, :heads_width]),
            placed(ff_sums[0]),
            placed(ff_sums[1] * gate_root),
        ]
    )
    vectors = all_sum(tensor_sum(vectors))
    loss = vectors[0] / token_count
    cuts = [1 + model_width * k for k in range(4)] + [1 + 3 * model_width + s_up.shape[0]]
    return (
        loss,
        output[None],
        grad_input[None],
        grad_w_attn[:, :heads_width],
        grad_w_attn[:, heads_width : 2 * heads_width],
        grad_w_attn[:, 2 * heads_width : 3 * heads_width],
        grad_w_attn[:, 3 * heads_width :].T,
        grad_w_pair[:, :ff_local],
        grad_w_pair[:, ff_local:],
        grad_w_down,
        vectors[cuts[2] : cuts[3]],
        vectors[cuts[0] : cuts[1]],
        vectors[cuts[1] : cuts[2]],
        vectors[cuts[3] : cuts[4]],
        vectors[cuts[4] :],
    )


def solution(mesh):
    in_specs = (
        P("dp", "tensor", None),
        P("dp"),
        P("dp", "tensor", None),
        P("dp", "tensor"),
        P("dp", "tensor"),
        P("dp", "tensor"),
        P("tensor", "dp"),
        P("dp", "tensor"),
        P("dp", "tensor"),
        P("tensor", "dp"),
        P(),
        P(),
        P(),
        P(),
        P(),
    )
    out_specs = (
        P(),
        P("dp", "tensor", None),
        P("dp", "tensor", None),
        P("dp", "tensor"),
        P("dp", "tensor"),
        P("dp", "tensor"),
        P("tensor", "dp"),
        P("dp", "tensor"),
        P("dp", "tensor"),
        P("tensor", "dp"),
        P(),
        P(),
        P(),
        P(),
        P(),
    )
    return jax.shard_map(
        on_device, mesh=mesh, in_specs=in_specs, out_specs=out_specs, check_vma=False
    )
```

```python
import functools
import math

import jax
import jax.numpy as jnp
from jax import lax
from jax.experimental import pallas as pl
from jax.experimental.pallas import tpu as pltpu
from jax.sharding import PartitionSpec as P

HEAD = 64
LANES = 2 * HEAD


EPSILON = 1e-06
BF16 = jnp.bfloat16
F32 = jnp.float32
MEGA = 2**20


def short_axis(size):
    return size % 2 == 0 and size <= 16


class Order:
    def __init__(self, token):
        self.token = token

    def tie(self, values):
        values, self.token = lax.optimization_barrier((values, self.token))
        return values


def ring_place(size, index):
    return index // 2 + (index % 2) * (size - 1 - 2 * (index // 2))


def ring_device(size, place):
    place = (place + 2 * size) % size
    later = (2 * place) // size
    return 2 * place + later * (2 * size - 1 - 4 * place)


def ring_steps(size):
    order = [ring_device(size, place) for place in range(size)]
    ahead = [(order[i], order[(i + 1) % size]) for i in range(size)]
    return ahead, [(b, a) for a, b in ahead]


def place_pieces(index, pieces, full, arrived):
    if len(pieces) == 1:
        copies = [pltpu.make_async_copy(pieces[0], full, arrived.at[0])]
    else:
        size = len(pieces) - 1
        rows, cols = full.shape[0] // size, full.shape[1]
        half = cols // 2
        mine = ring_place(size, index)
        copies = []
        for k, piece in enumerate(pieces):
            step = (k + 1) // 2
            source = ring_device(size, mine + (step if k % 2 == 0 else -step))
            span = pl.ds(pl.multiple_of(source * rows, rows), rows)
            target = full.at[span]
            if step == size // 2:
                target = full.at[span, pl.ds(0, half) if k % 2 else pl.ds(half, cols - half)]
            copies.append(pltpu.make_async_copy(piece, target, arrived.at[k]))
    for copy in copies:
        copy.start()
    return copies


class RingGather:
    def __init__(self, shard):
        self.size = lax.axis_size("dp")
        self.fore, self.hind = shard, shard
        self.pieces = [shard]
        if not short_axis(self.size):
            self.pieces = [lax.all_gather(shard, "dp", axis=0, tiled=True)]

    def hop(self, order):
        if not short_axis(self.size):
            return
        ahead, back = ring_steps(self.size)
        if len(self.pieces) > 1:
            self.fore, self.hind = self.pieces[-2:] = order.tie((self.fore, self.hind))
        else:
            self.fore = self.hind = self.pieces[0] = order.tie(self.fore)
        fore, hind = self.fore, self.hind
        if len(self.pieces) == self.size - 1:
            half = fore.shape[1] // 2
            fore, hind = fore[:, :half], hind[:, half:]
        self.fore = lax.ppermute(fore, "dp", ahead)
        self.hind = lax.ppermute(hind, "dp", back)
        self.pieces += [self.fore, self.hind]


class RingReduce:
    def __init__(self, partial, order):
        self.size = lax.axis_size("dp")
        self.partial = partial
        if not short_axis(self.size):
            return
        self.mine = ring_place(self.size, lax.axis_index("dp"))
        self.left = self.size // 2
        half = partial.shape[1] // 2
        block = self.block(self.left)
        self.send(order.tie((block[:, :half], block[:, half:])))

    def block(self, offset):
        rows, cols = self.partial.shape[0] // self.size, self.partial.shape[1]
        device = ring_device(self.size, self.mine + offset)
        return lax.dynamic_slice(self.partial, (device * rows, 0), (rows, cols))

    def send(self, parts):
        ahead, back = ring_steps(self.size)
        self.fore = lax.ppermute(parts[0], "dp", ahead)
        self.hind = lax.ppermute(parts[1], "dp", back)
        self.left -= 1

    def hop(self, order):
        if not short_axis(self.size):
            return
        cols = self.partial.shape[1]
        self.fore, self.hind = order.tie((self.fore, self.hind))

        def total(offset, came, start):
            stop = start + came.shape[1]
            block = self.block(offset)
            sum_part = (block[:, start:stop].astype(F32) + came.astype(F32)).astype(BF16)
            return lax.dynamic_update_slice(block, sum_part, (0, start))

        fore = total(self.left, self.fore, 0)
        hind = total(-self.left, self.hind, cols - self.hind.shape[1])
        self.send((fore, hind))

    def wait(self, order):
        if short_axis(self.size):
            self.fore, self.hind = order.tie((self.fore, self.hind))

    def total(self, order):
        if not short_axis(self.size):
            return lax.psum_scatter(self.partial, "dp", scatter_dimension=0, tiled=True).astype(F32)
        while self.left > 0:
            self.hop(order)
        return self.block(0).astype(F32) + self.fore.astype(F32) + self.hind.astype(F32)


def tensor_swap(values, bit):
    size = lax.axis_size("tensor")
    return lax.ppermute(values, "tensor", [(i, i ^ bit) for i in range(size)])


def gather_rows(rows, order, during=lambda: None):
    rows = order.tie(rows)
    across = tensor_swap(rows, 2)
    beside = tensor_swap(rows, 1)
    during()
    return [rows, beside, across, tensor_swap(across, 1)]


def scatter_rows(blocks, during=lambda: None):
    own, beside, across, opposite = blocks
    across = across.astype(F32) + tensor_swap(opposite, 1).astype(F32)
    across = tensor_swap(across.astype(BF16), 2)
    beside = tensor_swap(beside, 1)
    during()
    return [own, beside, across]


def all_sum(values, during=lambda values: values):
    dp_size = lax.axis_size("dp")
    if dp_size & (dp_size - 1) or dp_size > 16:
        return lax.psum(values, "dp")
    bit = 1
    while bit < dp_size:
        values = during(values)
        values = values + lax.ppermute(values, "dp", [(i, i ^ bit) for i in range(dp_size)])
        bit *= 2
    return values


def tensor_sum(values):
    values = values + tensor_swap(values, 1)
    return values + tensor_swap(values, 2)


def dot_nt(left, right):
    return lax.dot_general(left, right, (((1,), (1,)), ((), ())), preferred_element_type=F32)


def dot_nn(left, right):
    return lax.dot_general(left, right, (((1,), (0,)), ((), ())), preferred_element_type=F32)


def column_pair(values, start, stop):
    piece = values[:, start : min(start + LANES, stop)]
    if piece.shape[1] < LANES:
        piece = jnp.concatenate([piece, jnp.zeros((piece.shape[0], HEAD), piece.dtype)], axis=1)
    return piece


def low_half(rows):
    return lax.broadcasted_iota(jnp.int32, (rows, LANES), 1) < HEAD


def head_sums(values):
    first = low_half(values.shape[0])
    left = jnp.sum(jnp.where(first, values, 0.0), axis=-1, keepdims=True)
    right = jnp.sum(jnp.where(first, 0.0, values), axis=-1, keepdims=True)
    return jnp.where(first, left, right)


def head_norm(values):
    factor = lax.rsqrt(head_sums(values * values) + EPSILON)
    return values * factor, factor


def side_of(values, side):
    first = low_half(values.shape[0])
    zero = jnp.zeros_like(values)
    return jnp.where(first, values, zero) if side == 0 else jnp.where(first, zero, values)


def kernel_call(body, out_shape, order, arrays, room, scratch=()):
    whole = pl.BlockSpec(memory_space=pltpu.VMEM)
    small = pl.BlockSpec(memory_space=pltpu.SMEM)
    count = len(arrays) + 1

    def with_token(*refs):
        body(*refs[:count], *refs[count + 1 :])
        for k in range(3):
            refs[count][k] = refs[0][k]

    order.token, *out = pl.pallas_call(
        with_token,
        out_shape=[shaped(jnp.int32, 3), *out_shape],
        in_specs=[small] + [whole] * len(arrays),
        out_specs=[small] + [whole] * len(out_shape),
        scratch_shapes=list(scratch),
        cost_estimate=pl.CostEstimate(flops=1, transcendentals=0, bytes_accessed=1),
        compiler_params=pltpu.CompilerParams(vmem_limit_bytes=room * MEGA),
        name=(body.func if isinstance(body, functools.partial) else body).__name__,
    )(order.token, *arrays)
    return out


def shaped(dtype, *shape):
    return jax.ShapeDtypeStruct(shape, dtype)


def rank_rows(rank, slot_block, block):
    return pl.ds(pl.multiple_of((rank ^ slot_block) * block, block), block)


def attend_body(heads, count, scalars, *refs):
    pieces, (x0, x1, x2, x3, gain_ref) = refs[:count], refs[count : count + 5]
    (w_ref, raw_ref, low_ref, totals_ref, q_ref, k_ref, v_ref) = refs[count + 5 : count + 12]
    parts_out = refs[count + 12 : count + 16]
    arrived = refs[count + 16]
    rank, length = scalars[0], scalars[1]
    block = x0.shape[0]
    slots = 4 * block
    width = heads * HEAD
    pairs = (heads + 1) // 2
    for copy in place_pieces(scalars[2], pieces, w_ref, arrived):
        copy.wait()
    for k, x_ref in enumerate((x0, x1, x2, x3)):
        at = pl.ds(pl.multiple_of((rank ^ k) * block, block), block)
        raw = dot_nn(x_ref[...], w_ref[:, : 3 * width + HEAD])
        for j in range(pairs):
            gain = gain_ref[:, j * LANES : (j + 1) * LANES]
            q_raw = column_pair(raw, j * LANES, width)
            k_raw = column_pair(raw, width + j * LANES, 2 * width)
            raw_ref[j, at] = q_raw
            raw_ref[pairs + j, at] = k_raw
            q_ref[j, at] = (head_norm(q_raw)[0] * gain).astype(BF16)
            k_ref[j, at] = (head_norm(k_raw)[0] * gain).astype(BF16)
            v_ref[j, at] = column_pair(raw, 2 * width + j * LANES, 3 * width).astype(BF16)
    scale = jnp.asarray(math.sqrt(HEAD), BF16)
    here = lax.broadcasted_iota(jnp.int32, (slots, LANES), 0) < length
    counted = jnp.where(here, 1.0, 0.0).astype(BF16)
    causal = lax.broadcasted_iota(jnp.int32, (block, block), 1) <= lax.broadcasted_iota(
        jnp.int32, (block, block), 0
    )
    first_rows = low_half(slots)
    first = low_half(block)
    for j in range(pairs):
        value = jnp.where(here, v_ref[j], jnp.zeros((), BF16))
        with_count = [jnp.where(first_rows, value, counted), jnp.where(first_rows, counted, value)]
        for a in range(4):
            keys = (a + 1) * block
            parts, logs = [], []
            for side in range(2):
                if 2 * j + side >= heads:
                    parts.append(jnp.zeros((block, LANES), F32))
                    logs.append(jnp.zeros((block, LANES), F32))
                    continue
                query = side_of(q_ref[j, a * block : keys], side) * scale
                weight = jnp.exp(dot_nt(query, k_ref[j, :keys]))
                last = jnp.where(causal, weight[:, a * block :], 0.0)
                weight = jnp.concatenate([weight[:, : a * block], last], axis=1) if a else last
                summed = dot_nn(weight.astype(BF16), with_count[side][:keys])
                total = pltpu.roll(summed, HEAD, 1)
                parts.append(summed / total)
                logs.append(jnp.log(total))
            out = jnp.where(first, parts[0], parts[1])
            log_total = jnp.where(first, logs[0], logs[1])
            totals_ref[j, :, a * block : keys] = log_total.T
            stop = min((j + 1) * LANES, width)
            low_ref[rank_rows(rank, a, block), j * LANES : stop] = out[
                :, : stop - j * LANES
            ].astype(BF16)
    w_out = w_ref[:, 3 * width : 4 * width]
    for k, part_ref in enumerate(parts_out):
        part_ref[...] = dot_nt(low_ref[k * block : (k + 1) * block], w_out).astype(BF16)


def attend(order, pieces, blocks, gain, heads):
    block, model = blocks[0].shape
    slots = 4 * block
    pairs = (heads + 1) // 2
    low = shaped(BF16, pairs, slots, LANES)
    out_shape = [
        shaped(BF16, model, 4 * heads * HEAD),
        shaped(F32, 2 * pairs, slots, LANES),
        shaped(BF16, slots, heads * HEAD),
        shaped(F32, pairs, LANES, slots),
        low,
        low,
        low,
    ] + [shaped(BF16, block, model)] * 4
    out = kernel_call(
        functools.partial(attend_body, heads, len(pieces)),
        out_shape,
        order,
        [*pieces, *blocks, gain],
        10,
        [pltpu.SemaphoreType.DMA((len(pieces),))],
    )
    return out[:7], out[7:]


def attend_back_body(
    heads, scalars, g0, g1, g2, g3, w_ref, gain_ref, raw_ref, low_ref, totals_ref, q_ref, k_ref,
    v_ref, grad_ref, ggain_ref, p0, p1, p2, p3, ga_ref, dk_ref, dv_ref, gq_ref, gk_ref, gv_ref,
):
    rank = scalars[0]
    block = g0.shape[0]
    slots = 4 * block
    width = heads * HEAD
    pairs = (heads + 1) // 2
    w_out = w_ref[:, 3 * width : 4 * width]
    for k, g_ref in enumerate((g0, g1, g2, g3)):
        ga_ref[k * block : (k + 1) * block] = dot_nn(g_ref[...], w_out).astype(BF16)
    scale = jnp.asarray(math.sqrt(HEAD), BF16)
    causal = lax.broadcasted_iota(jnp.int32, (block, block), 0) <= lax.broadcasted_iota(
        jnp.int32, (block, block), 1
    )
    top = lax.broadcasted_iota(jnp.int32, (LANES, slots), 0) < HEAD
    for j in range(pairs):
        stop = min((j + 1) * LANES, width)
        key_turned = k_ref[j].T
        key_sides = [
            jnp.where(top, key_turned, jnp.zeros((), BF16)),
            jnp.where(top, jnp.zeros((), BF16), key_turned),
        ]
        gain = gain_ref[:, j * LANES : (j + 1) * LANES]
        dk_ref[...] = jnp.zeros_like(dk_ref)
        dv_ref[...] = jnp.zeros_like(dv_ref)
        gain_sum = jnp.zeros((1, LANES), F32)
        for a in range(4):
            rows = rank_rows(rank, a, block)
            keys = (a + 1) * block
            grad = column_pair(ga_ref[rows, j * LANES : stop], 0, LANES)
            out = column_pair(low_ref[rows, j * LANES : stop], 0, LANES)
            delta = (grad.astype(F32) * out.astype(F32)).T
            dq_turned = jnp.zeros((LANES, block), F32)
            for side in range(2):
                if 2 * j + side >= heads:
                    continue
                query = side_of(q_ref[j, a * block : keys], side) * scale
                grad_side = side_of(grad, side)
                log_row = totals_ref[j, side * HEAD : side * HEAD + 1, a * block : keys]
                delta_row = jnp.sum(delta[side * HEAD : (side + 1) * HEAD], axis=0, keepdims=True)
                weight = jnp.exp(dot_nt(k_ref[j, :keys], query) - log_row)
                last = jnp.where(causal, weight[a * block :], 0.0)
                weight = jnp.concatenate([weight[: a * block], last], axis=0) if a else last
                grad_weight = dot_nt(v_ref[j, :keys], grad_side)
                grad_score = (weight * (grad_weight - delta_row)).astype(BF16)
                dv_ref[:keys] += dot_nn(weight.astype(BF16), grad_side)
                dk_ref[:keys] += dot_nn(grad_score, query)
                dq_turned += dot_nn(key_sides[side][:, :keys], grad_score)
            dq = dq_turned.T * math.sqrt(HEAD)
            q_unit, factor = head_norm(raw_ref[j, a * block : keys])
            gain_sum += jnp.sum(dq * q_unit, axis=0, keepdims=True)
            scaled = dq * gain
            gq = factor * (scaled - q_unit * head_sums(scaled * q_unit))
            gq_ref[rows, j * LANES : stop] = gq[:, : stop - j * LANES].astype(BF16)
        for a in range(4):
            rows = rank_rows(rank, a, block)
            at = slice(a * block, (a + 1) * block)
            dk = dk_ref[at]
            k_unit, factor = head_norm(raw_ref[pairs + j, at])
            gain_sum += jnp.sum(dk * k_unit, axis=0, keepdims=True)
            scaled = dk * gain
            gk = factor * (scaled - k_unit * head_sums(scaled * k_unit))
            gk_ref[rows, j * LANES : stop] = gk[:, : stop - j * LANES].astype(BF16)
            gv_ref[rows, j * LANES : stop] = dv_ref[at][:, : stop - j * LANES].astype(BF16)
        ggain_ref[:, j * LANES : (j + 1) * LANES] = gain_sum
    w_project = w_ref[:, : 3 * width]
    for k, part_ref in enumerate((p0, p1, p2, p3)):
        at = slice(k * block, (k + 1) * block)
        grad = jnp.concatenate([gq_ref[at], gk_ref[at], gv_ref[at]], axis=1)
        grad_ref[at] = grad
        part_ref[...] = dot_nt(grad, w_project).astype(BF16)


def attend_back(order, grads, w_attn, gain, kept, heads):
    block, model = grads[0].shape
    slots = 4 * block
    width = heads * HEAD
    pairs = (heads + 1) // 2
    out_shape = [shaped(BF16, slots, 3 * width), shaped(F32, 1, pairs * LANES)] + [
        shaped(BF16, block, model)
    ] * 4
    return kernel_call(
        functools.partial(attend_back_body, heads),
        out_shape,
        order,
        [*grads, w_attn, gain, *kept],
        20,
        [pltpu.VMEM((slots, width), BF16)]
        + [pltpu.VMEM((slots, LANES), F32)] * 2
        + [pltpu.VMEM((slots, width), BF16)] * 3,
    )


def row_norm(values):
    factor = lax.rsqrt(jnp.sum(values * values, axis=-1, keepdims=True) + EPSILON)
    return values * factor, factor


def row_norm_back(grad, unit, factor):
    return factor * (grad - unit * jnp.sum(grad * unit, axis=-1, keepdims=True))


def branch_sum(parts):
    own, beside, across = (part[...].astype(F32) for part in parts)
    return own + beside + across


def first_norm_body(scalars, own, beside, across, hidden_ref, alpha_ref, unit_ref, out_ref, low_ref, factors_ref):
    unit, unit_factor = row_norm(branch_sum((own, beside, across)))
    hidden = hidden_ref[...]
    out, factor = row_norm(hidden + alpha_ref[...] * (unit - hidden))
    unit_ref[...] = unit
    out_ref[...] = out
    low_ref[...] = out.astype(BF16)
    lane = lax.broadcasted_iota(jnp.int32, factors_ref.shape, 1)
    factors_ref[...] = jnp.where(lane == 0, unit_factor, factor)


def first_norm(order, parts, hidden, alpha):
    rows, model = hidden.shape
    full = shaped(F32, rows, model)
    return kernel_call(
        first_norm_body,
        [full, full, shaped(BF16, rows, model), shaped(F32, rows, LANES)],
        order,
        [*parts, hidden, alpha.reshape(1, model)],
        10,
    )


def loss_body(
    total_slots, scalars, own, beside, across, first_ref, teacher_ref, alpha_ref, tokens_ref,
    out_ref, grad_ref, rest_ref, sums_ref,
):
    rank, length = scalars[0], scalars[1]
    unit, unit_factor = row_norm(branch_sum((own, beside, across)))
    first, alpha = first_ref[...], alpha_ref[...]
    out, factor = row_norm(first + alpha * (unit - first))
    out_ref[...] = out
    rows = out.shape[0]
    slot = rank * rows + lax.broadcasted_iota(jnp.int32, (rows, 1), 0)
    difference = jnp.where(slot < length, out - teacher_ref[...], 0.0)
    mixed = row_norm_back(2.0 * total_slots / tokens_ref[...] * difference, out, factor)
    rest_ref[...] = mixed * (1.0 - alpha)
    grad_ref[...] = row_norm_back(mixed * alpha, unit, unit_factor).astype(BF16)
    sums_ref[0:1] = jnp.sum(difference * difference, axis=0, keepdims=True)
    sums_ref[1:2] = jnp.sum(mixed * (unit - first), axis=0, keepdims=True)


def loss_and_grad(order, parts, first, teacher, alpha, tokens, total_slots):
    rows, model = first.shape
    full = shaped(F32, rows, model)
    return kernel_call(
        functools.partial(loss_body, total_slots),
        [full, shaped(BF16, rows, model), full, shaped(F32, 2, model)],
        order,
        [*parts, first, teacher, alpha.reshape(1, model), tokens.reshape(1, 1)],
        10,
    )


def first_back_body(
    scalars, own, beside, across, rest_ref, first_ref, unit_ref, hidden_ref, alpha_ref, factors_ref,
    grad_ref, out_ref, sums_ref,
):
    grad = rest_ref[...] + branch_sum((own, beside, across))
    alpha, unit = alpha_ref[...], unit_ref[...]
    mixed = row_norm_back(grad, first_ref[...], factors_ref[:, 1:2])
    sums_ref[...] = jnp.sum(mixed * (unit - hidden_ref[...]), axis=0, keepdims=True)
    out_ref[...] = mixed * (1.0 - alpha)
    grad_ref[...] = row_norm_back(mixed * alpha, unit, factors_ref[:, 0:1]).astype(BF16)


def first_back(order, parts, rest, first, unit, hidden, alpha, factors):
    rows, model = first.shape
    return kernel_call(
        first_back_body,
        [shaped(BF16, rows, model), shaped(F32, rows, model), shaped(F32, 1, model)],
        order,
        [*parts, rest, first, unit, hidden, alpha.reshape(1, model), factors],
        10,
    )


def feed_body(count, scalars, *refs):
    pieces, x_refs = refs[:count], refs[count : count + 4]
    gains_ref = refs[count + 4]
    w_ref, up_ref, gate_ref, hidden_ref = refs[count + 5 : count + 9]
    parts_out, arrived = refs[count + 9 : count + 13], refs[count + 13]
    ff = gains_ref.shape[1]
    block = x_refs[0].shape[0]
    for copy in place_pieces(scalars[2], pieces, w_ref, arrived):
        copy.wait()
    for k in (3, 2, 1, 0):
        at = slice(k * block, (k + 1) * block)
        x = x_refs[k][...]
        up = dot_nn(x, w_ref[:, :ff])
        gate = dot_nn(x, w_ref[:, ff : 2 * ff])
        scaled = gate * gains_ref[1:2]
        hidden = (up * gains_ref[0:1] * (scaled * jax.nn.sigmoid(scaled))).astype(BF16)
        up_ref[at] = up.astype(BF16)
        gate_ref[at] = gate.astype(BF16)
        hidden_ref[at] = hidden
        parts_out[k][...] = dot_nt(hidden, w_ref[:, 2 * ff :]).astype(BF16)


def feed(order, pieces, blocks, gains):
    block, model = blocks[0].shape
    ff = gains.shape[1]
    rows = shaped(BF16, 4 * block, ff)
    out = kernel_call(
        functools.partial(feed_body, len(pieces)),
        [shaped(BF16, model, 3 * ff), rows, rows, rows] + [shaped(BF16, block, model)] * 4,
        order,
        [*pieces, *blocks, gains],
        16,
        [pltpu.SemaphoreType.DMA((len(pieces),))],
    )
    return out[:4], out[4:]


def feed_back_body(scalars, g0, g1, g2, g3, w_ref, up_ref, gate_ref, gains_ref, grad_ref, sums_ref, p0, p1, p2, p3):
    ff = gains_ref.shape[1]
    block = g0.shape[0]
    grads, parts = (g0, g1, g2, g3), (p0, p1, p2, p3)
    up_gain, gate_gain = gains_ref[0:1], gains_ref[1:2]
    sums_ref[...] = jnp.zeros_like(sums_ref)
    for k in (3, 2, 1, 0):
        at = slice(k * block, (k + 1) * block)
        grad = dot_nn(grads[k][...], w_ref[:, 2 * ff :])
        up, gate = up_ref[at].astype(F32), gate_ref[at].astype(F32)
        scaled = gate * gate_gain
        chance = jax.nn.sigmoid(scaled)
        by_up = grad * (scaled * chance)
        by_gate = grad * (up * up_gain) * chance * (1.0 + scaled * (1.0 - chance))
        sums_ref[0:1] += jnp.sum(by_up * up, axis=0, keepdims=True)
        sums_ref[1:2] += jnp.sum(by_gate * gate, axis=0, keepdims=True)
        grad_ref[at, :ff] = (by_up * up_gain).astype(BF16)
        grad_ref[at, ff:] = (by_gate * gate_gain).astype(BF16)
        parts[k][...] = dot_nt(grad_ref[at], w_ref[:, : 2 * ff]).astype(BF16)


def feed_back(order, grads, w_feed, up, gate, gains):
    block, model = grads[0].shape
    ff = gains.shape[1]
    return kernel_call(
        feed_back_body,
        [shaped(BF16, 4 * block, 2 * ff), shaped(F32, 2, ff)] + [shaped(BF16, block, model)] * 4,
        order,
        [*grads, w_feed, up, gate, gains],
        18,
    )


def turned_dot(left, right):
    return jnp.einsum("rd,rf->df", left, right, preferred_element_type=F32).astype(BF16)


def on_device(
    hidden_in,
    lengths,
    teacher,
    w_query,
    w_key,
    w_value,
    w_attn_out,
    w_up,
    w_gate,
    w_down,
    s_qk,
    alpha_attn,
    alpha_mlp,
    s_up,
    s_gate,
):
    tensor_rank = lax.axis_index("tensor")
    seq_count, local_slots, model_width = hidden_in.shape
    slot_count = local_slots * lax.axis_size("tensor")
    heads_width = w_query.shape[1]
    head_count = heads_width // HEAD
    ff_local = w_up.shape[1]
    gate_root = math.sqrt(model_width)
    total_slots = slot_count * seq_count * lax.axis_size("dp")
    hidden = hidden_in.reshape(local_slots, model_width)
    teacher = teacher.reshape(local_slots, model_width)
    length = lengths[0]
    order = Order(
        jnp.stack([tensor_rank.astype(jnp.int32), length, lax.axis_index("dp").astype(jnp.int32)])
    )
    own_part = lambda vector, width: lax.dynamic_slice_in_dim(vector, tensor_rank * width, width)
    qk_gain = jnp.pad(own_part(s_qk, heads_width), (0, heads_width % LANES)).reshape(1, -1)
    gains = jnp.stack([own_part(s_up, ff_local), own_part(s_gate, ff_local) * gate_root])

    attn_ring = RingGather(jnp.concatenate([w_query, w_key, w_value, w_attn_out.T], axis=1))
    feed_ring = RingGather(jnp.concatenate([w_up, w_gate, w_down.T], axis=1))
    attn_ring.hop(order)
    attn_ring.hop(order)
    qk_gain, gains = order.tie((qk_gain, gains))
    stream = gather_rows(hidden.astype(BF16), order)
    attn_ring.hop(order)
    attn_ring.hop(order)
    if short_axis(attn_ring.size):
        attn_ring.pieces[-2:] = order.tie(attn_ring.pieces[-2:])
    feed_ring.hop(order)
    kept, parts = attend(order, attn_ring.pieces, stream, qk_gain, head_count)
    w_attn, kept = kept[0], kept[1:]
    parts = scatter_rows(parts, lambda: feed_ring.hop(order))
    attn_unit, first_out, first_low, factors = first_norm(order, parts, hidden, alpha_attn)
    mlp_in = gather_rows(first_low, order, lambda: feed_ring.hop(order))
    feed_ring.hop(order)
    token_count = all_sum(lengths.astype(F32))[0]
    (w_feed, up_raw, gate_raw, hidden_low), parts = feed(order, feed_ring.pieces, mlp_in, gains)
    parts = scatter_rows(parts)
    output, grad_mlp_sum, grad_first, loss_sums = loss_and_grad(
        order, parts, first_out, teacher, alpha_mlp, token_count, total_slots
    )

    grad_mlp = gather_rows(grad_mlp_sum, order)
    grad_rows, hidden_low = order.tie((jnp.concatenate(grad_mlp, axis=0), hidden_low))
    grad_low = order.tie(turned_dot(grad_rows, hidden_low))
    low_reduce = RingReduce(grad_low, order)
    grad_pair, ff_sums, *parts = feed_back(order, grad_mlp, w_feed, up_raw, gate_raw, gains)
    low_reduce.hop(order)
    mlp_rows = jnp.concatenate(mlp_in, axis=0)
    mlp_rows, grad_pair = order.tie((mlp_rows, grad_pair))
    grad_w_up = order.tie(turned_dot(mlp_rows, grad_pair[:, :ff_local]))
    low_reduce.hop(order)
    mlp_rows, grad_pair = order.tie((mlp_rows, grad_pair))
    grad_w_gate = order.tie(turned_dot(mlp_rows, grad_pair[:, ff_local:]))
    low_reduce.hop(order)
    parts = scatter_rows(parts)
    grad_attn_sum, grad_input, attn_sums = first_back(
        order, parts, grad_first, first_out, attn_unit, hidden, alpha_attn, factors
    )
    low_reduce.wait(order)
    pair_reduce = RingReduce(jnp.concatenate([grad_w_up, grad_w_gate], axis=1), order)
    grad_attn = gather_rows(grad_attn_sum, order, lambda: pair_reduce.hop(order))
    grad_w_down = low_reduce.total(order).T
    grad_project, gain_sums, *parts = attend_back(
        order, grad_attn, w_attn, qk_gain, kept, head_count
    )
    pair_reduce.hop(order)
    parts = scatter_rows(parts)
    stream_rows = jnp.concatenate(stream, axis=0)
    attn_rows = jnp.concatenate(grad_attn, axis=0)
    grad_w_attn = order.tie(
        jnp.concatenate(
            [turned_dot(stream_rows, grad_project), turned_dot(attn_rows, kept[1])], axis=1
        )
    )
    pair_reduce.hop(order)
    pair_reduce.wait(order)
    attn_reduce = RingReduce(grad_w_attn, order)
    grad_w_pair = pair_reduce.total(order)
    grad_input = grad_input + sum(part.astype(F32) for part in parts)

    def placed(values):
        width = values.shape[0]
        return lax.dynamic_update_slice_in_dim(
            jnp.zeros((width * lax.axis_size("tensor"),), F32), values, tensor_rank * width, 0
        )

    vectors = jnp.concatenate(
        [
            jnp.sum(loss_sums[0]).reshape(1),
            attn_sums[0],
            loss_sums[1],
            placed(gain_sums[0, :heads_width]),
            placed(ff_sums[0]),
            placed(ff_sums[1] * gate_root),
        ]
    )
    def attn_step(values):
        attn_reduce.hop(order)
        return order.tie(values)

    vectors = all_sum(tensor_sum(vectors), attn_step)
    grad_w_attn = attn_reduce.total(order)
    loss = vectors[0] / token_count
    cuts = [1 + model_width * k for k in range(4)] + [1 + 3 * model_width + s_up.shape[0]]
    return (
        loss,
        output[None],
        grad_input[None],
        grad_w_attn[:, :heads_width],
        grad_w_attn[:, heads_width : 2 * heads_width],
        grad_w_attn[:, 2 * heads_width : 3 * heads_width],
        grad_w_attn[:, 3 * heads_width :].T,
        grad_w_pair[:, :ff_local],
        grad_w_pair[:, ff_local:],
        grad_w_down,
        vectors[cuts[2] : cuts[3]],
        vectors[cuts[0] : cuts[1]],
        vectors[cuts[1] : cuts[2]],
        vectors[cuts[3] : cuts[4]],
        vectors[cuts[4] :],
    )


def solution(mesh):
    in_specs = (
        P("dp", "tensor", None),
        P("dp"),
        P("dp", "tensor", None),
        P("dp", "tensor"),
        P("dp", "tensor"),
        P("dp", "tensor"),
        P("tensor", "dp"),
        P("dp", "tensor"),
        P("dp", "tensor"),
        P("tensor", "dp"),
        P(),
        P(),
        P(),
        P(),
        P(),
    )
    out_specs = (
        P(),
        P("dp", "tensor", None),
        P("dp", "tensor", None),
        P("dp", "tensor"),
        P("dp", "tensor"),
        P("dp", "tensor"),
        P("tensor", "dp"),
        P("dp", "tensor"),
        P("dp", "tensor"),
        P("tensor", "dp"),
        P(),
        P(),
        P(),
        P(),
        P(),
    )
    return jax.shard_map(
        on_device, mesh=mesh, in_specs=in_specs, out_specs=out_specs, check_vma=False
    )
```

```python
import functools
import math

import jax
import jax.numpy as jnp
from jax import lax
from jax.experimental import pallas as pl
from jax.experimental.pallas import tpu as pltpu
from jax.sharding import PartitionSpec as P

HEAD = 64
LANES = 2 * HEAD


EPSILON = 1e-06
BF16 = jnp.bfloat16
F32 = jnp.float32
MEGA = 2**20


def short_axis(size):
    return size % 2 == 0 and size <= 16


class Order:
    def __init__(self, token):
        self.token = token

    def tie(self, values):
        values, self.token = lax.optimization_barrier((values, self.token))
        return values


def ring_place(size, index):
    return index // 2 + (index % 2) * (size - 1 - 2 * (index // 2))


def ring_device(size, place):
    place = (place + 2 * size) % size
    later = (2 * place) // size
    return 2 * place + later * (2 * size - 1 - 4 * place)


def ring_steps(size):
    order = [ring_device(size, place) for place in range(size)]
    ahead = [(order[i], order[(i + 1) % size]) for i in range(size)]
    return ahead, [(b, a) for a, b in ahead]


def place_pieces(index, pieces, full, arrived):
    if len(pieces) == 1:
        copies = [pltpu.make_async_copy(pieces[0], full, arrived.at[0])]
    else:
        size = len(pieces) - 1
        rows, cols = full.shape[0] // size, full.shape[1]
        half = cols // 2
        mine = ring_place(size, index)
        copies = []
        for k, piece in enumerate(pieces):
            step = (k + 1) // 2
            source = ring_device(size, mine + (step if k % 2 == 0 else -step))
            span = pl.ds(pl.multiple_of(source * rows, rows), rows)
            target = full.at[span]
            if step == size // 2:
                target = full.at[span, pl.ds(0, half) if k % 2 else pl.ds(half, cols - half)]
            copies.append(pltpu.make_async_copy(piece, target, arrived.at[k]))
    for copy in copies:
        copy.start()
    return copies


class RingGather:
    def __init__(self, shard):
        self.size = lax.axis_size("dp")
        self.fore, self.hind = shard, shard
        self.pieces = [shard]
        if not short_axis(self.size):
            self.pieces = [lax.all_gather(shard, "dp", axis=0, tiled=True)]

    def hop(self, order):
        if not short_axis(self.size):
            return
        ahead, back = ring_steps(self.size)
        if len(self.pieces) > 1:
            self.fore, self.hind = self.pieces[-2:] = order.tie((self.fore, self.hind))
        else:
            self.fore = self.hind = self.pieces[0] = order.tie(self.fore)
        fore, hind = self.fore, self.hind
        if len(self.pieces) == self.size - 1:
            half = fore.shape[1] // 2
            fore, hind = fore[:, :half], hind[:, half:]
        self.fore = lax.ppermute(fore, "dp", ahead)
        self.hind = lax.ppermute(hind, "dp", back)
        self.pieces += [self.fore, self.hind]


class RingReduce:
    def __init__(self, partial, order):
        self.size = lax.axis_size("dp")
        self.partial = partial
        if not short_axis(self.size):
            return
        self.mine = ring_place(self.size, lax.axis_index("dp"))
        self.left = self.size // 2
        half = partial.shape[1] // 2
        block = self.block(self.left)
        self.send(order.tie((block[:, :half], block[:, half:])))

    def block(self, offset):
        rows, cols = self.partial.shape[0] // self.size, self.partial.shape[1]
        device = ring_device(self.size, self.mine + offset)
        return lax.dynamic_slice(self.partial, (device * rows, 0), (rows, cols))

    def send(self, parts):
        ahead, back = ring_steps(self.size)
        self.fore = lax.ppermute(parts[0], "dp", ahead)
        self.hind = lax.ppermute(parts[1], "dp", back)
        self.left -= 1

    def hop(self, order):
        if not short_axis(self.size):
            return
        cols = self.partial.shape[1]
        self.fore, self.hind = order.tie((self.fore, self.hind))

        def total(offset, came, start):
            stop = start + came.shape[1]
            block = self.block(offset)
            sum_part = (block[:, start:stop].astype(F32) + came.astype(F32)).astype(BF16)
            return lax.dynamic_update_slice(block, sum_part, (0, start))

        fore = total(self.left, self.fore, 0)
        hind = total(-self.left, self.hind, cols - self.hind.shape[1])
        self.send(order.tie((fore, hind)))

    def wait(self, order):
        if short_axis(self.size):
            self.fore, self.hind = order.tie((self.fore, self.hind))

    def total(self, order, last=False):
        if not short_axis(self.size):
            return lax.psum_scatter(self.partial, "dp", scatter_dimension=0, tiled=True).astype(F32)
        while self.left > 0:
            self.hop(order)
        if last:
            pieces = order.tie((self.block(0), self.fore, self.hind))
            return kernel_call(last_body, [shaped(F32, *pieces[0].shape)], order, pieces, 8)[0]
        return self.block(0).astype(F32) + self.fore.astype(F32) + self.hind.astype(F32)


def tensor_swap(values, bit):
    size = lax.axis_size("tensor")
    return lax.ppermute(values, "tensor", [(i, i ^ bit) for i in range(size)])


def gather_rows(rows, order, during=lambda: None):
    rows = order.tie(rows)
    across = tensor_swap(rows, 2)
    beside = tensor_swap(rows, 1)
    during()
    return [rows, beside, across, tensor_swap(across, 1)]


def scatter_rows(blocks, during=lambda: None):
    own, beside, across, opposite = blocks
    across = across.astype(F32) + tensor_swap(opposite, 1).astype(F32)
    across = tensor_swap(across.astype(BF16), 2)
    beside = tensor_swap(beside, 1)
    during()
    return [own, beside, across]


def all_sum(values, during=lambda values: values):
    dp_size = lax.axis_size("dp")
    if dp_size & (dp_size - 1) or dp_size > 16:
        return lax.psum(values, "dp")
    bit = 1
    while bit < dp_size:
        values = during(values)
        values = values + lax.ppermute(values, "dp", [(i, i ^ bit) for i in range(dp_size)])
        bit *= 2
    return values


def tensor_sum(values):
    values = values + tensor_swap(values, 1)
    return values + tensor_swap(values, 2)


def dot_nt(left, right):
    return lax.dot_general(left, right, (((1,), (1,)), ((), ())), preferred_element_type=F32)


def dot_nn(left, right):
    return lax.dot_general(left, right, (((1,), (0,)), ((), ())), preferred_element_type=F32)


def column_pair(values, start, stop):
    piece = values[:, start : min(start + LANES, stop)]
    if piece.shape[1] < LANES:
        piece = jnp.concatenate([piece, jnp.zeros((piece.shape[0], HEAD), piece.dtype)], axis=1)
    return piece


def low_half(rows):
    return lax.broadcasted_iota(jnp.int32, (rows, LANES), 1) < HEAD


def head_sums(values):
    first = low_half(values.shape[0])
    left = jnp.sum(jnp.where(first, values, 0.0), axis=-1, keepdims=True)
    right = jnp.sum(jnp.where(first, 0.0, values), axis=-1, keepdims=True)
    return jnp.where(first, left, right)


def head_norm(values):
    factor = lax.rsqrt(head_sums(values * values) + EPSILON)
    return values * factor, factor


def side_of(values, side):
    first = low_half(values.shape[0])
    zero = jnp.zeros_like(values)
    return jnp.where(first, values, zero) if side == 0 else jnp.where(first, zero, values)


def kernel_call(body, out_shape, order, arrays, room, scratch=()):
    whole = pl.BlockSpec(memory_space=pltpu.VMEM)
    small = pl.BlockSpec(memory_space=pltpu.SMEM)
    count = len(arrays) + 1

    def with_token(*refs):
        body(*refs[:count], *refs[count + 1 :])
        for k in range(3):
            refs[count][k] = refs[0][k]

    order.token, *out = pl.pallas_call(
        with_token,
        out_shape=[shaped(jnp.int32, 3), *out_shape],
        in_specs=[small] + [whole] * len(arrays),
        out_specs=[small] + [whole] * len(out_shape),
        scratch_shapes=list(scratch),
        cost_estimate=pl.CostEstimate(flops=1, transcendentals=0, bytes_accessed=1),
        compiler_params=pltpu.CompilerParams(vmem_limit_bytes=room * MEGA),
        name=(body.func if isinstance(body, functools.partial) else body).__name__,
    )(order.token, *arrays)
    return out


def shaped(dtype, *shape):
    return jax.ShapeDtypeStruct(shape, dtype)


def rank_rows(rank, slot_block, block):
    return pl.ds(pl.multiple_of((rank ^ slot_block) * block, block), block)


def attend_body(heads, count, scalars, *refs):
    pieces, (x0, x1, x2, x3, gain_ref) = refs[:count], refs[count : count + 5]
    (w_ref, raw_ref, low_ref, totals_ref, q_ref, k_ref, v_ref) = refs[count + 5 : count + 12]
    parts_out = refs[count + 12 : count + 16]
    arrived = refs[count + 16]
    rank, length = scalars[0], scalars[1]
    block = x0.shape[0]
    slots = 4 * block
    width = heads * HEAD
    pairs = (heads + 1) // 2
    for copy in place_pieces(scalars[2], pieces, w_ref, arrived):
        copy.wait()
    for k, x_ref in enumerate((x0, x1, x2, x3)):
        at = pl.ds(pl.multiple_of((rank ^ k) * block, block), block)
        raw = dot_nn(x_ref[...], w_ref[:, : 3 * width + HEAD])
        for j in range(pairs):
            gain = gain_ref[:, j * LANES : (j + 1) * LANES]
            q_raw = column_pair(raw, j * LANES, width)
            k_raw = column_pair(raw, width + j * LANES, 2 * width)
            raw_ref[j, at] = q_raw
            raw_ref[pairs + j, at] = k_raw
            q_ref[j, at] = (head_norm(q_raw)[0] * gain).astype(BF16)
            k_ref[j, at] = (head_norm(k_raw)[0] * gain).astype(BF16)
            v_ref[j, at] = column_pair(raw, 2 * width + j * LANES, 3 * width).astype(BF16)
    scale = jnp.asarray(math.sqrt(HEAD), BF16)
    here = lax.broadcasted_iota(jnp.int32, (slots, LANES), 0) < length
    counted = jnp.where(here, 1.0, 0.0).astype(BF16)
    causal = lax.broadcasted_iota(jnp.int32, (block, block), 1) <= lax.broadcasted_iota(
        jnp.int32, (block, block), 0
    )
    first_rows = low_half(slots)
    first = low_half(block)
    for j in range(pairs):
        value = jnp.where(here, v_ref[j], jnp.zeros((), BF16))
        with_count = [jnp.where(first_rows, value, counted), jnp.where(first_rows, counted, value)]
        for a in range(4):
            keys = (a + 1) * block
            parts, logs = [], []
            for side in range(2):
                if 2 * j + side >= heads:
                    parts.append(jnp.zeros((block, LANES), F32))
                    logs.append(jnp.zeros((block, LANES), F32))
                    continue
                query = side_of(q_ref[j, a * block : keys], side) * scale
                weight = jnp.exp(dot_nt(query, k_ref[j, :keys]))
                last = jnp.where(causal, weight[:, a * block :], 0.0)
                weight = jnp.concatenate([weight[:, : a * block], last], axis=1) if a else last
                summed = dot_nn(weight.astype(BF16), with_count[side][:keys])
                total = pltpu.roll(summed, HEAD, 1)
                parts.append(summed / total)
                logs.append(jnp.log(total))
            out = jnp.where(first, parts[0], parts[1])
            log_total = jnp.where(first, logs[0], logs[1])
            totals_ref[j, :, a * block : keys] = log_total.T
            stop = min((j + 1) * LANES, width)
            low_ref[rank_rows(rank, a, block), j * LANES : stop] = out[
                :, : stop - j * LANES
            ].astype(BF16)
    w_out = w_ref[:, 3 * width : 4 * width]
    for k, part_ref in enumerate(parts_out):
        part_ref[...] = dot_nt(low_ref[k * block : (k + 1) * block], w_out).astype(BF16)


def attend(order, pieces, blocks, gain, heads):
    block, model = blocks[0].shape
    slots = 4 * block
    pairs = (heads + 1) // 2
    low = shaped(BF16, pairs, slots, LANES)
    out_shape = [
        shaped(BF16, model, 4 * heads * HEAD),
        shaped(F32, 2 * pairs, slots, LANES),
        shaped(BF16, slots, heads * HEAD),
        shaped(F32, pairs, LANES, slots),
        low,
        low,
        low,
    ] + [shaped(BF16, block, model)] * 4
    out = kernel_call(
        functools.partial(attend_body, heads, len(pieces)),
        out_shape,
        order,
        [*pieces, *blocks, gain],
        10,
        [pltpu.SemaphoreType.DMA((len(pieces),))],
    )
    return out[:7], out[7:]


def attend_back_body(
    heads, scalars, g0, g1, g2, g3, w_ref, gain_ref, raw_ref, low_ref, totals_ref, q_ref, k_ref,
    v_ref, grad_ref, ggain_ref, p0, p1, p2, p3, ga_ref, dk_ref, dv_ref, gq_ref, gk_ref, gv_ref,
):
    rank = scalars[0]
    block = g0.shape[0]
    slots = 4 * block
    width = heads * HEAD
    pairs = (heads + 1) // 2
    w_out = w_ref[:, 3 * width : 4 * width]
    for k, g_ref in enumerate((g0, g1, g2, g3)):
        ga_ref[k * block : (k + 1) * block] = dot_nn(g_ref[...], w_out).astype(BF16)
    scale = jnp.asarray(math.sqrt(HEAD), BF16)
    causal = lax.broadcasted_iota(jnp.int32, (block, block), 0) <= lax.broadcasted_iota(
        jnp.int32, (block, block), 1
    )
    top = lax.broadcasted_iota(jnp.int32, (LANES, slots), 0) < HEAD
    for j in range(pairs):
        stop = min((j + 1) * LANES, width)
        key_turned = k_ref[j].T
        key_sides = [
            jnp.where(top, key_turned, jnp.zeros((), BF16)),
            jnp.where(top, jnp.zeros((), BF16), key_turned),
        ]
        gain = gain_ref[:, j * LANES : (j + 1) * LANES]
        dk_ref[...] = jnp.zeros_like(dk_ref)
        dv_ref[...] = jnp.zeros_like(dv_ref)
        gain_sum = jnp.zeros((1, LANES), F32)
        for a in range(4):
            rows = rank_rows(rank, a, block)
            keys = (a + 1) * block
            grad = column_pair(ga_ref[rows, j * LANES : stop], 0, LANES)
            out = column_pair(low_ref[rows, j * LANES : stop], 0, LANES)
            delta = (grad.astype(F32) * out.astype(F32)).T
            dq_turned = jnp.zeros((LANES, block), F32)
            for side in range(2):
                if 2 * j + side >= heads:
                    continue
                query = side_of(q_ref[j, a * block : keys], side) * scale
                grad_side = side_of(grad, side)
                log_row = totals_ref[j, side * HEAD : side * HEAD + 1, a * block : keys]
                delta_row = jnp.sum(delta[side * HEAD : (side + 1) * HEAD], axis=0, keepdims=True)
                weight = jnp.exp(dot_nt(k_ref[j, :keys], query) - log_row)
                last = jnp.where(causal, weight[a * block :], 0.0)
                weight = jnp.concatenate([weight[: a * block], last], axis=0) if a else last
                grad_weight = dot_nt(v_ref[j, :keys], grad_side)
                grad_score = (weight * (grad_weight - delta_row)).astype(BF16)
                dv_ref[:keys] += dot_nn(weight.astype(BF16), grad_side)
                dk_ref[:keys] += dot_nn(grad_score, query)
                dq_turned += dot_nn(key_sides[side][:, :keys], grad_score)
            dq = dq_turned.T * math.sqrt(HEAD)
            q_unit, factor = head_norm(raw_ref[j, a * block : keys])
            gain_sum += jnp.sum(dq * q_unit, axis=0, keepdims=True)
            scaled = dq * gain
            gq = factor * (scaled - q_unit * head_sums(scaled * q_unit))
            gq_ref[rows, j * LANES : stop] = gq[:, : stop - j * LANES].astype(BF16)
        for a in range(4):
            rows = rank_rows(rank, a, block)
            at = slice(a * block, (a + 1) * block)
            dk = dk_ref[at]
            k_unit, factor = head_norm(raw_ref[pairs + j, at])
            gain_sum += jnp.sum(dk * k_unit, axis=0, keepdims=True)
            scaled = dk * gain
            gk = factor * (scaled - k_unit * head_sums(scaled * k_unit))
            gk_ref[rows, j * LANES : stop] = gk[:, : stop - j * LANES].astype(BF16)
            gv_ref[rows, j * LANES : stop] = dv_ref[at][:, : stop - j * LANES].astype(BF16)
        ggain_ref[:, j * LANES : (j + 1) * LANES] = gain_sum
    w_project = w_ref[:, : 3 * width]
    for k, part_ref in enumerate((p0, p1, p2, p3)):
        at = slice(k * block, (k + 1) * block)
        grad = jnp.concatenate([gq_ref[at], gk_ref[at], gv_ref[at]], axis=1)
        grad_ref[at] = grad
        part_ref[...] = dot_nt(grad, w_project).astype(BF16)


def attend_back(order, grads, w_attn, gain, kept, heads):
    block, model = grads[0].shape
    slots = 4 * block
    width = heads * HEAD
    pairs = (heads + 1) // 2
    out_shape = [shaped(BF16, slots, 3 * width), shaped(F32, 1, pairs * LANES)] + [
        shaped(BF16, block, model)
    ] * 4
    return kernel_call(
        functools.partial(attend_back_body, heads),
        out_shape,
        order,
        [*grads, w_attn, gain, *kept],
        20,
        [pltpu.VMEM((slots, width), BF16)]
        + [pltpu.VMEM((slots, LANES), F32)] * 2
        + [pltpu.VMEM((slots, width), BF16)] * 3,
    )


def row_norm(values):
    factor = lax.rsqrt(jnp.sum(values * values, axis=-1, keepdims=True) + EPSILON)
    return values * factor, factor


def row_norm_back(grad, unit, factor):
    return factor * (grad - unit * jnp.sum(grad * unit, axis=-1, keepdims=True))


def branch_sum(parts):
    own, beside, across = (part[...].astype(F32) for part in parts)
    return own + beside + across


def first_norm_body(scalars, own, beside, across, hidden_ref, alpha_ref, unit_ref, out_ref, low_ref, factors_ref):
    unit, unit_factor = row_norm(branch_sum((own, beside, across)))
    hidden = hidden_ref[...]
    out, factor = row_norm(hidden + alpha_ref[...] * (unit - hidden))
    unit_ref[...] = unit
    out_ref[...] = out
    low_ref[...] = out.astype(BF16)
    lane = lax.broadcasted_iota(jnp.int32, factors_ref.shape, 1)
    factors_ref[...] = jnp.where(lane == 0, unit_factor, factor)


def first_norm(order, parts, hidden, alpha):
    rows, model = hidden.shape
    full = shaped(F32, rows, model)
    return kernel_call(
        first_norm_body,
        [full, full, shaped(BF16, rows, model), shaped(F32, rows, LANES)],
        order,
        [*parts, hidden, alpha.reshape(1, model)],
        10,
    )


def loss_body(
    total_slots, scalars, own, beside, across, first_ref, teacher_ref, alpha_ref, tokens_ref,
    out_ref, grad_ref, rest_ref, sums_ref,
):
    rank, length = scalars[0], scalars[1]
    unit, unit_factor = row_norm(branch_sum((own, beside, across)))
    first, alpha = first_ref[...], alpha_ref[...]
    out, factor = row_norm(first + alpha * (unit - first))
    out_ref[...] = out
    rows = out.shape[0]
    slot = rank * rows + lax.broadcasted_iota(jnp.int32, (rows, 1), 0)
    difference = jnp.where(slot < length, out - teacher_ref[...], 0.0)
    mixed = row_norm_back(2.0 * total_slots / tokens_ref[...] * difference, out, factor)
    rest_ref[...] = mixed * (1.0 - alpha)
    grad_ref[...] = row_norm_back(mixed * alpha, unit, unit_factor).astype(BF16)
    sums_ref[0:1] = jnp.sum(difference * difference, axis=0, keepdims=True)
    sums_ref[1:2] = jnp.sum(mixed * (unit - first), axis=0, keepdims=True)


def loss_and_grad(order, parts, first, teacher, alpha, tokens, total_slots):
    rows, model = first.shape
    full = shaped(F32, rows, model)
    return kernel_call(
        functools.partial(loss_body, total_slots),
        [full, shaped(BF16, rows, model), full, shaped(F32, 2, model)],
        order,
        [*parts, first, teacher, alpha.reshape(1, model), tokens.reshape(1, 1)],
        10,
    )


def first_back_body(
    scalars, own, beside, across, rest_ref, first_ref, unit_ref, hidden_ref, alpha_ref, factors_ref,
    grad_ref, out_ref, sums_ref,
):
    grad = rest_ref[...] + branch_sum((own, beside, across))
    alpha, unit = alpha_ref[...], unit_ref[...]
    mixed = row_norm_back(grad, first_ref[...], factors_ref[:, 1:2])
    sums_ref[...] = jnp.sum(mixed * (unit - hidden_ref[...]), axis=0, keepdims=True)
    out_ref[...] = mixed * (1.0 - alpha)
    grad_ref[...] = row_norm_back(mixed * alpha, unit, factors_ref[:, 0:1]).astype(BF16)


def first_back(order, parts, rest, first, unit, hidden, alpha, factors):
    rows, model = first.shape
    return kernel_call(
        first_back_body,
        [shaped(BF16, rows, model), shaped(F32, rows, model), shaped(F32, 1, model)],
        order,
        [*parts, rest, first, unit, hidden, alpha.reshape(1, model), factors],
        10,
    )


def feed_body(count, scalars, *refs):
    pieces, x_refs = refs[:count], refs[count : count + 4]
    gains_ref = refs[count + 4]
    w_ref, up_ref, gate_ref, hidden_ref = refs[count + 5 : count + 9]
    parts_out, arrived = refs[count + 9 : count + 13], refs[count + 13]
    ff = gains_ref.shape[1]
    block = x_refs[0].shape[0]
    for copy in place_pieces(scalars[2], pieces, w_ref, arrived):
        copy.wait()
    for k in (3, 2, 1, 0):
        at = slice(k * block, (k + 1) * block)
        x = x_refs[k][...]
        up = dot_nn(x, w_ref[:, :ff])
        gate = dot_nn(x, w_ref[:, ff : 2 * ff])
        scaled = gate * gains_ref[1:2]
        hidden = (up * gains_ref[0:1] * (scaled * jax.nn.sigmoid(scaled))).astype(BF16)
        up_ref[at] = up.astype(BF16)
        gate_ref[at] = gate.astype(BF16)
        hidden_ref[at] = hidden
        parts_out[k][...] = dot_nt(hidden, w_ref[:, 2 * ff :]).astype(BF16)


def feed(order, pieces, blocks, gains):
    block, model = blocks[0].shape
    ff = gains.shape[1]
    rows = shaped(BF16, 4 * block, ff)
    out = kernel_call(
        functools.partial(feed_body, len(pieces)),
        [shaped(BF16, model, 3 * ff), rows, rows, rows] + [shaped(BF16, block, model)] * 4,
        order,
        [*pieces, *blocks, gains],
        16,
        [pltpu.SemaphoreType.DMA((len(pieces),))],
    )
    return out[:4], out[4:]


def feed_back_body(scalars, g0, g1, g2, g3, w_ref, up_ref, gate_ref, gains_ref, grad_ref, sums_ref, p0, p1, p2, p3):
    ff = gains_ref.shape[1]
    block = g0.shape[0]
    grads, parts = (g0, g1, g2, g3), (p0, p1, p2, p3)
    up_gain, gate_gain = gains_ref[0:1], gains_ref[1:2]
    sums_ref[...] = jnp.zeros_like(sums_ref)
    for k in (3, 2, 1, 0):
        at = slice(k * block, (k + 1) * block)
        grad = dot_nn(grads[k][...], w_ref[:, 2 * ff :])
        up, gate = up_ref[at].astype(F32), gate_ref[at].astype(F32)
        scaled = gate * gate_gain
        chance = jax.nn.sigmoid(scaled)
        by_up = grad * (scaled * chance)
        by_gate = grad * (up * up_gain) * chance * (1.0 + scaled * (1.0 - chance))
        sums_ref[0:1] += jnp.sum(by_up * up, axis=0, keepdims=True)
        sums_ref[1:2] += jnp.sum(by_gate * gate, axis=0, keepdims=True)
        grad_ref[at, :ff] = (by_up * up_gain).astype(BF16)
        grad_ref[at, ff:] = (by_gate * gate_gain).astype(BF16)
        parts[k][...] = dot_nt(grad_ref[at], w_ref[:, : 2 * ff]).astype(BF16)


def feed_back(order, grads, w_feed, up, gate, gains):
    block, model = grads[0].shape
    ff = gains.shape[1]
    return kernel_call(
        feed_back_body,
        [shaped(BF16, 4 * block, 2 * ff), shaped(F32, 2, ff)] + [shaped(BF16, block, model)] * 4,
        order,
        [*grads, w_feed, up, gate, gains],
        18,
    )


def last_body(scalars, block, fore, hind, out_ref):
    out_ref[...] = block[...].astype(F32) + fore[...].astype(F32) + hind[...].astype(F32)


def turned_dot(left, right):
    return jnp.einsum("rd,rf->df", left, right, preferred_element_type=F32).astype(BF16)


def turn(blocks, turned_ref):
    rows = blocks[0].shape[0]
    for k, block in enumerate(blocks):
        turned_ref[:, k * rows : (k + 1) * rows] = block[...].T


def turned_body(scalars, left0, left1, left2, left3, right, token, out_ref, turned_ref):
    @pl.when(pl.program_id(0) == 0)
    def _():
        turn((left0, left1, left2, left3), turned_ref)
        for k in range(3):
            token[k] = scalars[k]

    out_ref[...] = dot_nn(turned_ref[...], right[...]).astype(BF16)


def turned_kernel(order, blocks, right):
    rows, width = blocks[0].shape
    chunk = 5 * LANES
    if right.shape[1] % chunk:
        chunk = right.shape[1]
    small = pl.BlockSpec(memory_space=pltpu.SMEM)
    order.token, out = pl.pallas_call(
        turned_body,
        grid=(right.shape[1] // chunk,),
        out_shape=[shaped(jnp.int32, 3), shaped(BF16, width, right.shape[1])],
        in_specs=[small]
        + [pl.BlockSpec((rows, width), lambda i: (0, 0))] * 4
        + [pl.BlockSpec((4 * rows, chunk), lambda i: (0, i))],
        out_specs=[small, pl.BlockSpec((width, chunk), lambda i: (0, i))],
        scratch_shapes=[pltpu.VMEM((width, 4 * rows), BF16)],
        cost_estimate=pl.CostEstimate(flops=1, transcendentals=0, bytes_accessed=1),
        compiler_params=pltpu.CompilerParams(vmem_limit_bytes=60 * MEGA),
        name="turned_dot",
    )(order.token, *blocks, right)
    return out


def on_device(
    hidden_in,
    lengths,
    teacher,
    w_query,
    w_key,
    w_value,
    w_attn_out,
    w_up,
    w_gate,
    w_down,
    s_qk,
    alpha_attn,
    alpha_mlp,
    s_up,
    s_gate,
):
    tensor_rank = lax.axis_index("tensor")
    seq_count, local_slots, model_width = hidden_in.shape
    slot_count = local_slots * lax.axis_size("tensor")
    heads_width = w_query.shape[1]
    head_count = heads_width // HEAD
    ff_local = w_up.shape[1]
    gate_root = math.sqrt(model_width)
    total_slots = slot_count * seq_count * lax.axis_size("dp")
    hidden = hidden_in.reshape(local_slots, model_width)
    teacher = teacher.reshape(local_slots, model_width)
    length = lengths[0]
    order = Order(
        jnp.stack([tensor_rank.astype(jnp.int32), length, lax.axis_index("dp").astype(jnp.int32)])
    )
    own_part = lambda vector, width: lax.dynamic_slice_in_dim(vector, tensor_rank * width, width)
    qk_gain = jnp.pad(own_part(s_qk, heads_width), (0, heads_width % LANES)).reshape(1, -1)
    gains = jnp.stack([own_part(s_up, ff_local), own_part(s_gate, ff_local) * gate_root])

    attn_ring = RingGather(jnp.concatenate([w_query, w_key, w_value, w_attn_out.T], axis=1))
    feed_ring = RingGather(jnp.concatenate([w_up, w_gate, w_down.T], axis=1))
    attn_ring.hop(order)
    attn_ring.hop(order)
    qk_gain, gains = order.tie((qk_gain, gains))
    stream = gather_rows(hidden.astype(BF16), order)
    attn_ring.hop(order)
    attn_ring.hop(order)
    if short_axis(attn_ring.size):
        attn_ring.pieces[-2:] = order.tie(attn_ring.pieces[-2:])
    feed_ring.hop(order)
    kept, parts = attend(order, attn_ring.pieces, stream, qk_gain, head_count)
    w_attn, kept = kept[0], kept[1:]
    parts = scatter_rows(parts, lambda: feed_ring.hop(order))
    attn_unit, first_out, first_low, factors = first_norm(order, parts, hidden, alpha_attn)
    mlp_in = gather_rows(first_low, order, lambda: feed_ring.hop(order))
    feed_ring.hop(order)
    token_count = all_sum(lengths.astype(F32))[0]
    mlp_rows = order.tie(jnp.concatenate(mlp_in, axis=0))
    (w_feed, up_raw, gate_raw, hidden_low), parts = feed(order, feed_ring.pieces, mlp_in, gains)
    parts = scatter_rows(parts)
    output, grad_mlp_sum, grad_first, loss_sums = loss_and_grad(
        order, parts, first_out, teacher, alpha_mlp, token_count, total_slots
    )

    grad_mlp = gather_rows(grad_mlp_sum, order)
    grad_rows, hidden_low = order.tie((jnp.concatenate(grad_mlp, axis=0), hidden_low))
    grad_low = order.tie(turned_dot(grad_rows, hidden_low))
    low_reduce = RingReduce(grad_low, order)
    grad_pair, ff_sums, *parts = feed_back(order, grad_mlp, w_feed, up_raw, gate_raw, gains)
    low_reduce.hop(order)
    mlp_rows, grad_pair = order.tie((mlp_rows, grad_pair))
    grad_w_up = order.tie(turned_dot(mlp_rows, grad_pair[:, :ff_local]))
    low_reduce.hop(order)
    mlp_rows, grad_pair = order.tie((mlp_rows, grad_pair))
    grad_w_gate = order.tie(turned_dot(mlp_rows, grad_pair[:, ff_local:]))
    low_reduce.hop(order)
    parts = scatter_rows(parts)
    low_reduce.wait(order)
    pair_reduce = RingReduce(jnp.concatenate([grad_w_up, grad_w_gate], axis=1), order)
    grad_attn_sum, grad_input, attn_sums = first_back(
        order, parts, grad_first, first_out, attn_unit, hidden, alpha_attn, factors
    )
    grad_attn = gather_rows(grad_attn_sum, order, lambda: pair_reduce.hop(order))
    pair_reduce.hop(order)
    grad_w_down = low_reduce.total(order).T
    grad_project, gain_sums, *parts = attend_back(
        order, grad_attn, w_attn, qk_gain, kept, head_count
    )
    pair_reduce.hop(order)
    parts = scatter_rows(parts)
    grad_w_attn = order.tie(
        jnp.concatenate(
            [
                turned_kernel(order, stream, grad_project),
                turned_kernel(order, grad_attn, kept[1]),
            ],
            axis=1,
        )
    )
    attn_reduce = RingReduce(grad_w_attn, order)
    pair_reduce.wait(order)
    parts = order.tie(parts)
    loss_sums, attn_sums, gain_sums, ff_sums = order.tie(
        (loss_sums, attn_sums, gain_sums, ff_sums)
    )
    grad_input = grad_input + sum(part.astype(F32) for part in parts)

    def placed(values):
        width = values.shape[0]
        return lax.dynamic_update_slice_in_dim(
            jnp.zeros((width * lax.axis_size("tensor"),), F32), values, tensor_rank * width, 0
        )

    vectors = jnp.concatenate(
        [
            jnp.sum(loss_sums[0]).reshape(1),
            attn_sums[0],
            loss_sums[1],
            placed(gain_sums[0, :heads_width]),
            placed(ff_sums[0]),
            placed(ff_sums[1] * gate_root),
        ]
    )
    vectors = order.tie(tensor_sum(vectors))

    def attn_step(values):
        attn_reduce.hop(order)
        return order.tie(values)

    vectors = all_sum(vectors, attn_step)
    grad_w_pair = pair_reduce.total(order)
    grad_w_attn = attn_reduce.total(order, last=True)
    loss = vectors[0] / token_count
    cuts = [1 + model_width * k for k in range(4)] + [1 + 3 * model_width + s_up.shape[0]]
    return (
        loss,
        output[None],
        grad_input[None],
        grad_w_attn[:, :heads_width],
        grad_w_attn[:, heads_width : 2 * heads_width],
        grad_w_attn[:, 2 * heads_width : 3 * heads_width],
        grad_w_attn[:, 3 * heads_width :].T,
        grad_w_pair[:, :ff_local],
        grad_w_pair[:, ff_local:],
        grad_w_down,
        vectors[cuts[2] : cuts[3]],
        vectors[cuts[0] : cuts[1]],
        vectors[cuts[1] : cuts[2]],
        vectors[cuts[3] : cuts[4]],
        vectors[cuts[4] :],
    )


def solution(mesh):
    in_specs = (
        P("dp", "tensor", None),
        P("dp"),
        P("dp", "tensor", None),
        P("dp", "tensor"),
        P("dp", "tensor"),
        P("dp", "tensor"),
        P("tensor", "dp"),
        P("dp", "tensor"),
        P("dp", "tensor"),
        P("tensor", "dp"),
        P(),
        P(),
        P(),
        P(),
        P(),
    )
    out_specs = (
        P(),
        P("dp", "tensor", None),
        P("dp", "tensor", None),
        P("dp", "tensor"),
        P("dp", "tensor"),
        P("dp", "tensor"),
        P("tensor", "dp"),
        P("dp", "tensor"),
        P("dp", "tensor"),
        P("tensor", "dp"),
        P(),
        P(),
        P(),
        P(),
        P(),
    )
    return jax.shard_map(
        on_device, mesh=mesh, in_specs=in_specs, out_specs=out_specs, check_vma=False
    )
```

```python
import functools
import math

import jax
import jax.numpy as jnp
from jax import lax
from jax.experimental import pallas as pl
from jax.experimental.pallas import tpu as pltpu
from jax.sharding import PartitionSpec as P

HEAD = 64
LANES = 2 * HEAD


EPSILON = 1e-06
BF16 = jnp.bfloat16
F32 = jnp.float32
MEGA = 2**20


def short_axis(size):
    return size % 2 == 0 and size <= 16


class Order:
    def __init__(self, token):
        self.token = token

    def tie(self, values):
        values, self.token = lax.optimization_barrier((values, self.token))
        return values


def ring_place(size, index):
    return index // 2 + (index % 2) * (size - 1 - 2 * (index // 2))


def ring_device(size, place):
    place = (place + 2 * size) % size
    later = (2 * place) // size
    return 2 * place + later * (2 * size - 1 - 4 * place)


def ring_steps(size):
    order = [ring_device(size, place) for place in range(size)]
    ahead = [(order[i], order[(i + 1) % size]) for i in range(size)]
    return ahead, [(b, a) for a, b in ahead]


def place_pieces(index, pieces, full, arrived):
    if len(pieces) == 1:
        copies = [pltpu.make_async_copy(pieces[0], full, arrived.at[0])]
    else:
        size = len(pieces) - 1
        rows, cols = full.shape[0] // size, full.shape[1]
        half = cols // 2
        mine = ring_place(size, index)
        copies = []
        for k, piece in enumerate(pieces):
            step = (k + 1) // 2
            source = ring_device(size, mine + (step if k % 2 == 0 else -step))
            span = pl.ds(pl.multiple_of(source * rows, rows), rows)
            target = full.at[span]
            if step == size // 2:
                target = full.at[span, pl.ds(0, half) if k % 2 else pl.ds(half, cols - half)]
            copies.append(pltpu.make_async_copy(piece, target, arrived.at[k]))
    for copy in copies:
        copy.start()
    return copies


class RingGather:
    def __init__(self, shard):
        self.size = lax.axis_size("dp")
        self.fore, self.hind = shard, shard
        self.pieces = [shard]
        if not short_axis(self.size):
            self.pieces = [lax.all_gather(shard, "dp", axis=0, tiled=True)]

    def hop(self, order):
        if not short_axis(self.size):
            return
        ahead, back = ring_steps(self.size)
        if len(self.pieces) > 1:
            self.fore, self.hind = self.pieces[-2:] = order.tie((self.fore, self.hind))
        else:
            self.fore = self.hind = self.pieces[0] = order.tie(self.fore)
        fore, hind = self.fore, self.hind
        if len(self.pieces) == self.size - 1:
            half = fore.shape[1] // 2
            fore, hind = fore[:, :half], hind[:, half:]
        self.fore = lax.ppermute(fore, "dp", ahead)
        self.hind = lax.ppermute(hind, "dp", back)
        self.pieces += [self.fore, self.hind]


class RingReduce:
    def __init__(self, partial, order):
        self.size = lax.axis_size("dp")
        self.partial = partial
        if not short_axis(self.size):
            return
        self.mine = ring_place(self.size, lax.axis_index("dp"))
        self.left = self.size // 2
        half = partial.shape[1] // 2
        block = self.block(self.left)
        self.send(order.tie((block[:, :half], block[:, half:])))

    def block(self, offset):
        rows, cols = self.partial.shape[0] // self.size, self.partial.shape[1]
        device = ring_device(self.size, self.mine + offset)
        return lax.dynamic_slice(self.partial, (device * rows, 0), (rows, cols))

    def send(self, parts):
        ahead, back = ring_steps(self.size)
        self.fore = lax.ppermute(parts[0], "dp", ahead)
        self.hind = lax.ppermute(parts[1], "dp", back)
        self.left -= 1

    def hop(self, order):
        if not short_axis(self.size):
            return
        cols = self.partial.shape[1]
        self.fore, self.hind = order.tie((self.fore, self.hind))

        def total(offset, came, start):
            stop = start + came.shape[1]
            block = self.block(offset)
            sum_part = (block[:, start:stop].astype(F32) + came.astype(F32)).astype(BF16)
            return lax.dynamic_update_slice(block, sum_part, (0, start))

        fore = total(self.left, self.fore, 0)
        hind = total(-self.left, self.hind, cols - self.hind.shape[1])
        self.send(order.tie((fore, hind)))

    def wait(self, order):
        if short_axis(self.size):
            self.fore, self.hind = order.tie((self.fore, self.hind))

    def total(self, order, last=False):
        if not short_axis(self.size):
            return lax.psum_scatter(self.partial, "dp", scatter_dimension=0, tiled=True).astype(F32)
        while self.left > 0:
            self.hop(order)
        if last:
            pieces = order.tie((self.block(0), self.fore, self.hind))
            return kernel_call(last_body, [shaped(F32, *pieces[0].shape)], order, pieces, 8)[0]
        return self.block(0).astype(F32) + self.fore.astype(F32) + self.hind.astype(F32)


def tensor_swap(values, bit):
    size = lax.axis_size("tensor")
    return lax.ppermute(values, "tensor", [(i, i ^ bit) for i in range(size)])


def gather_rows(rows, order, during=lambda: None):
    rows = order.tie(rows)
    across = tensor_swap(rows, 2)
    beside = tensor_swap(rows, 1)
    during()
    return [rows, beside, across, tensor_swap(across, 1)]


def scatter_rows(blocks, during=lambda: None, order=None):
    own, beside, across, opposite = blocks
    across = across.astype(F32) + tensor_swap(opposite, 1).astype(F32)
    across = across.astype(BF16)
    if order is not None:
        across = order.tie(across)
    across = tensor_swap(across, 2)
    beside = tensor_swap(beside, 1)
    during()
    return [own, beside, across]


def all_sum(values, during=lambda values: values):
    dp_size = lax.axis_size("dp")
    if dp_size & (dp_size - 1) or dp_size > 16:
        return lax.psum(values, "dp")
    bit = 1
    while bit < dp_size:
        values = during(values)
        values = values + lax.ppermute(values, "dp", [(i, i ^ bit) for i in range(dp_size)])
        bit *= 2
    return values


def tensor_sum(values):
    values = values + tensor_swap(values, 1)
    return values + tensor_swap(values, 2)


def dot_nt(left, right):
    return lax.dot_general(left, right, (((1,), (1,)), ((), ())), preferred_element_type=F32)


def dot_nn(left, right):
    return lax.dot_general(left, right, (((1,), (0,)), ((), ())), preferred_element_type=F32)


def column_pair(values, start, stop):
    piece = values[:, start : min(start + LANES, stop)]
    if piece.shape[1] < LANES:
        piece = jnp.concatenate([piece, jnp.zeros((piece.shape[0], HEAD), piece.dtype)], axis=1)
    return piece


def low_half(rows):
    return lax.broadcasted_iota(jnp.int32, (rows, LANES), 1) < HEAD


def head_sums(values):
    first = low_half(values.shape[0])
    left = jnp.sum(jnp.where(first, values, 0.0), axis=-1, keepdims=True)
    right = jnp.sum(jnp.where(first, 0.0, values), axis=-1, keepdims=True)
    return jnp.where(first, left, right)


def head_norm(values):
    factor = lax.rsqrt(head_sums(values * values) + EPSILON)
    return values * factor, factor


def side_of(values, side):
    first = low_half(values.shape[0])
    zero = jnp.zeros_like(values)
    return jnp.where(first, values, zero) if side == 0 else jnp.where(first, zero, values)


def kernel_call(body, out_shape, order, arrays, room, scratch=()):
    whole = pl.BlockSpec(memory_space=pltpu.VMEM)
    small = pl.BlockSpec(memory_space=pltpu.SMEM)
    count = len(arrays) + 1

    def with_token(*refs):
        body(*refs[:count], *refs[count + 1 :])
        for k in range(3):
            refs[count][k] = refs[0][k]

    order.token, *out = pl.pallas_call(
        with_token,
        out_shape=[shaped(jnp.int32, 3), *out_shape],
        in_specs=[small] + [whole] * len(arrays),
        out_specs=[small] + [whole] * len(out_shape),
        scratch_shapes=list(scratch),
        cost_estimate=pl.CostEstimate(flops=1, transcendentals=0, bytes_accessed=1),
        compiler_params=pltpu.CompilerParams(vmem_limit_bytes=room * MEGA),
        name=(body.func if isinstance(body, functools.partial) else body).__name__,
    )(order.token, *arrays)
    return out


def shaped(dtype, *shape):
    return jax.ShapeDtypeStruct(shape, dtype)


def rank_rows(rank, slot_block, block):
    return pl.ds(pl.multiple_of((rank ^ slot_block) * block, block), block)


def attend_body(heads, count, scalars, *refs):
    pieces, (x0, x1, x2, x3, gain_ref) = refs[:count], refs[count : count + 5]
    (w_ref, raw_ref, low_ref, totals_ref, q_ref, k_ref, v_ref) = refs[count + 5 : count + 12]
    parts_out = refs[count + 12 : count + 16]
    arrived = refs[count + 16]
    rank, length = scalars[0], scalars[1]
    block = x0.shape[0]
    slots = 4 * block
    width = heads * HEAD
    pairs = (heads + 1) // 2
    for copy in place_pieces(scalars[2], pieces, w_ref, arrived):
        copy.wait()
    for k, x_ref in enumerate((x0, x1, x2, x3)):
        at = pl.ds(pl.multiple_of((rank ^ k) * block, block), block)
        raw = dot_nn(x_ref[...], w_ref[:, : 3 * width + HEAD])
        for j in range(pairs):
            gain = gain_ref[:, j * LANES : (j + 1) * LANES]
            q_raw = column_pair(raw, j * LANES, width)
            k_raw = column_pair(raw, width + j * LANES, 2 * width)
            raw_ref[j, at] = q_raw
            raw_ref[pairs + j, at] = k_raw
            q_ref[j, at] = (head_norm(q_raw)[0] * gain).astype(BF16)
            k_ref[j, at] = (head_norm(k_raw)[0] * gain).astype(BF16)
            v_ref[j, at] = column_pair(raw, 2 * width + j * LANES, 3 * width).astype(BF16)
    scale = jnp.asarray(math.sqrt(HEAD), BF16)
    here = lax.broadcasted_iota(jnp.int32, (slots, LANES), 0) < length
    counted = jnp.where(here, 1.0, 0.0).astype(BF16)
    causal = lax.broadcasted_iota(jnp.int32, (block, block), 1) <= lax.broadcasted_iota(
        jnp.int32, (block, block), 0
    )
    first_rows = low_half(slots)
    first = low_half(block)
    for j in range(pairs):
        value = jnp.where(here, v_ref[j], jnp.zeros((), BF16))
        with_count = [jnp.where(first_rows, value, counted), jnp.where(first_rows, counted, value)]
        for a in range(4):
            keys = (a + 1) * block
            parts, logs = [], []
            for side in range(2):
                if 2 * j + side >= heads:
                    parts.append(jnp.zeros((block, LANES), F32))
                    logs.append(jnp.zeros((block, LANES), F32))
                    continue
                query = side_of(q_ref[j, a * block : keys], side) * scale
                weight = jnp.exp(dot_nt(query, k_ref[j, :keys]))
                last = jnp.where(causal, weight[:, a * block :], 0.0)
                weight = jnp.concatenate([weight[:, : a * block], last], axis=1) if a else last
                summed = dot_nn(weight.astype(BF16), with_count[side][:keys])
                total = pltpu.roll(summed, HEAD, 1)
                parts.append(summed / total)
                logs.append(jnp.log(total))
            out = jnp.where(first, parts[0], parts[1])
            log_total = jnp.where(first, logs[0], logs[1])
            totals_ref[j, :, a * block : keys] = log_total.T
            stop = min((j + 1) * LANES, width)
            low_ref[rank_rows(rank, a, block), j * LANES : stop] = out[
                :, : stop - j * LANES
            ].astype(BF16)
    w_out = w_ref[:, 3 * width : 4 * width]
    for k, part_ref in enumerate(parts_out):
        part_ref[...] = dot_nt(low_ref[k * block : (k + 1) * block], w_out).astype(BF16)


def attend(order, pieces, blocks, gain, heads):
    block, model = blocks[0].shape
    slots = 4 * block
    pairs = (heads + 1) // 2
    low = shaped(BF16, pairs, slots, LANES)
    out_shape = [
        shaped(BF16, model, 4 * heads * HEAD),
        shaped(F32, 2 * pairs, slots, LANES),
        shaped(BF16, slots, heads * HEAD),
        shaped(F32, pairs, LANES, slots),
        low,
        low,
        low,
    ] + [shaped(BF16, block, model)] * 4
    out = kernel_call(
        functools.partial(attend_body, heads, len(pieces)),
        out_shape,
        order,
        [*pieces, *blocks, gain],
        10,
        [pltpu.SemaphoreType.DMA((len(pieces),))],
    )
    return out[:7], out[7:]


def attend_back_body(
    heads, scalars, g0, g1, g2, g3, w_ref, gain_ref, raw_ref, low_ref, totals_ref, q_ref, k_ref,
    v_ref, grad_ref, ggain_ref, p0, p1, p2, p3, ga_ref, dk_ref, dv_ref, gq_ref, gk_ref, gv_ref,
):
    rank = scalars[0]
    block = g0.shape[0]
    slots = 4 * block
    width = heads * HEAD
    pairs = (heads + 1) // 2
    w_out = w_ref[:, 3 * width : 4 * width]
    for k, g_ref in enumerate((g0, g1, g2, g3)):
        ga_ref[k * block : (k + 1) * block] = dot_nn(g_ref[...], w_out).astype(BF16)
    scale = jnp.asarray(math.sqrt(HEAD), BF16)
    causal = lax.broadcasted_iota(jnp.int32, (block, block), 0) <= lax.broadcasted_iota(
        jnp.int32, (block, block), 1
    )
    top = lax.broadcasted_iota(jnp.int32, (LANES, slots), 0) < HEAD
    for j in range(pairs):
        stop = min((j + 1) * LANES, width)
        key_turned = k_ref[j].T
        key_sides = [
            jnp.where(top, key_turned, jnp.zeros((), BF16)),
            jnp.where(top, jnp.zeros((), BF16), key_turned),
        ]
        gain = gain_ref[:, j * LANES : (j + 1) * LANES]
        dk_ref[...] = jnp.zeros_like(dk_ref)
        dv_ref[...] = jnp.zeros_like(dv_ref)
        gain_sum = jnp.zeros((1, LANES), F32)
        for a in range(4):
            rows = rank_rows(rank, a, block)
            keys = (a + 1) * block
            grad = column_pair(ga_ref[rows, j * LANES : stop], 0, LANES)
            out = column_pair(low_ref[rows, j * LANES : stop], 0, LANES)
            delta = (grad.astype(F32) * out.astype(F32)).T
            dq_turned = jnp.zeros((LANES, block), F32)
            for side in range(2):
                if 2 * j + side >= heads:
                    continue
                query = side_of(q_ref[j, a * block : keys], side) * scale
                grad_side = side_of(grad, side)
                log_row = totals_ref[j, side * HEAD : side * HEAD + 1, a * block : keys]
                delta_row = jnp.sum(delta[side * HEAD : (side + 1) * HEAD], axis=0, keepdims=True)
                weight = jnp.exp(dot_nt(k_ref[j, :keys], query) - log_row)
                last = jnp.where(causal, weight[a * block :], 0.0)
                weight = jnp.concatenate([weight[: a * block], last], axis=0) if a else last
                grad_weight = dot_nt(v_ref[j, :keys], grad_side)
                grad_score = (weight * (grad_weight - delta_row)).astype(BF16)
                dv_ref[:keys] += dot_nn(weight.astype(BF16), grad_side)
                dk_ref[:keys] += dot_nn(grad_score, query)
                dq_turned += dot_nn(key_sides[side][:, :keys], grad_score)
            dq = dq_turned.T * math.sqrt(HEAD)
            q_unit, factor = head_norm(raw_ref[j, a * block : keys])
            gain_sum += jnp.sum(dq * q_unit, axis=0, keepdims=True)
            scaled = dq * gain
            gq = factor * (scaled - q_unit * head_sums(scaled * q_unit))
            gq_ref[rows, j * LANES : stop] = gq[:, : stop - j * LANES].astype(BF16)
        for a in range(4):
            rows = rank_rows(rank, a, block)
            at = slice(a * block, (a + 1) * block)
            dk = dk_ref[at]
            k_unit, factor = head_norm(raw_ref[pairs + j, at])
            gain_sum += jnp.sum(dk * k_unit, axis=0, keepdims=True)
            scaled = dk * gain
            gk = factor * (scaled - k_unit * head_sums(scaled * k_unit))
            gk_ref[rows, j * LANES : stop] = gk[:, : stop - j * LANES].astype(BF16)
            gv_ref[rows, j * LANES : stop] = dv_ref[at][:, : stop - j * LANES].astype(BF16)
        ggain_ref[:, j * LANES : (j + 1) * LANES] = gain_sum
    w_project = w_ref[:, : 3 * width]
    for k, part_ref in enumerate((p0, p1, p2, p3)):
        at = slice(k * block, (k + 1) * block)
        grad = jnp.concatenate([gq_ref[at], gk_ref[at], gv_ref[at]], axis=1)
        grad_ref[at] = grad
        part_ref[...] = dot_nt(grad, w_project).astype(BF16)


def attend_back(order, grads, w_attn, gain, kept, heads):
    block, model = grads[0].shape
    slots = 4 * block
    width = heads * HEAD
    pairs = (heads + 1) // 2
    out_shape = [shaped(BF16, slots, 3 * width), shaped(F32, 1, pairs * LANES)] + [
        shaped(BF16, block, model)
    ] * 4
    return kernel_call(
        functools.partial(attend_back_body, heads),
        out_shape,
        order,
        [*grads, w_attn, gain, *kept],
        20,
        [pltpu.VMEM((slots, width), BF16)]
        + [pltpu.VMEM((slots, LANES), F32)] * 2
        + [pltpu.VMEM((slots, width), BF16)] * 3,
    )


def row_norm(values):
    factor = lax.rsqrt(jnp.sum(values * values, axis=-1, keepdims=True) + EPSILON)
    return values * factor, factor


def row_norm_back(grad, unit, factor):
    return factor * (grad - unit * jnp.sum(grad * unit, axis=-1, keepdims=True))


def branch_sum(parts):
    own, beside, across = (part[...].astype(F32) for part in parts)
    return own + beside + across


def first_norm_body(scalars, own, beside, across, hidden_ref, alpha_ref, unit_ref, out_ref, low_ref, factors_ref):
    unit, unit_factor = row_norm(branch_sum((own, beside, across)))
    hidden = hidden_ref[...]
    out, factor = row_norm(hidden + alpha_ref[...] * (unit - hidden))
    unit_ref[...] = unit
    out_ref[...] = out
    low_ref[...] = out.astype(BF16)
    lane = lax.broadcasted_iota(jnp.int32, factors_ref.shape, 1)
    factors_ref[...] = jnp.where(lane == 0, unit_factor, factor)


def first_norm(order, parts, hidden, alpha):
    rows, model = hidden.shape
    full = shaped(F32, rows, model)
    return kernel_call(
        first_norm_body,
        [full, full, shaped(BF16, rows, model), shaped(F32, rows, LANES)],
        order,
        [*parts, hidden, alpha.reshape(1, model)],
        10,
    )


def loss_body(
    total_slots, scalars, own, beside, across, first_ref, teacher_ref, alpha_ref, tokens_ref,
    out_ref, grad_ref, rest_ref, sums_ref,
):
    rank, length = scalars[0], scalars[1]
    unit, unit_factor = row_norm(branch_sum((own, beside, across)))
    first, alpha = first_ref[...], alpha_ref[...]
    out, factor = row_norm(first + alpha * (unit - first))
    out_ref[...] = out
    rows = out.shape[0]
    slot = rank * rows + lax.broadcasted_iota(jnp.int32, (rows, 1), 0)
    difference = jnp.where(slot < length, out - teacher_ref[...], 0.0)
    mixed = row_norm_back(2.0 * total_slots / tokens_ref[...] * difference, out, factor)
    rest_ref[...] = mixed * (1.0 - alpha)
    grad_ref[...] = row_norm_back(mixed * alpha, unit, unit_factor).astype(BF16)
    sums_ref[0:1] = jnp.sum(difference * difference, axis=0, keepdims=True)
    sums_ref[1:2] = jnp.sum(mixed * (unit - first), axis=0, keepdims=True)


def loss_and_grad(order, parts, first, teacher, alpha, tokens, total_slots):
    rows, model = first.shape
    full = shaped(F32, rows, model)
    return kernel_call(
        functools.partial(loss_body, total_slots),
        [full, shaped(BF16, rows, model), full, shaped(F32, 2, model)],
        order,
        [*parts, first, teacher, alpha.reshape(1, model), tokens.reshape(1, 1)],
        10,
    )


def first_back_body(
    scalars, own, beside, across, rest_ref, first_ref, unit_ref, hidden_ref, alpha_ref, factors_ref,
    grad_ref, out_ref, sums_ref,
):
    grad = rest_ref[...] + branch_sum((own, beside, across))
    alpha, unit = alpha_ref[...], unit_ref[...]
    mixed = row_norm_back(grad, first_ref[...], factors_ref[:, 1:2])
    sums_ref[...] = jnp.sum(mixed * (unit - hidden_ref[...]), axis=0, keepdims=True)
    out_ref[...] = mixed * (1.0 - alpha)
    grad_ref[...] = row_norm_back(mixed * alpha, unit, factors_ref[:, 0:1]).astype(BF16)


def first_back(order, parts, rest, first, unit, hidden, alpha, factors):
    rows, model = first.shape
    return kernel_call(
        first_back_body,
        [shaped(BF16, rows, model), shaped(F32, rows, model), shaped(F32, 1, model)],
        order,
        [*parts, rest, first, unit, hidden, alpha.reshape(1, model), factors],
        10,
    )


def feed_body(count, scalars, *refs):
    pieces, x_refs = refs[:count], refs[count : count + 4]
    gains_ref = refs[count + 4]
    w_ref, up_ref, gate_ref, hidden_ref = refs[count + 5 : count + 9]
    parts_out, arrived = refs[count + 9 : count + 13], refs[count + 13]
    ff = gains_ref.shape[1]
    block = x_refs[0].shape[0]
    for copy in place_pieces(scalars[2], pieces, w_ref, arrived):
        copy.wait()
    for k in (3, 2, 1, 0):
        at = slice(k * block, (k + 1) * block)
        x = x_refs[k][...]
        up = dot_nn(x, w_ref[:, :ff])
        gate = dot_nn(x, w_ref[:, ff : 2 * ff])
        scaled = gate * gains_ref[1:2]
        hidden = (up * gains_ref[0:1] * (scaled * jax.nn.sigmoid(scaled))).astype(BF16)
        up_ref[at] = up.astype(BF16)
        gate_ref[at] = gate.astype(BF16)
        hidden_ref[at] = hidden
        parts_out[k][...] = dot_nt(hidden, w_ref[:, 2 * ff :]).astype(BF16)


def feed(order, pieces, blocks, gains):
    block, model = blocks[0].shape
    ff = gains.shape[1]
    rows = shaped(BF16, 4 * block, ff)
    out = kernel_call(
        functools.partial(feed_body, len(pieces)),
        [shaped(BF16, model, 3 * ff), rows, rows, rows] + [shaped(BF16, block, model)] * 4,
        order,
        [*pieces, *blocks, gains],
        16,
        [pltpu.SemaphoreType.DMA((len(pieces),))],
    )
    return out[:4], out[4:]


def feed_back_body(scalars, g0, g1, g2, g3, w_ref, up_ref, gate_ref, gains_ref, grad_ref, sums_ref, p0, p1, p2, p3):
    ff = gains_ref.shape[1]
    block = g0.shape[0]
    grads, parts = (g0, g1, g2, g3), (p0, p1, p2, p3)
    up_gain, gate_gain = gains_ref[0:1], gains_ref[1:2]
    sums_ref[...] = jnp.zeros_like(sums_ref)
    for k in (3, 2, 1, 0):
        at = slice(k * block, (k + 1) * block)
        grad = dot_nn(grads[k][...], w_ref[:, 2 * ff :])
        up, gate = up_ref[at].astype(F32), gate_ref[at].astype(F32)
        scaled = gate * gate_gain
        chance = jax.nn.sigmoid(scaled)
        by_up = grad * (scaled * chance)
        by_gate = grad * (up * up_gain) * chance * (1.0 + scaled * (1.0 - chance))
        sums_ref[0:1] += jnp.sum(by_up * up, axis=0, keepdims=True)
        sums_ref[1:2] += jnp.sum(by_gate * gate, axis=0, keepdims=True)
        grad_ref[at, :ff] = (by_up * up_gain).astype(BF16)
        grad_ref[at, ff:] = (by_gate * gate_gain).astype(BF16)
        parts[k][...] = dot_nt(grad_ref[at], w_ref[:, : 2 * ff]).astype(BF16)


def feed_back(order, grads, w_feed, up, gate, gains):
    block, model = grads[0].shape
    ff = gains.shape[1]
    return kernel_call(
        feed_back_body,
        [shaped(BF16, 4 * block, 2 * ff), shaped(F32, 2, ff)] + [shaped(BF16, block, model)] * 4,
        order,
        [*grads, w_feed, up, gate, gains],
        18,
    )


def last_body(scalars, block, fore, hind, out_ref):
    out_ref[...] = block[...].astype(F32) + fore[...].astype(F32) + hind[...].astype(F32)


def turned_dot(left, right):
    return jnp.einsum("rd,rf->df", left, right, preferred_element_type=F32).astype(BF16)


def turn(blocks, turned_ref):
    rows = blocks[0].shape[0]
    for k, block in enumerate(blocks):
        turned_ref[:, k * rows : (k + 1) * rows] = block[...].T


def turned_body(scalars, left0, left1, left2, left3, right, token, out_ref, turned_ref):
    @pl.when(pl.program_id(0) == 0)
    def _():
        turn((left0, left1, left2, left3), turned_ref)
        for k in range(3):
            token[k] = scalars[k]

    out_ref[...] = dot_nn(turned_ref[...], right[...]).astype(BF16)


def turned_kernel(order, blocks, right):
    rows, width = blocks[0].shape
    chunk = 5 * LANES
    if right.shape[1] % chunk:
        chunk = right.shape[1]
    small = pl.BlockSpec(memory_space=pltpu.SMEM)
    order.token, out = pl.pallas_call(
        turned_body,
        grid=(right.shape[1] // chunk,),
        out_shape=[shaped(jnp.int32, 3), shaped(BF16, width, right.shape[1])],
        in_specs=[small]
        + [pl.BlockSpec((rows, width), lambda i: (0, 0))] * 4
        + [pl.BlockSpec((4 * rows, chunk), lambda i: (0, i))],
        out_specs=[small, pl.BlockSpec((width, chunk), lambda i: (0, i))],
        scratch_shapes=[pltpu.VMEM((width, 4 * rows), BF16)],
        cost_estimate=pl.CostEstimate(flops=1, transcendentals=0, bytes_accessed=1),
        compiler_params=pltpu.CompilerParams(vmem_limit_bytes=60 * MEGA),
        name="turned_dot",
    )(order.token, *blocks, right)
    return out


def on_device(
    hidden_in,
    lengths,
    teacher,
    w_query,
    w_key,
    w_value,
    w_attn_out,
    w_up,
    w_gate,
    w_down,
    s_qk,
    alpha_attn,
    alpha_mlp,
    s_up,
    s_gate,
):
    tensor_rank = lax.axis_index("tensor")
    seq_count, local_slots, model_width = hidden_in.shape
    slot_count = local_slots * lax.axis_size("tensor")
    heads_width = w_query.shape[1]
    head_count = heads_width // HEAD
    ff_local = w_up.shape[1]
    gate_root = math.sqrt(model_width)
    total_slots = slot_count * seq_count * lax.axis_size("dp")
    hidden = hidden_in.reshape(local_slots, model_width)
    teacher = teacher.reshape(local_slots, model_width)
    length = lengths[0]
    order = Order(
        jnp.stack([tensor_rank.astype(jnp.int32), length, lax.axis_index("dp").astype(jnp.int32)])
    )
    own_part = lambda vector, width: lax.dynamic_slice_in_dim(vector, tensor_rank * width, width)
    qk_gain = jnp.pad(own_part(s_qk, heads_width), (0, heads_width % LANES)).reshape(1, -1)
    gains = jnp.stack([own_part(s_up, ff_local), own_part(s_gate, ff_local) * gate_root])

    attn_ring = RingGather(jnp.concatenate([w_query, w_key, w_value, w_attn_out.T], axis=1))
    feed_ring = RingGather(jnp.concatenate([w_up, w_gate, w_down.T], axis=1))
    attn_ring.hop(order)
    attn_ring.hop(order)
    qk_gain, gains = order.tie((qk_gain, gains))
    stream = gather_rows(hidden.astype(BF16), order)
    attn_ring.hop(order)
    attn_ring.hop(order)
    if short_axis(attn_ring.size):
        attn_ring.pieces[-2:] = order.tie(attn_ring.pieces[-2:])
    feed_ring.hop(order)
    kept, parts = attend(order, attn_ring.pieces, stream, qk_gain, head_count)
    w_attn, kept = kept[0], kept[1:]
    parts = scatter_rows(parts, lambda: feed_ring.hop(order))
    attn_unit, first_out, first_low, factors = first_norm(order, parts, hidden, alpha_attn)
    mlp_in = gather_rows(first_low, order, lambda: feed_ring.hop(order))
    feed_ring.hop(order)
    token_count = all_sum(lengths.astype(F32))[0]
    mlp_rows = order.tie(jnp.concatenate(mlp_in, axis=0))
    (w_feed, up_raw, gate_raw, hidden_low), parts = feed(order, feed_ring.pieces, mlp_in, gains)
    parts = scatter_rows(parts)
    output, grad_mlp_sum, grad_first, loss_sums = loss_and_grad(
        order, parts, first_out, teacher, alpha_mlp, token_count, total_slots
    )

    grad_mlp = gather_rows(grad_mlp_sum, order)
    grad_rows, hidden_low = order.tie((jnp.concatenate(grad_mlp, axis=0), hidden_low))
    grad_low = order.tie(turned_dot(grad_rows, hidden_low))
    low_reduce = RingReduce(grad_low, order)
    grad_pair, ff_sums, *parts = feed_back(order, grad_mlp, w_feed, up_raw, gate_raw, gains)
    low_reduce.hop(order)
    mlp_rows, grad_pair = order.tie((mlp_rows, grad_pair))
    grad_w_up = order.tie(turned_dot(mlp_rows, grad_pair[:, :ff_local]))
    low_reduce.hop(order)
    parts = scatter_rows(parts, order=order)
    mlp_rows, grad_pair = order.tie((mlp_rows, grad_pair))
    grad_w_gate = order.tie(turned_dot(mlp_rows, grad_pair[:, ff_local:]))
    low_reduce.hop(order)
    low_reduce.wait(order)
    pair_reduce = RingReduce(jnp.concatenate([grad_w_up, grad_w_gate], axis=1), order)
    grad_attn_sum, grad_input, attn_sums = first_back(
        order, parts, grad_first, first_out, attn_unit, hidden, alpha_attn, factors
    )
    grad_attn = gather_rows(grad_attn_sum, order, lambda: pair_reduce.hop(order))
    pair_reduce.hop(order)
    grad_w_down = low_reduce.total(order).T
    grad_project, gain_sums, *parts = attend_back(
        order, grad_attn, w_attn, qk_gain, kept, head_count
    )
    pair_reduce.hop(order)
    parts = scatter_rows(parts)
    grad_w_attn = order.tie(
        jnp.concatenate(
            [
                turned_kernel(order, stream, grad_project),
                turned_kernel(order, grad_attn, kept[1]),
            ],
            axis=1,
        )
    )
    attn_reduce = RingReduce(grad_w_attn, order)
    pair_reduce.wait(order)
    parts = order.tie(parts)
    loss_sums, attn_sums, gain_sums, ff_sums = order.tie(
        (loss_sums, attn_sums, gain_sums, ff_sums)
    )
    grad_input = grad_input + sum(part.astype(F32) for part in parts)

    def placed(values):
        width = values.shape[0]
        return lax.dynamic_update_slice_in_dim(
            jnp.zeros((width * lax.axis_size("tensor"),), F32), values, tensor_rank * width, 0
        )

    vectors = jnp.concatenate(
        [
            jnp.sum(loss_sums[0]).reshape(1),
            attn_sums[0],
            loss_sums[1],
            placed(gain_sums[0, :heads_width]),
            placed(ff_sums[0]),
            placed(ff_sums[1] * gate_root),
        ]
    )
    vectors = order.tie(tensor_sum(vectors))

    def attn_step(values):
        attn_reduce.hop(order)
        return order.tie(values)

    vectors = all_sum(vectors, attn_step)
    grad_w_pair = pair_reduce.total(order)
    grad_w_attn = attn_reduce.total(order, last=True)
    loss = vectors[0] / token_count
    cuts = [1 + model_width * k for k in range(4)] + [1 + 3 * model_width + s_up.shape[0]]
    return (
        loss,
        output[None],
        grad_input[None],
        grad_w_attn[:, :heads_width],
        grad_w_attn[:, heads_width : 2 * heads_width],
        grad_w_attn[:, 2 * heads_width : 3 * heads_width],
        grad_w_attn[:, 3 * heads_width :].T,
        grad_w_pair[:, :ff_local],
        grad_w_pair[:, ff_local:],
        grad_w_down,
        vectors[cuts[2] : cuts[3]],
        vectors[cuts[0] : cuts[1]],
        vectors[cuts[1] : cuts[2]],
        vectors[cuts[3] : cuts[4]],
        vectors[cuts[4] :],
    )


def solution(mesh):
    in_specs = (
        P("dp", "tensor", None),
        P("dp"),
        P("dp", "tensor", None),
        P("dp", "tensor"),
        P("dp", "tensor"),
        P("dp", "tensor"),
        P("tensor", "dp"),
        P("dp", "tensor"),
        P("dp", "tensor"),
        P("tensor", "dp"),
        P(),
        P(),
        P(),
        P(),
        P(),
    )
    out_specs = (
        P(),
        P("dp", "tensor", None),
        P("dp", "tensor", None),
        P("dp", "tensor"),
        P("dp", "tensor"),
        P("dp", "tensor"),
        P("tensor", "dp"),
        P("dp", "tensor"),
        P("dp", "tensor"),
        P("tensor", "dp"),
        P(),
        P(),
        P(),
        P(),
        P(),
    )
    return jax.shard_map(
        on_device, mesh=mesh, in_specs=in_specs, out_specs=out_specs, check_vma=False
    )
```
